32 devices in a mesh: groups: 2 (over x), gx: 4 (over y, core), gy: 4 (over z).
Axes of the slice: x: 2, y: 2, z: 4, core: 2. Of those that a mesh axis runs over, the one named last changes fastest.
Arguments:
- field_input: bfloat16 [64, 256, 1024], P(('groups', 'gx'), 'gy'), parts along dimension 0, may hold values from -8 to 8
- cotangent: bfloat16 [64, 256, 1024], P(('groups', 'gx'), 'gy'), parts along dimension 0, may hold values from -8 to 8
- spectral_weight: bfloat16 [256, 32768], P(('gx', 'gy')), may hold values from -0.75 to 0.75
- point_weight: bfloat16 [32, 32], replicated, may hold values from -1 to 1
- point_bias: float32 [32], replicated, may hold values from -3 to 3
Outputs:
- grad_field: bfloat16 [64, 256, 1024], P(('groups', 'gx'), 'gy'), parts along dimension 0
- grad_spectral: float32 [512, 32768], P(('groups', 'gx', 'gy')), parts along dimension 0
- grad_point: float32 [64, 32], P('groups'), parts along dimension 0
- grad_bias: float32 [64], P('groups'), parts along dimension 0
The draws below stay inside these ranges and needn't reach their ends.
There are 2 independent parts, one for each index of `groups`. The reference program is written for one: setup_inputs(seed, part) draws one part's arguments, and reference() takes and returns one part's arrays. A program takes and returns all parts, laid end to end along the dimension named above; an argument that names none is the same for every part. Nothing has to cross between parts.
All inputs are finite; a program needn't handle non-finite values.
Results may differ from the reference program's by a relative error of at most 0.0052.
Values sent between devices are 32-bit elements; how exact they have to be, the bound alone decides.
No kernel may reach another device: no remote copies, remote signals or barrier semaphores. Data moves between devices by JAX's collectives and lax.ppermute only.
A program may use at most 64 MiB of HBM per device.

```python
import math
import jax
import jax.numpy as jnp
from jax import lax

C = 32
KX = 16
KY = 16
KZ = 16
NZ = 32
CX = 8
NX = 32
NY = 256


def series_draw(seed_key, series_count, mode_count, length):
    coeffs = jax.random.normal(seed_key, (series_count, mode_count, 2), jnp.float32)
    steps = jnp.arange(mode_count, dtype=jnp.int32)[:, None] * jnp.arange(length, dtype=jnp.int32)[None, :] % length
    angles = 2.0 * math.pi / length * steps.astype(jnp.float32)
    waves = coeffs[:, :, 0:1] * jnp.cos(angles)[None] + coeffs[:, :, 1:2] * jnp.sin(angles)[None]
    return jnp.sum(waves, axis=1) / math.sqrt(mode_count)


def smooth_field(seed_key):
    keys = jax.random.split(seed_key, 3)
    along_x = series_draw(keys[0], 4, KX // 2, NX)
    along_y = series_draw(keys[1], 4, KY // 2, NY)
    along_z = series_draw(keys[2], 4 * C, KZ, NZ).reshape(4, C, NZ).transpose(0, 2, 1).reshape(4, NZ * C)
    plane = along_x[:, :, None] * along_y[:, None, :]
    return jnp.einsum('jab,jm->abm', plane, along_z) / 2.0


def mixed_field(seed_key):
    keys = jax.random.split(seed_key, 2)
    smooth = smooth_field(keys[0])
    values = jax.random.normal(keys[1], (NX, NY, NZ * C), jnp.float32) + smooth
    return jnp.clip(values, -8.0, 8.0).astype(jnp.bfloat16)


def draw_field_input(key, part):
    return mixed_field(jax.random.fold_in(key, 11))


def draw_cotangent(key, part):
    return mixed_field(jax.random.fold_in(key, 23))


def block_scale(own_key, shape, cuts, least, high):
    factor_of = 1.0
    for dim, blocks in cuts:
        draws = jax.random.uniform(jax.random.fold_in(jax.random.fold_in(own_key, 6), dim), (blocks,), jnp.float32, least / len(cuts), high / len(cuts))
        factor_of = factor_of * jnp.repeat(jnp.exp(draws), shape[dim] // blocks).reshape((-1,) + (1,) * (len(shape) - 1 - dim))
    return factor_of


def centred(rng, dims, spread, bound, cuts=(), kind=jnp.bfloat16):
    array = spread * jax.random.normal(rng, dims, jnp.float32)
    if cuts:
        array = array * block_scale(rng, dims, cuts, -0.22, 0.18)
    return jnp.clip(array, -bound, bound).astype(kind)


def setup_inputs(seed: int = 0, part: int = 0) -> dict:
    seeds = jax.random.split(jax.random.key(seed), 6)
    part_keys = jax.random.split(jax.random.fold_in(seeds[5], part), 6)
    field_input = draw_field_input(jax.random.fold_in(jax.random.fold_in(seeds[5], part), 71), part)
    cotangent = draw_cotangent(jax.random.fold_in(jax.random.fold_in(seeds[5], part), 71), part)
    spectral_weight = centred(seeds[2], (KY * KZ, KX * 2 * C * C), (2 * C) ** -0.5, 0.75, ((0, 16),))
    point_weight = centred(seeds[3], (C, C), C ** -0.5, 1.0)
    point_bias = centred(seeds[4], (C,), 0.5, 3.0, (), jnp.float32)
    return {"field_input": field_input, "cotangent": cotangent, "spectral_weight": spectral_weight, "point_weight": point_weight, "point_bias": point_bias}


def mode_values(mode_count, length):
    position = jnp.arange(mode_count, dtype=jnp.int32)
    return jnp.where(position < mode_count // 2, position, length - mode_count + position).astype(jnp.int32)

def phase_angles(positions, wavenumbers, length):
    steps = positions[:, None] * wavenumbers[None, :] % length
    return 2.0 * math.pi / length * steps.astype(jnp.float32)

def complex_table(positions, wavenumbers, length, factor):
    angles = phase_angles(positions, wavenumbers, length)
    cosine = jnp.cos(angles) * factor
    sine = jnp.sin(angles) * factor
    return jnp.stack([jnp.stack([cosine, -sine], axis=-1), jnp.stack([sine, cosine], axis=-1)], axis=1)

def depth_table(depth_count, mode_count):
    angles = phase_angles(jnp.arange(depth_count, dtype=jnp.int32), jnp.arange(mode_count, dtype=jnp.int32), depth_count)
    return jnp.stack([jnp.cos(angles), -jnp.sin(angles)], axis=1).astype(jnp.bfloat16)

def doubled(table):
    factor = jnp.where(jnp.arange(table.shape[2]) == 0, 1.0, 2.0).astype(jnp.float32)
    return table.astype(jnp.float32) * factor[None, None, :]

def spectral_product(spectrum, weights):
    shaped = spectrum.reshape(spectrum.shape[0], KX, 2, C)
    real_in, imag_in = (shaped[:, :, 0], shaped[:, :, 1])
    real_w, imag_w = (weights[:, :, 0], weights[:, :, 1])
    hp = lax.Precision.HIGHEST
    real_out = jnp.einsum('rmi,rmio->rmo', real_in, real_w, precision=hp) - jnp.einsum('rmi,rmio->rmo', imag_in, imag_w, precision=hp)
    imag_out = jnp.einsum('rmi,rmio->rmo', real_in, imag_w, precision=hp) + jnp.einsum('rmi,rmio->rmo', imag_in, real_w, precision=hp)
    return jnp.stack([real_out, imag_out], axis=2).reshape(spectrum.shape)

def adjoint_product(spectrum, weights):
    shaped = spectrum.reshape(spectrum.shape[0], KX, 2, C)
    real_in, imag_in = (shaped[:, :, 0], shaped[:, :, 1])
    real_w, imag_w = (weights[:, :, 0], weights[:, :, 1])
    hp = lax.Precision.HIGHEST
    real_out = jnp.einsum('rmo,rmio->rmi', real_in, real_w, precision=hp) + jnp.einsum('rmo,rmio->rmi', imag_in, imag_w, precision=hp)
    imag_out = jnp.einsum('rmo,rmio->rmi', imag_in, real_w, precision=hp) - jnp.einsum('rmo,rmio->rmi', real_in, imag_w, precision=hp)
    return jnp.stack([real_out, imag_out], axis=2).reshape(spectrum.shape)

def weight_gradient(field_spec, adjoint_spec):
    field_shaped = field_spec.reshape(field_spec.shape[0], KX, 2, C)
    adjoint_shaped = adjoint_spec.reshape(adjoint_spec.shape[0], KX, 2, C)
    real_v, imag_v = (field_shaped[:, :, 0], field_shaped[:, :, 1])
    real_h, imag_h = (adjoint_shaped[:, :, 0], adjoint_shaped[:, :, 1])
    real_g = real_v[:, :, :, None] * real_h[:, :, None, :] + imag_v[:, :, :, None] * imag_h[:, :, None, :]
    imag_g = real_v[:, :, :, None] * imag_h[:, :, None, :] - imag_v[:, :, :, None] * real_h[:, :, None, :]
    return jnp.stack([real_g, imag_g], axis=2).reshape(field_spec.shape[0], KX * 2 * C * C)

def forward_block(values, z_table, y_table, x_block):
    block_rows = values.shape[0]
    hp = lax.Precision.HIGHEST
    shaped = values.reshape(block_rows, NY, NZ, C).astype(jnp.float32)
    zpart = jnp.einsum('xyzc,zpk->xypkc', shaped, z_table.astype(jnp.float32), precision=hp).reshape(block_rows, NY, 2, KZ * C)
    ypart = jnp.einsum('xyqm,yqjp->xjpm', zpart, y_table, precision=hp).reshape(block_rows, KY, 2, KZ, C)
    xpart = jnp.einsum('xjqkc,xqmp->jkmpc', ypart, x_block, precision=hp)
    return xpart.reshape(KY * KZ, KX * 2 * C)

def inverse_block(spectrum, z_float, y_table, x_block):
    block_rows = x_block.shape[0]
    hp = lax.Precision.HIGHEST
    shaped = spectrum.reshape(KY, KZ, KX, 2, C)
    xpart = jnp.einsum('jkmqc,xpmq->xjpkc', shaped, x_block, precision=hp).reshape(block_rows, KY, 2, KZ * C)
    ypart = jnp.einsum('xjqm,ypjq->xypm', xpart, y_table, precision=hp).reshape(block_rows, NY, 2, KZ, C)
    return jnp.einsum('xypkc,zpk->xyzc', ypart, z_float, precision=hp).reshape(block_rows, NY, NZ * C)

def channel_mix(values, weight):
    rows = values.reshape(-1, C)
    return jnp.dot(rows, weight, preferred_element_type=jnp.float32).reshape(values.shape)

def reference(field_input, cotangent, spectral_weight, point_weight, point_bias):
    cell_scale = 1.0 / math.sqrt(NX * NY * NZ)
    block_count = NX // CX
    z_plain = depth_table(NZ, KZ)
    z_double = doubled(z_plain).astype(jnp.bfloat16)
    y_table = complex_table(jnp.arange(NY, dtype=jnp.int32), mode_values(KY, NY), NY, 1.0)
    x_table = complex_table(jnp.arange(NX, dtype=jnp.int32), mode_values(KX, NX), NX, cell_scale)
    x_blocks = x_table.reshape(block_count, CX, 2, KX, 2)
    field_blocks = field_input.reshape(block_count, CX, NY, NZ * C)
    cot_blocks = cotangent.reshape(block_count, CX, NY, NZ * C)
    empty = jnp.zeros((KY * KZ, KX * 2 * C), jnp.float32)

    def forward_step(running, items):
        values, x_block = items
        return (running + forward_block(values, z_plain, y_table, x_block), None)
    field_spec, _ = lax.scan(forward_step, empty, (field_blocks, x_blocks))
    weights = spectral_weight.astype(jnp.float32).reshape(KY * KZ, KX, 2, C, C)
    mode_output = spectral_product(field_spec, weights)
    bias_row = jnp.tile(point_bias, NZ)
    z_double_float = doubled(z_plain)

    def backward_step(carry, items):
        adjoint_spec, point_sum, bias_sum = carry
        values, cot_block, x_block = items
        spectral_out = inverse_block(mode_output, z_double_float, y_table, x_block)
        preact = spectral_out + channel_mix(values, point_weight) + bias_row
        _, pullback = jax.vjp(jax.nn.gelu, preact)
        adjoint = pullback(cot_block.astype(jnp.float32))[0].astype(jnp.bfloat16)
        adjoint_spec = adjoint_spec + forward_block(adjoint, z_double, y_table, x_block)
        flat_values = values.reshape(-1, C)
        flat_adjoint = adjoint.reshape(-1, C)
        point_sum = point_sum + jnp.dot(flat_values.T, flat_adjoint, preferred_element_type=jnp.float32)
        bias_sum = bias_sum + lax.optimization_barrier(jnp.sum(flat_adjoint.astype(jnp.float32), axis=0))
        return ((adjoint_spec, point_sum, bias_sum), adjoint)
    start = (empty, jnp.zeros((C, C), jnp.float32), jnp.zeros((C,), jnp.float32))
    (adjoint_spec, point_sum, bias_sum), adjoint_all = lax.scan(backward_step, start, (field_blocks, cot_blocks, x_blocks))
    grad_spectral = weight_gradient(field_spec, adjoint_spec) * cell_scale
    mode_adjoint = adjoint_product(adjoint_spec, weights)
    z_plain_float = z_plain.astype(jnp.float32)

    def final_block(items):
        adjoint, x_block = items
        back_field = inverse_block(mode_adjoint, z_plain_float, y_table, x_block)
        return (channel_mix(adjoint, point_weight.T) + back_field).astype(jnp.bfloat16)
    grad_field = lax.map(final_block, (adjoint_all, x_blocks)).reshape(NX, NY, NZ * C)
    return (grad_field, grad_spectral, point_sum * cell_scale, bias_sum * cell_scale)
```

```python
import functools
import math

import jax
import jax.numpy as jnp
import ml_dtypes
import numpy as np
from jax import lax
from jax.experimental import pallas as pl
from jax.experimental.pallas import tpu as pltpu
from jax.sharding import PartitionSpec as P

C = 32
KX = 16
KY = 16
KZ = 16
NZ = 32


def mode_values(mode_count, length):
    position = jnp.arange(mode_count, dtype=jnp.int32)
    return jnp.where(position < mode_count // 2, position, length - mode_count + position)


def phase_angles(positions, wavenumbers, length):
    steps = positions[:, None] * wavenumbers[None, :] % length
    return 2.0 * math.pi / length * steps.astype(jnp.float32)


def complex_table(positions, wavenumbers, length, factor):
    angles = phase_angles(positions, wavenumbers, length)
    cosine = jnp.cos(angles) * factor
    sine = jnp.sin(angles) * factor
    return jnp.stack(
        [jnp.stack([cosine, -sine], axis=-1), jnp.stack([sine, cosine], axis=-1)], axis=1
    )


def depth_table(depth_count, mode_count):
    angles = phase_angles(
        jnp.arange(depth_count, dtype=jnp.int32),
        jnp.arange(mode_count, dtype=jnp.int32),
        depth_count,
    )
    return jnp.stack([jnp.cos(angles), -jnp.sin(angles)], axis=1).astype(jnp.bfloat16)


def doubled(table):
    factor = jnp.where(jnp.arange(table.shape[2]) == 0, 1.0, 2.0).astype(jnp.float32)
    return table.astype(jnp.float32) * factor[None, None, :]


def spectral_product(spectrum, weights):
    shaped = spectrum.reshape(spectrum.shape[0], KX, 2, C)
    real_in, imag_in = (shaped[:, :, 0], shaped[:, :, 1])
    real_w, imag_w = (weights[:, :, 0], weights[:, :, 1])
    hp = lax.Precision.HIGHEST
    real_out = jnp.einsum("rmi,rmio->rmo", real_in, real_w, precision=hp) - jnp.einsum(
        "rmi,rmio->rmo", imag_in, imag_w, precision=hp
    )
    imag_out = jnp.einsum("rmi,rmio->rmo", real_in, imag_w, precision=hp) + jnp.einsum(
        "rmi,rmio->rmo", imag_in, real_w, precision=hp
    )
    return jnp.stack([real_out, imag_out], axis=2).reshape(spectrum.shape)


def adjoint_product(spectrum, weights):
    shaped = spectrum.reshape(spectrum.shape[0], KX, 2, C)
    real_in, imag_in = (shaped[:, :, 0], shaped[:, :, 1])
    real_w, imag_w = (weights[:, :, 0], weights[:, :, 1])
    hp = lax.Precision.HIGHEST
    real_out = jnp.einsum("rmo,rmio->rmi", real_in, real_w, precision=hp) + jnp.einsum(
        "rmo,rmio->rmi", imag_in, imag_w, precision=hp
    )
    imag_out = jnp.einsum("rmo,rmio->rmi", imag_in, real_w, precision=hp) - jnp.einsum(
        "rmo,rmio->rmi", real_in, imag_w, precision=hp
    )
    return jnp.stack([real_out, imag_out], axis=2).reshape(spectrum.shape)


def weight_gradient(field_spec, adjoint_spec):
    field_shaped = field_spec.reshape(field_spec.shape[0], KX, 2, C)
    adjoint_shaped = adjoint_spec.reshape(adjoint_spec.shape[0], KX, 2, C)
    real_v, imag_v = (field_shaped[:, :, 0], field_shaped[:, :, 1])
    real_h, imag_h = (adjoint_shaped[:, :, 0], adjoint_shaped[:, :, 1])
    real_g = (
        real_v[:, :, :, None] * real_h[:, :, None, :]
        + imag_v[:, :, :, None] * imag_h[:, :, None, :]
    )
    imag_g = (
        real_v[:, :, :, None] * imag_h[:, :, None, :]
        - imag_v[:, :, :, None] * real_h[:, :, None, :]
    )
    return jnp.stack([real_g, imag_g], axis=2).reshape(field_spec.shape[0], KX * 2 * C * C)


def channel_mix(values, weight):
    group_size = max(1, 128 // weight.shape[0])
    block = jnp.kron(jnp.eye(group_size, dtype=weight.dtype), weight)
    rows = values.reshape(-1, block.shape[0])
    return jnp.dot(rows, block, preferred_element_type=jnp.float32).reshape(values.shape)


def spectrum(values, z_table, y_table, x_local, x_whole):
    rows_x, rows_y, _ = values.shape
    hp = lax.Precision.HIGHEST
    shaped = values.reshape(rows_x, rows_y, NZ, C)
    zpart = jnp.einsum(
        "xyzc,zpk->xypkc", shaped, z_table, preferred_element_type=jnp.float32
    ).reshape(rows_x, rows_y, 2, KZ * C)
    ypart = jnp.einsum("xyqm,yqjp->xjpm", zpart, y_table, precision=hp)
    pencil = lax.all_to_all(ypart, "gx", split_axis=1, concat_axis=0, tiled=True)
    mode_rows = pencil.shape[1]
    pencil = pencil.reshape(pencil.shape[0], mode_rows, 2, KZ, C)
    partial_value = jnp.einsum("xjqkc,xqmp->jkmpc", pencil, x_whole, precision=hp).reshape(
        mode_rows * KZ, KX * 2 * C
    )
    return lax.psum_scatter(partial_value, "gy", scatter_dimension=0, tiled=True)


def synthesis(owned, z_float, y_table, x_whole, rows_x, rows_y):
    hp = lax.Precision.HIGHEST
    planes = lax.all_gather(owned, "gy", axis=0, tiled=True)
    mode_rows = planes.shape[0] // KZ
    shaped = planes.reshape(mode_rows, KZ, KX, 2, C)
    wide = jnp.einsum("jkmqc,xpmq->xjpkc", shaped, x_whole, precision=hp).reshape(
        x_whole.shape[0], mode_rows, 2, KZ * C
    )
    slab = lax.all_to_all(wide, "gx", split_axis=0, concat_axis=1, tiled=True)
    ypart = jnp.einsum("xjqm,ypjq->xypm", slab, y_table, precision=hp).reshape(
        rows_x, rows_y, 2, KZ, C
    )
    return jnp.einsum("xypkc,zpk->xyzc", ypart, z_float, precision=hp).reshape(
        rows_x, rows_y, NZ * C
    )


def general_device(field_input, cotangent, spectral_weight, point_weight, point_bias):
    rows_x, rows_y, _ = field_input.shape
    full_x = rows_x * lax.axis_size("gx")
    full_y = rows_y * lax.axis_size("gy")
    cell_scale = 1.0 / math.sqrt(full_x * full_y * NZ)
    x_start = lax.axis_index("gx") * rows_x
    y_start = lax.axis_index("gy") * rows_y
    y_table = complex_table(
        y_start + jnp.arange(rows_y, dtype=jnp.int32), mode_values(KY, full_y), full_y, 1.0
    )
    x_local = complex_table(
        x_start + jnp.arange(rows_x, dtype=jnp.int32), mode_values(KX, full_x), full_x, cell_scale
    )
    x_whole = complex_table(
        jnp.arange(full_x, dtype=jnp.int32), mode_values(KX, full_x), full_x, cell_scale
    )
    z_plain = depth_table(NZ, KZ)
    z_double_float = doubled(z_plain)
    z_double = z_double_float.astype(jnp.bfloat16)
    field_spec = spectrum(field_input, z_plain, y_table, x_local, x_whole)
    weights = spectral_weight.astype(jnp.float32).reshape(-1, KX, 2, C, C)
    mode_output = spectral_product(field_spec, weights)
    spectral_out = synthesis(mode_output, z_double_float, y_table, x_whole, rows_x, rows_y)
    bias_row = jnp.tile(point_bias, NZ)
    preact = spectral_out + channel_mix(field_input, point_weight) + bias_row
    _, pullback = jax.vjp(jax.nn.gelu, preact)
    adjoint = pullback(cotangent.astype(jnp.float32))[0].astype(jnp.bfloat16)
    adjoint_spec = spectrum(adjoint, z_double, y_table, x_local, x_whole)
    grad_spectral = weight_gradient(field_spec, adjoint_spec) * cell_scale
    mode_adjoint = adjoint_product(adjoint_spec, weights)
    flat_field = field_input.reshape(-1, C)
    flat_adjoint = adjoint.reshape(-1, C)
    point_term = (
        jnp.einsum("rc,rd->cd", flat_field, flat_adjoint, preferred_element_type=jnp.float32)
        * cell_scale
    )
    bias_term = jnp.sum(flat_adjoint.astype(jnp.float32), axis=0) * cell_scale
    grad_point, grad_bias = lax.psum((point_term, bias_term), ("gx", "gy"))
    back_field = synthesis(
        mode_adjoint, z_plain.astype(jnp.float32), y_table, x_whole, rows_x, rows_y
    )
    grad_field = (channel_mix(adjoint, point_weight.T) + back_field).astype(jnp.bfloat16)
    return (grad_field, grad_spectral, grad_point, grad_bias)


BF = jnp.bfloat16
F32 = jnp.float32
LANES = 128
CHUNKS = KZ * C // LANES
WIDE = KZ * C
DATA_ROWS = 16 * CHUNKS
SUM_ROWS = 16


def dot(left, right, dims=((1,), (0,))):
    return lax.dot_general(left, right, (dims, ((), ())), preferred_element_type=F32)


def halves(values):
    high = values.astype(BF)
    return high, (values - high.astype(F32)).astype(BF)


def iota(shape, axis):
    return lax.broadcasted_iota(jnp.int32, shape, axis)


def lane_take(values, index):
    return jnp.take_along_axis(values, index, axis=1, mode="promise_in_bounds")


def np_halves(table):
    high = table.astype(ml_dtypes.bfloat16).astype(np.float64)
    low = (table - high).astype(ml_dtypes.bfloat16).astype(np.float64)
    return high, low


def np_modes(count, length):
    position = np.arange(count)
    return np.where(position < count // 2, position, length - count + position)


def np_angles(positions, modes, length):
    return 2.0 * np.pi * ((positions[:, None] * modes[None, :]) % length) / length


def depth_matrix():
    angles = np_angles(np.arange(NZ), np.arange(KZ), NZ)
    table = np.stack([np.cos(angles), -np.sin(angles)], axis=1).astype(ml_dtypes.bfloat16)
    table = table.astype(np.float32).reshape(NZ, 2 * KZ)
    return np.kron(table, np.eye(C, dtype=np.float32)).astype(ml_dtypes.bfloat16)


def y_tables(full_y, rows_y, rows_x, parts):
    angles = np_angles(np.arange(full_y), np_modes(KY, full_y), full_y)
    table = np.stack([np.cos(angles), -np.sin(angles)], axis=0)
    both = np.stack(np_halves(table), axis=0).reshape(2, 2, parts, rows_y, KY)
    forward = both.transpose(2, 0, 1, 4, 3).reshape(parts, 4 * KY, rows_y)
    forward = np.tile(forward, (1, 1, LANES // rows_y))
    inverse = np.repeat(both.transpose(2, 0, 3, 1, 4), rows_x, axis=-1)
    inverse = inverse.reshape(parts, 2 * rows_y, 2 * KY * rows_x)
    return forward.astype(np.float32), inverse.astype(np.float32)


def x_tables(full_x, rows_x, factor):
    angles = np_angles(np.arange(full_x), np_modes(KX, full_x), full_x)
    cosine, sine = np.cos(angles) * factor, np.sin(angles) * factor
    table = np.stack([np.stack([cosine, -sine], -1), np.stack([sine, cosine], -1)], axis=1)
    blocked = table.reshape(full_x // rows_x, rows_x, 2, KX, 2).transpose(0, 2, 1, 3, 4)
    inverse = blocked.reshape(2 * full_x, 2 * KX)
    forward = inverse.T

    def packed(matrix):
        high, low = np_halves(matrix)
        return np.concatenate([high, low, high], axis=1).astype(ml_dtypes.bfloat16)

    return packed(forward), packed(inverse)


def tripled(values):
    high, low = halves(values)
    return jnp.concatenate([high, high, low], axis=0)


def forward_matrix(table_ref, rows_x, rows_y):
    table = table_ref[lax.axis_index("gy")]
    count = table.shape[0]
    spread = jnp.broadcast_to(table[:, None, :], (count, rows_x, LANES))
    spread = spread.reshape(count * rows_x, LANES)
    spread = jnp.concatenate([spread] * (rows_x * rows_y // LANES), axis=1)
    shape = spread.shape
    return jnp.where(iota(shape, 1) // rows_y == iota(shape, 0) % rows_x, spread, 0.0).astype(BF)


def inverse_matrix(table_ref, rows_x, rows_y):
    table = table_ref[lax.axis_index("gy")]
    wide = table.shape[1]
    both = []
    for part in range(2):
        block = table[part * rows_y : (part + 1) * rows_y]
        owner = iota((rows_y, wide), 1) % rows_x
        rows = [jnp.where(owner == x, block, 0.0) for x in range(rows_x)]
        both.append(jnp.concatenate(rows, axis=0).astype(BF))
    return jnp.concatenate([both[0], both[1], both[0]], axis=1)


def field_spectrum(values, matrix, depth_ref, out_ref, rows_x):
    rows = KY * rows_x
    both = dot(matrix, values)
    high, low = halves(both[: 2 * rows] + both[2 * rows :])
    both = dot(jnp.concatenate([high, low], axis=0), depth_ref[...])
    both = both[: 2 * rows] + both[2 * rows :]
    real = both[:rows, :WIDE] - both[rows:, WIDE:]
    imag = both[:rows, WIDE:] + both[rows:, :WIDE]
    for part, piece in ((0, real), (1, imag)):
        for chunk in range(CHUNKS):
            start = (chunk * 2 + part) * rows_x
            block = piece[:, chunk * LANES : (chunk + 1) * LANES]
            out_ref[:, start : start + rows_x, :] = block.reshape(KY, rows_x, LANES)


def field_synthesis(in_ref, matrix, depth_ref, rows_x):
    rows = KY * rows_x
    parts = []
    for part in range(2):
        pieces = []
        for chunk in range(CHUNKS):
            start = (chunk * 2 + part) * rows_x
            pieces.append(in_ref[:, start : start + rows_x, :].reshape(rows, LANES))
        parts.append(jnp.concatenate(pieces, axis=1))
    real, imag = parts
    stacked = jnp.concatenate(
        [jnp.concatenate([real, imag], axis=1), jnp.concatenate([imag, -real], axis=1)], axis=0
    )
    high, low = halves(stacked)
    both = dot(jnp.concatenate([high, low], axis=0), depth_ref[...], ((1,), (1,)))
    planes = both[: 2 * rows] + both[2 * rows :]
    return dot(matrix, tripled(planes))


def mixing_matrix(weight_ref):
    wide = 8 * C
    pick = (iota((wide, C), 0) % C == iota((wide, C), 1)).astype(F32).astype(BF)
    tall = dot(pick, weight_ref[...]).astype(BF)
    tiled = dot(tall, pick, ((1,), (1,)))
    shape = (wide, wide)
    return jnp.where(iota(shape, 0) // C == iota(shape, 1) // C, tiled, 0.0).astype(BF)


def mixed(values, matrix, dims):
    wide = matrix.shape[0]
    pieces = []
    for start in range(0, values.shape[1], wide):
        pieces.append(dot(values[:, start : start + wide], matrix, dims))
    return jnp.concatenate(pieces, axis=1)


def folded(row):
    total = row[:, :LANES]
    for start in range(LANES, row.shape[1], LANES):
        total = total + row[:, start : start + LANES]
    total = total + pltpu.roll(total, 64, 1)
    return total + pltpu.roll(total, 32, 1)


def own_spectrum(in_ref, table_ref, x_parts, y_parts):
    chunks = []
    for chunk in range(CHUNKS):
        rows = []
        for x_part in range(x_parts):
            block = [
                in_ref[x_part * y_parts + y_part, chunk * 16 : (chunk + 1) * 16, :]
                for y_part in range(y_parts)
            ]
            rows.append(functools.reduce(jnp.add, block))
        chunks.append(jnp.concatenate(rows, axis=0))
    return dot(table_ref[...], tripled(jnp.concatenate(chunks, axis=1)))


def depth_factor():
    return jnp.where(iota((1, WIDE), 1) < C, 1.0, 2.0).astype(F32)


def spread_modes(values, table_ref, out_ref, x_parts, y_parts):
    cells = dot(table_ref[...], tripled(values))
    for x_part in range(x_parts):
        for chunk in range(CHUNKS):
            block = cells[x_part * 16 : (x_part + 1) * 16, chunk * LANES : (chunk + 1) * LANES]
            for y_part in range(y_parts):
                out_ref[x_part * y_parts + y_part, chunk * 16 : (chunk + 1) * 16, :] = block


def mode_row(ref, row):
    wide = jnp.broadcast_to(ref[pl.ds(row, 1), :], (KZ, WIDE))
    group = iota((KZ, LANES), 0) // 4
    chosen = wide[:, :LANES]
    for chunk in range(1, CHUNKS):
        chosen = jnp.where(group == chunk, wide[:, chunk * LANES : (chunk + 1) * LANES], chosen)
    return chosen


def in_index(step):
    return iota((KZ, LANES), 0) % 4 * C + step * 4 + iota((KZ, LANES), 1) // C


def out_index():
    return iota((KZ, LANES), 0) % 4 * C + iota((KZ, LANES), 1) % C


def own_group():
    return iota((KZ, LANES), 0) % 4 == iota((KZ, LANES), 1) // C


def gathered_rows(scratch):
    pieces = []
    for chunk in range(CHUNKS):
        terms = [scratch[pl.ds(chunk * 4 + a, 2 * KX, stride=KZ), :] for a in range(4)]
        pieces.append((terms[0] + terms[1]) + (terms[2] + terms[3]))
    return jnp.concatenate(pieces, axis=1)


def weight_parts(weight_ref, mode):
    start = pl.multiple_of(mode * 2 * C * C, LANES)
    both = weight_ref[:, pl.ds(start, 2 * C * C)].astype(F32)
    return both[:, : C * C], both[:, C * C :]


def lanes_of(values, step):
    return values[:, step * LANES : (step + 1) * LANES]


def first_kernel(rows_x, rows_y, field_ref, table_ref, depth_ref, out_ref):
    matrix = forward_matrix(table_ref, rows_x, rows_y)
    field_spectrum(field_ref[...], matrix, depth_ref, out_ref, rows_x)


def product_kernel(
    x_parts, y_parts, in_ref, forward_ref, inverse_ref, weight_ref, out_ref, spec_ref, scratch
):
    spec_ref[...] = own_spectrum(in_ref, forward_ref, x_parts, y_parts)
    keep = own_group()

    def step(mode, carry):
        real, imag = mode_row(spec_ref, 2 * mode), mode_row(spec_ref, 2 * mode + 1)
        real_w, imag_w = weight_parts(weight_ref, mode)
        real_sum = jnp.zeros((KZ, LANES), F32)
        imag_sum = jnp.zeros((KZ, LANES), F32)
        for part in range(C // 4):
            index = in_index(part)
            real_v, imag_v = lane_take(real, index), lane_take(imag, index)
            real_p, imag_p = lanes_of(real_w, part), lanes_of(imag_w, part)
            real_sum = real_sum + (real_v * real_p - imag_v * imag_p)
            imag_sum = imag_sum + (real_v * imag_p + imag_v * real_p)
        for part, total in ((0, real_sum), (1, imag_sum)):
            start = pl.multiple_of((2 * mode + part) * KZ, KZ)
            scratch[pl.ds(start, KZ), :] = jnp.where(keep, folded(total), 0.0)
        return carry

    lax.fori_loop(0, KX, step, 0, unroll=4)
    spread_modes(gathered_rows(scratch) * depth_factor(), inverse_ref, out_ref, x_parts, y_parts)


def middle_kernel(
    rows_x,
    rows_y,
    in_ref,
    field_ref,
    cotangent_ref,
    point_ref,
    bias_ref,
    table_ref,
    back_ref,
    depth_ref,
    out_ref,
    adjoint_ref,
    sums_ref,
):
    spectral = field_synthesis(in_ref, inverse_matrix(back_ref, rows_x, rows_y), depth_ref, rows_x)
    mixing = mixing_matrix(point_ref)
    field = field_ref[...]
    bias = jnp.concatenate([bias_ref[...]] * NZ, axis=1)
    value = spectral + mixed(field, mixing, ((1,), (0,))) + bias
    root = math.sqrt(2.0 / math.pi)
    square = value * value
    bent = jnp.tanh(value * (root + (root * 0.044715) * square))
    slope = 0.5 * (1.0 + bent) + (0.5 * value) * (1.0 - bent * bent) * (
        root + (3.0 * root * 0.044715) * square
    )
    adjoint = (cotangent_ref[...].astype(F32) * slope).astype(BF)
    adjoint_ref[...] = adjoint
    field_spectrum(adjoint, forward_matrix(table_ref, rows_x, rows_y), depth_ref, out_ref, rows_x)
    wide = mixing.shape[0]
    total = jnp.zeros((wide, wide), F32)
    for start in range(0, NZ * C, wide):
        total = total + dot(
            field[:, start : start + wide], adjoint[:, start : start + wide], ((0,), (0,))
        )
    total = jnp.where(iota((wide, wide), 0) // C == iota((wide, wide), 1) // C, total, 0.0)
    point = total[:C]
    for start in range(C, wide, C):
        point = point + total[start : start + C]
    point = folded(point)
    group = iota((8, LANES), 1) // C
    packed = point[:8]
    for part in range(1, 4):
        packed = jnp.where(group == part, point[part * 8 : (part + 1) * 8], packed)
    sums_ref[:8, :] = packed
    sums_ref[8:, :] = folded(dot(jnp.ones((8, adjoint.shape[0]), BF), adjoint))


def swapped(values, index, distance):
    return lane_take(values, index ^ distance)


def adjoint_kernel(
    x_parts,
    y_parts,
    in_ref,
    forward_ref,
    inverse_ref,
    weight_ref,
    sums_ref,
    out_ref,
    spec_ref,
    scratch,
):
    spec_ref[...] = own_spectrum(in_ref, forward_ref, x_parts, y_parts) * depth_factor()
    keep = own_group()
    lane = iota((KZ, LANES), 1)
    final = lane % C % 4 * C + lane % C // 4 * 4

    def reduced(parts):
        distance = 16
        while len(parts) > 1:
            bit = (lane & distance) != 0
            half = len(parts) // 2
            merged = []
            for low, high in zip(parts[:half], parts[half:]):
                kept = jnp.where(bit, high, low)
                other = jnp.where(bit, low, high)
                merged.append(kept + swapped(other, lane, distance))
            parts = merged
            distance //= 2
        total = parts[0]
        while distance:
            total = total + swapped(total, lane, distance)
            distance //= 2
        return lane_take(total, final)

    def step(mode, carry):
        index = out_index()
        real = lane_take(mode_row(spec_ref, 2 * mode), index)
        imag = lane_take(mode_row(spec_ref, 2 * mode + 1), index)
        real_w, imag_w = weight_parts(weight_ref, mode)
        real_parts, imag_parts = [], []
        for part in range(C // 4):
            real_p, imag_p = lanes_of(real_w, part), lanes_of(imag_w, part)
            real_parts.append(real * real_p + imag * imag_p)
            imag_parts.append(imag * real_p - real * imag_p)
        for part, parts in ((0, real_parts), (1, imag_parts)):
            start = pl.multiple_of((2 * mode + part) * KZ, KZ)
            scratch[pl.ds(start, KZ), :] = jnp.where(keep, reduced(parts), 0.0)
        return carry

    lax.fori_loop(0, KX, step, 0, unroll=4)
    spread_modes(gathered_rows(scratch), inverse_ref, out_ref, x_parts, y_parts)
    for device in range(x_parts * y_parts):
        out_ref[device, DATA_ROWS:, :] = sums_ref[...]


def weight_kernel(scale, modes, field_ref, adjoint_ref, out_ref):
    first = pl.program_id(0) * modes
    index = out_index()
    for local in range(modes):
        row = 2 * (first + local)
        real_v, imag_v = mode_row(field_ref, row), mode_row(field_ref, row + 1)
        real_h = lane_take(mode_row(adjoint_ref, row), index) * scale
        imag_h = lane_take(mode_row(adjoint_ref, row + 1), index) * scale
        for part in range(C // 4):
            take = in_index(part)
            real, imag = lane_take(real_v, take), lane_take(imag_v, take)
            start = local * 2 * C * C + part * LANES
            out_ref[:, start : start + LANES] = real * real_h + imag * imag_h
            start += C * C
            out_ref[:, start : start + LANES] = real * imag_h - imag * real_h


def last_kernel(
    rows_x,
    rows_y,
    scale,
    in_ref,
    adjoint_ref,
    point_ref,
    back_ref,
    depth_ref,
    out_ref,
    grad_ref,
    bias_ref,
):
    spectral = field_synthesis(in_ref, inverse_matrix(back_ref, rows_x, rows_y), depth_ref, rows_x)
    mixing = mixing_matrix(point_ref)
    out_ref[...] = (mixed(adjoint_ref[...], mixing, ((1,), (1,))) + spectral).astype(BF)
    total = in_ref[0, DATA_ROWS:, :]
    for device in range(1, in_ref.shape[0]):
        total = total + in_ref[device, DATA_ROWS:, :]
    total = total * scale
    packed = total[:8]
    for part in range(4):
        piece = packed if part == 0 else pltpu.roll(packed, LANES - part * C, 1)
        grad_ref[part * 8 : (part + 1) * 8, :] = piece[:, :C]
    bias_ref[...] = total[8:9, :C]


def call(kernel, outs, scratch=(), **options):
    shapes = [jax.ShapeDtypeStruct(shape, kind) for shape, kind in outs]
    params = pltpu.CompilerParams(vmem_limit_bytes=56 * 1024 * 1024)
    return pl.pallas_call(
        kernel, out_shape=shapes, scratch_shapes=list(scratch), compiler_params=params, **options
    )


def exchange(values):
    return lax.all_to_all(values, ("gx", "gy"), split_axis=0, concat_axis=0, tiled=True)


def fast_device(field_input, cotangent, spectral_weight, point_weight, point_bias):
    rows_x, rows_y, depth = field_input.shape
    x_parts, y_parts = lax.axis_size("gx"), lax.axis_size("gy")
    devices = x_parts * y_parts
    full_x, full_y = rows_x * x_parts, rows_y * y_parts
    scale = 1.0 / math.sqrt(full_x * full_y * NZ)
    cells = rows_x * rows_y
    depth_table = jnp.asarray(depth_matrix())
    forward_y, inverse_y = map(jnp.asarray, y_tables(full_y, rows_y, rows_x, y_parts))
    forward_x, inverse_x = map(jnp.asarray, x_tables(full_x, rows_x, scale))
    field = field_input.reshape(cells, depth)
    bias = point_bias.reshape(1, C)
    payload = ((devices, DATA_ROWS, LANES), F32)
    spectrum_shape = ((2 * KX, WIDE), F32)
    rows_scratch = pltpu.VMEM((2 * KX * KZ, LANES), F32)

    (sent,) = call(functools.partial(first_kernel, rows_x, rows_y), [payload])(
        field, forward_y, depth_table
    )
    sent, field_modes = call(
        functools.partial(product_kernel, x_parts, y_parts),
        [payload, spectrum_shape],
        [rows_scratch],
    )(exchange(sent), forward_x, inverse_x, spectral_weight)
    sent, adjoint, sums = call(
        functools.partial(middle_kernel, rows_x, rows_y),
        [payload, ((cells, depth), BF), ((SUM_ROWS, LANES), F32)],
    )(
        exchange(sent),
        field,
        cotangent.reshape(cells, depth),
        point_weight,
        bias,
        forward_y,
        inverse_y,
        depth_table,
    )
    sent, adjoint_modes = call(
        functools.partial(adjoint_kernel, x_parts, y_parts),
        [((devices, DATA_ROWS + SUM_ROWS, LANES), F32), spectrum_shape],
        [rows_scratch],
    )(exchange(sent), forward_x, inverse_x, spectral_weight, sums)
    steps = 4
    modes = KX // steps
    whole = pl.BlockSpec((2 * KX, WIDE), lambda i: (0, 0))
    (grad_spectral,) = call(
        functools.partial(weight_kernel, scale, modes),
        [((KZ, KX * 2 * C * C), F32)],
        grid=(steps,),
        in_specs=[whole, whole],
        out_specs=[pl.BlockSpec((KZ, modes * 2 * C * C), lambda i: (0, i))],
    )(field_modes, adjoint_modes)
    grad_field, grad_point, grad_bias = call(
        functools.partial(last_kernel, rows_x, rows_y, scale),
        [((cells, depth), BF), ((C, C), F32), ((1, C), F32)],
    )(exchange(sent), adjoint, point_weight, inverse_y, depth_table)
    return (
        grad_field.reshape(field_input.shape),
        grad_spectral,
        grad_point,
        grad_bias.reshape(C),
    )


def on_device(*arguments):
    rows_x, rows_y, _ = arguments[0].shape
    if rows_x == 8 and rows_y == 64 and arguments[2].shape[0] == KZ:
        return fast_device(*arguments)
    return general_device(*arguments)


def solution(mesh):
    return jax.shard_map(
        on_device,
        mesh=mesh,
        in_specs=(
            P(("groups", "gx"), "gy", None),
            P(("groups", "gx"), "gy", None),
            P(("gx", "gy"), None),
            P(),
            P(),
        ),
        out_specs=(
            P(("groups", "gx"), "gy", None),
            P(("groups", "gx", "gy"), None),
            P("groups", None),
            P("groups"),
        ),
        check_vma=False,
    )
```

```python
import functools
import math

import jax
import jax.numpy as jnp
import ml_dtypes
import numpy as np
from jax import lax
from jax.experimental import pallas as pl
from jax.experimental.pallas import tpu as pltpu
from jax.sharding import PartitionSpec as P

C = 32
KX = 16
KY = 16
KZ = 16
NZ = 32


def mode_values(mode_count, length):
    position = jnp.arange(mode_count, dtype=jnp.int32)
    return jnp.where(position < mode_count // 2, position, length - mode_count + position)


def phase_angles(positions, wavenumbers, length):
    steps = positions[:, None] * wavenumbers[None, :] % length
    return 2.0 * math.pi / length * steps.astype(jnp.float32)


def complex_table(positions, wavenumbers, length, factor):
    angles = phase_angles(positions, wavenumbers, length)
    cosine = jnp.cos(angles) * factor
    sine = jnp.sin(angles) * factor
    return jnp.stack(
        [jnp.stack([cosine, -sine], axis=-1), jnp.stack([sine, cosine], axis=-1)], axis=1
    )


def depth_table(depth_count, mode_count):
    angles = phase_angles(
        jnp.arange(depth_count, dtype=jnp.int32),
        jnp.arange(mode_count, dtype=jnp.int32),
        depth_count,
    )
    return jnp.stack([jnp.cos(angles), -jnp.sin(angles)], axis=1).astype(jnp.bfloat16)


def doubled(table):
    factor = jnp.where(jnp.arange(table.shape[2]) == 0, 1.0, 2.0).astype(jnp.float32)
    return table.astype(jnp.float32) * factor[None, None, :]


def spectral_product(spectrum, weights):
    shaped = spectrum.reshape(spectrum.shape[0], KX, 2, C)
    real_in, imag_in = (shaped[:, :, 0], shaped[:, :, 1])
    real_w, imag_w = (weights[:, :, 0], weights[:, :, 1])
    hp = lax.Precision.HIGHEST
    real_out = jnp.einsum("rmi,rmio->rmo", real_in, real_w, precision=hp) - jnp.einsum(
        "rmi,rmio->rmo", imag_in, imag_w, precision=hp
    )
    imag_out = jnp.einsum("rmi,rmio->rmo", real_in, imag_w, precision=hp) + jnp.einsum(
        "rmi,rmio->rmo", imag_in, real_w, precision=hp
    )
    return jnp.stack([real_out, imag_out], axis=2).reshape(spectrum.shape)


def adjoint_product(spectrum, weights):
    shaped = spectrum.reshape(spectrum.shape[0], KX, 2, C)
    real_in, imag_in = (shaped[:, :, 0], shaped[:, :, 1])
    real_w, imag_w = (weights[:, :, 0], weights[:, :, 1])
    hp = lax.Precision.HIGHEST
    real_out = jnp.einsum("rmo,rmio->rmi", real_in, real_w, precision=hp) + jnp.einsum(
        "rmo,rmio->rmi", imag_in, imag_w, precision=hp
    )
    imag_out = jnp.einsum("rmo,rmio->rmi", imag_in, real_w, precision=hp) - jnp.einsum(
        "rmo,rmio->rmi", real_in, imag_w, precision=hp
    )
    return jnp.stack([real_out, imag_out], axis=2).reshape(spectrum.shape)


def weight_gradient(field_spec, adjoint_spec):
    field_shaped = field_spec.reshape(field_spec.shape[0], KX, 2, C)
    adjoint_shaped = adjoint_spec.reshape(adjoint_spec.shape[0], KX, 2, C)
    real_v, imag_v = (field_shaped[:, :, 0], field_shaped[:, :, 1])
    real_h, imag_h = (adjoint_shaped[:, :, 0], adjoint_shaped[:, :, 1])
    real_g = (
        real_v[:, :, :, None] * real_h[:, :, None, :]
        + imag_v[:, :, :, None] * imag_h[:, :, None, :]
    )
    imag_g = (
        real_v[:, :, :, None] * imag_h[:, :, None, :]
        - imag_v[:, :, :, None] * real_h[:, :, None, :]
    )
    return jnp.stack([real_g, imag_g], axis=2).reshape(field_spec.shape[0], KX * 2 * C * C)


def channel_mix(values, weight):
    group_size = max(1, 128 // weight.shape[0])
    block = jnp.kron(jnp.eye(group_size, dtype=weight.dtype), weight)
    rows = values.reshape(-1, block.shape[0])
    return jnp.dot(rows, block, preferred_element_type=jnp.float32).reshape(values.shape)


def spectrum(values, z_table, y_table, x_local, x_whole):
    rows_x, rows_y, _ = values.shape
    hp = lax.Precision.HIGHEST
    shaped = values.reshape(rows_x, rows_y, NZ, C)
    zpart = jnp.einsum(
        "xyzc,zpk->xypkc", shaped, z_table, preferred_element_type=jnp.float32
    ).reshape(rows_x, rows_y, 2, KZ * C)
    ypart = jnp.einsum("xyqm,yqjp->xjpm", zpart, y_table, precision=hp)
    pencil = lax.all_to_all(ypart, "gx", split_axis=1, concat_axis=0, tiled=True)
    mode_rows = pencil.shape[1]
    pencil = pencil.reshape(pencil.shape[0], mode_rows, 2, KZ, C)
    partial_value = jnp.einsum("xjqkc,xqmp->jkmpc", pencil, x_whole, precision=hp).reshape(
        mode_rows * KZ, KX * 2 * C
    )
    return lax.psum_scatter(partial_value, "gy", scatter_dimension=0, tiled=True)


def synthesis(owned, z_float, y_table, x_whole, rows_x, rows_y):
    hp = lax.Precision.HIGHEST
    planes = lax.all_gather(owned, "gy", axis=0, tiled=True)
    mode_rows = planes.shape[0] // KZ
    shaped = planes.reshape(mode_rows, KZ, KX, 2, C)
    wide = jnp.einsum("jkmqc,xpmq->xjpkc", shaped, x_whole, precision=hp).reshape(
        x_whole.shape[0], mode_rows, 2, KZ * C
    )
    slab = lax.all_to_all(wide, "gx", split_axis=0, concat_axis=1, tiled=True)
    ypart = jnp.einsum("xjqm,ypjq->xypm", slab, y_table, precision=hp).reshape(
        rows_x, rows_y, 2, KZ, C
    )
    return jnp.einsum("xypkc,zpk->xyzc", ypart, z_float, precision=hp).reshape(
        rows_x, rows_y, NZ * C
    )


def general_device(field_input, cotangent, spectral_weight, point_weight, point_bias):
    rows_x, rows_y, _ = field_input.shape
    full_x = rows_x * lax.axis_size("gx")
    full_y = rows_y * lax.axis_size("gy")
    cell_scale = 1.0 / math.sqrt(full_x * full_y * NZ)
    x_start = lax.axis_index("gx") * rows_x
    y_start = lax.axis_index("gy") * rows_y
    y_table = complex_table(
        y_start + jnp.arange(rows_y, dtype=jnp.int32), mode_values(KY, full_y), full_y, 1.0
    )
    x_local = complex_table(
        x_start + jnp.arange(rows_x, dtype=jnp.int32), mode_values(KX, full_x), full_x, cell_scale
    )
    x_whole = complex_table(
        jnp.arange(full_x, dtype=jnp.int32), mode_values(KX, full_x), full_x, cell_scale
    )
    z_plain = depth_table(NZ, KZ)
    z_double_float = doubled(z_plain)
    z_double = z_double_float.astype(jnp.bfloat16)
    field_spec = spectrum(field_input, z_plain, y_table, x_local, x_whole)
    weights = spectral_weight.astype(jnp.float32).reshape(-1, KX, 2, C, C)
    mode_output = spectral_product(field_spec, weights)
    spectral_out = synthesis(mode_output, z_double_float, y_table, x_whole, rows_x, rows_y)
    bias_row = jnp.tile(point_bias, NZ)
    preact = spectral_out + channel_mix(field_input, point_weight) + bias_row
    _, pullback = jax.vjp(jax.nn.gelu, preact)
    adjoint = pullback(cotangent.astype(jnp.float32))[0].astype(jnp.bfloat16)
    adjoint_spec = spectrum(adjoint, z_double, y_table, x_local, x_whole)
    grad_spectral = weight_gradient(field_spec, adjoint_spec) * cell_scale
    mode_adjoint = adjoint_product(adjoint_spec, weights)
    flat_field = field_input.reshape(-1, C)
    flat_adjoint = adjoint.reshape(-1, C)
    point_term = (
        jnp.einsum("rc,rd->cd", flat_field, flat_adjoint, preferred_element_type=jnp.float32)
        * cell_scale
    )
    bias_term = jnp.sum(flat_adjoint.astype(jnp.float32), axis=0) * cell_scale
    grad_point, grad_bias = lax.psum((point_term, bias_term), ("gx", "gy"))
    back_field = synthesis(
        mode_adjoint, z_plain.astype(jnp.float32), y_table, x_whole, rows_x, rows_y
    )
    grad_field = (channel_mix(adjoint, point_weight.T) + back_field).astype(jnp.bfloat16)
    return (grad_field, grad_spectral, grad_point, grad_bias)


BF = jnp.bfloat16
F32 = jnp.float32
LANES = 128
CHUNKS = KZ * C // LANES
WIDE = KZ * C
DATA_ROWS = 16 * CHUNKS
SUM_ROWS = 16


def dot(left, right, dims=((1,), (0,))):
    return lax.dot_general(left, right, (dims, ((), ())), preferred_element_type=F32)


def halves(values):
    high = values.astype(BF)
    return high, (values - high.astype(F32)).astype(BF)


def halved(values, table, dims):
    high, low = halves(values)
    both = dot(jnp.concatenate([high, low], axis=0), table, ((dims[0],), (dims[1],)))
    return both[: values.shape[0]] + both[values.shape[0] :]


def iota(shape, axis):
    return lax.broadcasted_iota(jnp.int32, shape, axis)


def lane_take(values, index):
    return jnp.take_along_axis(values, index, axis=1, mode="promise_in_bounds")


def np_halves(table):
    high = table.astype(ml_dtypes.bfloat16).astype(np.float64)
    low = (table - high).astype(ml_dtypes.bfloat16).astype(np.float64)
    return high, low


def np_modes(count, length):
    position = np.arange(count)
    return np.where(position < count // 2, position, length - count + position)


def np_angles(positions, modes, length):
    return 2.0 * np.pi * ((positions[:, None] * modes[None, :]) % length) / length


def depth_matrix():
    angles = np_angles(np.arange(NZ), np.arange(KZ), NZ)
    table = np.stack([np.cos(angles), -np.sin(angles)], axis=1).astype(ml_dtypes.bfloat16)
    table = table.astype(np.float32).reshape(NZ, 2 * KZ)
    return np.kron(table, np.eye(C, dtype=np.float32)).astype(ml_dtypes.bfloat16)


def y_tables(full_y, rows_y, rows_x, parts):
    angles = np_angles(np.arange(full_y), np_modes(KY, full_y), full_y)
    table = np.stack([np.cos(angles), -np.sin(angles)], axis=0)
    both = np.stack(np_halves(table), axis=0).reshape(2, 2, parts, rows_y, KY)
    forward = both.transpose(2, 0, 1, 4, 3).reshape(parts, 4 * KY, rows_y)
    forward = np.tile(forward, (1, 1, LANES // rows_y))
    inverse = np.repeat(both.transpose(2, 0, 3, 1, 4), rows_x, axis=-1)
    inverse = inverse.reshape(parts, 2 * rows_y, 2 * KY * rows_x)
    return forward.astype(np.float32), inverse.astype(np.float32)


def x_tables(full_x, rows_x, factor):
    angles = np_angles(np.arange(full_x), np_modes(KX, full_x), full_x)
    cosine, sine = np.cos(angles) * factor, np.sin(angles) * factor
    table = np.stack([np.stack([cosine, -sine], -1), np.stack([sine, cosine], -1)], axis=1)
    blocked = table.reshape(full_x // rows_x, rows_x, 2, KX, 2).transpose(0, 2, 1, 3, 4)
    inverse = blocked.reshape(2 * full_x, 2 * KX)
    forward = inverse.T

    def packed(matrix):
        high, low = np_halves(matrix)
        return np.concatenate([high, low, high], axis=1).astype(ml_dtypes.bfloat16)

    return packed(forward), packed(inverse)


def tripled(values):
    high, low = halves(values)
    return jnp.concatenate([high, high, low], axis=0)


def forward_matrix(table, rows_x, rows_y):
    count = table.shape[0]
    spread = jnp.broadcast_to(table[:, None, :], (count, rows_x, LANES))
    spread = spread.reshape(count * rows_x, LANES)
    spread = jnp.concatenate([spread] * (rows_x * rows_y // LANES), axis=1)
    shape = spread.shape
    return jnp.where(iota(shape, 1) // rows_y == iota(shape, 0) % rows_x, spread, 0.0).astype(BF)


def inverse_matrix(table_ref, rows_x, rows_y):
    table = table_ref[lax.axis_index("gy")]
    wide = table.shape[1]
    both = []
    for part in range(2):
        block = table[part * rows_y : (part + 1) * rows_y]
        owner = iota((rows_y, wide), 1) % rows_x
        rows = [jnp.where(owner == x, block, 0.0) for x in range(rows_x)]
        both.append(jnp.concatenate(rows, axis=0).astype(BF))
    return jnp.concatenate([both[0], both[1], both[0]], axis=1)


def y_spectrum(values, matrix):
    rows = matrix.shape[0] // 2
    both = dot(matrix, values)
    return both[:rows] + both[rows:]


def z_spectrum(planes, depth_ref, out_ref, rows_x):
    rows = KY * rows_x
    both = halved(planes, depth_ref[...], (1, 0))
    real = both[:rows, :WIDE] - both[rows:, WIDE:]
    imag = both[:rows, WIDE:] + both[rows:, :WIDE]
    for part, piece in ((0, real), (1, imag)):
        for chunk in range(CHUNKS):
            start = (chunk * 2 + part) * rows_x
            block = piece[:, chunk * LANES : (chunk + 1) * LANES]
            out_ref[:, start : start + rows_x, :] = block.reshape(KY, rows_x, LANES)


def z_synthesis(in_ref, depth_ref, rows_x):
    rows = KY * rows_x
    parts = []
    for part in range(2):
        pieces = []
        for chunk in range(CHUNKS):
            start = (chunk * 2 + part) * rows_x
            pieces.append(in_ref[:, start : start + rows_x, :].reshape(rows, LANES))
        parts.append(jnp.concatenate(pieces, axis=1))
    real, imag = parts
    stacked = jnp.concatenate(
        [jnp.concatenate([real, imag], axis=1), jnp.concatenate([imag, -real], axis=1)], axis=0
    )
    planes = halved(stacked, depth_ref[...], (1, 1))
    return tripled(planes)


def mixing_matrix(weight_ref):
    wide = 8 * C
    pick = (iota((wide, C), 0) % C == iota((wide, C), 1)).astype(F32).astype(BF)
    tall = dot(pick, weight_ref[...]).astype(BF)
    tiled = dot(tall, pick, ((1,), (1,)))
    shape = (wide, wide)
    return jnp.where(iota(shape, 0) // C == iota(shape, 1) // C, tiled, 0.0).astype(BF)


def mixed(values, matrix, dims):
    wide = matrix.shape[0]
    pieces = []
    for start in range(0, values.shape[1], wide):
        pieces.append(dot(values[:, start : start + wide], matrix, dims))
    return jnp.concatenate(pieces, axis=1)


def folded(row):
    total = row[:, :LANES]
    for start in range(LANES, row.shape[1], LANES):
        total = total + row[:, start : start + LANES]
    total = total + pltpu.roll(total, 64, 1)
    return total + pltpu.roll(total, 32, 1)


def own_spectrum(in_ref, table_ref, x_parts, y_parts):
    chunks = []
    for chunk in range(CHUNKS):
        rows = []
        for x_part in range(x_parts):
            block = [
                in_ref[x_part * y_parts + y_part, chunk * 16 : (chunk + 1) * 16, :]
                for y_part in range(y_parts)
            ]
            rows.append(functools.reduce(jnp.add, block))
        chunks.append(jnp.concatenate(rows, axis=0))
    return dot(table_ref[...], tripled(jnp.concatenate(chunks, axis=1)))


def depth_factor():
    return jnp.where(iota((1, WIDE), 1) < C, 1.0, 2.0).astype(F32)


def spread_modes(values, table_ref, out_ref, x_parts, y_parts, done=lambda x_part: None):
    cells = dot(table_ref[...], tripled(values))
    for x_part in range(x_parts):
        for chunk in range(CHUNKS):
            block = cells[x_part * 16 : (x_part + 1) * 16, chunk * LANES : (chunk + 1) * LANES]
            for y_part in range(y_parts):
                out_ref[x_part * y_parts + y_part, chunk * 16 : (chunk + 1) * 16, :] = block
        done(x_part)


def mode_row(ref, row):
    wide = jnp.broadcast_to(ref[pl.ds(row, 1), :], (KZ, WIDE))
    group = iota((KZ, LANES), 0) // 4
    chosen = wide[:, :LANES]
    for chunk in range(1, CHUNKS):
        chosen = jnp.where(group == chunk, wide[:, chunk * LANES : (chunk + 1) * LANES], chosen)
    return chosen


def in_index(step):
    return iota((KZ, LANES), 0) % 4 * C + step * 4 + iota((KZ, LANES), 1) // C


def out_index():
    return iota((KZ, LANES), 0) % 4 * C + iota((KZ, LANES), 1) % C


def own_group():
    return iota((KZ, LANES), 0) % 4 == iota((KZ, LANES), 1) // C


def gathered_rows(scratch):
    pieces = []
    for chunk in range(CHUNKS):
        terms = [scratch[pl.ds(chunk * 4 + a, 2 * KX, stride=KZ), :] for a in range(4)]
        pieces.append((terms[0] + terms[1]) + (terms[2] + terms[3]))
    return jnp.concatenate(pieces, axis=1)


def weight_parts(weight_ref, mode):
    start = pl.multiple_of(mode * 2 * C * C, LANES)
    both = weight_ref[:, pl.ds(start, 2 * C * C)].astype(F32)
    return both[:, : C * C], both[:, C * C :]


def lanes_of(values, step):
    return values[:, step * LANES : (step + 1) * LANES]


def first_kernel(
    rows_x, rows_y, field_ref, table_ref, depth_ref, out_ref, field, table, depth, gates
):
    copies = [pltpu.make_async_copy(table_ref.at[lax.axis_index("gy")], table, gates.at[0])]
    for part in range(2):
        rows = pl.ds(part * field.shape[0] // 2, field.shape[0] // 2)
        copies.append(
            pltpu.make_async_copy(field_ref.at[rows], field.at[rows], gates.at[1 + part])
        )
    for part in range(4):
        rows = pl.ds(part * depth.shape[0] // 4, depth.shape[0] // 4)
        copies.append(
            pltpu.make_async_copy(depth_ref.at[rows], depth.at[rows], gates.at[3 + part])
        )
    for copy in copies:
        copy.start()
    copies[0].wait()
    matrix = forward_matrix(table[...], rows_x, rows_y)
    copies[1].wait()
    copies[2].wait()
    planes = y_spectrum(field[...], matrix)
    for copy in copies[3:]:
        copy.wait()
    z_spectrum(planes, depth, out_ref, rows_x)


def product_kernel(
    x_parts, y_parts, in_ref, forward_ref, inverse_ref, weight_ref, out_ref, spec_ref, scratch
):
    spec_ref[...] = own_spectrum(in_ref, forward_ref, x_parts, y_parts)
    keep = own_group()

    def step(mode, carry):
        real, imag = mode_row(spec_ref, 2 * mode), mode_row(spec_ref, 2 * mode + 1)
        real_w, imag_w = weight_parts(weight_ref, mode)
        real_sum = jnp.zeros((KZ, LANES), F32)
        imag_sum = jnp.zeros((KZ, LANES), F32)
        for part in range(C // 4):
            index = in_index(part)
            real_v, imag_v = lane_take(real, index), lane_take(imag, index)
            real_p, imag_p = lanes_of(real_w, part), lanes_of(imag_w, part)
            real_sum = real_sum + (real_v * real_p - imag_v * imag_p)
            imag_sum = imag_sum + (real_v * imag_p + imag_v * real_p)
        for part, total in ((0, real_sum), (1, imag_sum)):
            start = pl.multiple_of((2 * mode + part) * KZ, KZ)
            scratch[pl.ds(start, KZ), :] = jnp.where(keep, folded(total), 0.0)
        return carry

    lax.fori_loop(0, KX, step, 0, unroll=4)
    spread_modes(gathered_rows(scratch) * depth_factor(), inverse_ref, out_ref, x_parts, y_parts)


def middle_kernel(
    rows_x,
    rows_y,
    in_ref,
    field_ref,
    cotangent_ref,
    point_ref,
    bias_ref,
    table_ref,
    back_ref,
    depth_ref,
    out_ref,
    adjoint_ref,
    sums_ref,
    held,
    gate,
):
    matrix = inverse_matrix(back_ref, rows_x, rows_y)
    spectral = dot(matrix, z_synthesis(in_ref, depth_ref, rows_x))
    mixing = mixing_matrix(point_ref)
    field = field_ref[...]
    bias = jnp.concatenate([bias_ref[...]] * NZ, axis=1)
    value = spectral + mixed(field, mixing, ((1,), (0,))) + bias
    root = math.sqrt(2.0 / math.pi)
    square = value * value
    bent = jnp.tanh(value * (root + (root * 0.044715) * square))
    slope = 0.5 * (1.0 + bent) + (0.5 * value) * (1.0 - bent * bent) * (
        root + (3.0 * root * 0.044715) * square
    )
    adjoint = (cotangent_ref[...].astype(F32) * slope).astype(BF)
    held[...] = adjoint
    copy = pltpu.make_async_copy(held, adjoint_ref, gate)
    copy.start()
    matrix = forward_matrix(table_ref[lax.axis_index("gy")], rows_x, rows_y)
    z_spectrum(y_spectrum(adjoint, matrix), depth_ref, out_ref, rows_x)
    wide = mixing.shape[0]
    total = jnp.zeros((wide, wide), F32)
    for start in range(0, NZ * C, wide):
        total = total + dot(
            field[:, start : start + wide], adjoint[:, start : start + wide], ((0,), (0,))
        )
    total = jnp.where(iota((wide, wide), 0) // C == iota((wide, wide), 1) // C, total, 0.0)
    point = total[:C]
    for start in range(C, wide, C):
        point = point + total[start : start + C]
    point = folded(point)
    group = iota((8, LANES), 1) // C
    packed = point[:8]
    for part in range(1, 4):
        packed = jnp.where(group == part, point[part * 8 : (part + 1) * 8], packed)
    sums_ref[:8, :] = packed
    sums_ref[8:, :] = folded(dot(jnp.ones((8, adjoint.shape[0]), BF), adjoint))
    copy.wait()


def swapped(values, index, distance):
    return lane_take(values, index ^ distance)


def adjoint_kernel(
    x_parts,
    y_parts,
    in_ref,
    forward_ref,
    inverse_ref,
    weight_ref,
    sums_ref,
    out_ref,
    spec_ref,
    scratch,
    staged,
    gates,
):
    spec_ref[...] = own_spectrum(in_ref, forward_ref, x_parts, y_parts) * depth_factor()
    keep = own_group()
    lane = iota((KZ, LANES), 1)
    final = lane % C % 4 * C + lane % C // 4 * 4

    def reduced(parts):
        distance = 16
        while len(parts) > 1:
            bit = (lane & distance) != 0
            half = len(parts) // 2
            merged = []
            for low, high in zip(parts[:half], parts[half:]):
                kept = jnp.where(bit, high, low)
                other = jnp.where(bit, low, high)
                merged.append(kept + swapped(other, lane, distance))
            parts = merged
            distance //= 2
        total = parts[0]
        while distance:
            total = total + swapped(total, lane, distance)
            distance //= 2
        return lane_take(total, final)

    def step(mode, carry):
        index = out_index()
        real = lane_take(mode_row(spec_ref, 2 * mode), index)
        imag = lane_take(mode_row(spec_ref, 2 * mode + 1), index)
        real_w, imag_w = weight_parts(weight_ref, mode)
        real_parts, imag_parts = [], []
        for part in range(C // 4):
            real_p, imag_p = lanes_of(real_w, part), lanes_of(imag_w, part)
            real_parts.append(real * real_p + imag * imag_p)
            imag_parts.append(imag * real_p - real * imag_p)
        for part, parts in ((0, real_parts), (1, imag_parts)):
            start = pl.multiple_of((2 * mode + part) * KZ, KZ)
            scratch[pl.ds(start, KZ), :] = jnp.where(keep, reduced(parts), 0.0)
        return carry

    lax.fori_loop(0, KX, step, 0, unroll=4)
    for device in range(x_parts * y_parts):
        staged[device, DATA_ROWS:, :] = sums_ref[...]
    stores = []

    def send(x_part):
        block = pl.ds(x_part * y_parts, y_parts)
        stores.append(
            pltpu.make_async_copy(staged.at[block], out_ref.at[block], gates.at[x_part])
        )
        stores[-1].start()

    spread_modes(gathered_rows(scratch), inverse_ref, staged, x_parts, y_parts, send)
    for store in stores:
        store.wait()


def weight_kernel(scale, field_ref, adjoint_ref, out_ref, staged, gates):
    index = out_index()
    stores = []
    turns = gates.shape[0]
    modes = KX // turns

    def step(mode, carry):
        row = 2 * mode
        real_v, imag_v = mode_row(field_ref, row), mode_row(field_ref, row + 1)
        real_h = lane_take(mode_row(adjoint_ref, row), index) * scale
        imag_h = lane_take(mode_row(adjoint_ref, row + 1), index) * scale
        real_g, imag_g = [], []
        for part in range(C // 4):
            take = in_index(part)
            real, imag = lane_take(real_v, take), lane_take(imag_v, take)
            real_g.append(real * real_h + imag * imag_h)
            imag_g.append(real * imag_h - imag * real_h)
        start = pl.multiple_of(mode * 2 * C * C, LANES)
        staged[:, pl.ds(start, 2 * C * C)] = jnp.concatenate(real_g + imag_g, axis=1)
        return carry

    for turn in range(turns):
        lax.fori_loop(turn * modes, (turn + 1) * modes, step, 0, unroll=2)
        block = pl.ds(turn * modes * 2 * C * C, modes * 2 * C * C)
        stores.append(
            pltpu.make_async_copy(staged.at[:, block], out_ref.at[:, block], gates.at[turn])
        )
        stores[-1].start()
    for store in stores:
        store.wait()


def last_kernel(
    rows_x,
    rows_y,
    scale,
    in_ref,
    adjoint_ref,
    point_ref,
    back_ref,
    depth_ref,
    out_ref,
    grad_ref,
    bias_ref,
    adjoint,
    result,
    gate,
    gates,
):
    fetch = pltpu.make_async_copy(adjoint_ref, adjoint, gate)
    fetch.start()
    total = in_ref[0, DATA_ROWS:, :]
    for device in range(1, in_ref.shape[0]):
        total = total + in_ref[device, DATA_ROWS:, :]
    total = total * scale
    packed = total[:8]
    for part in range(4):
        piece = packed if part == 0 else pltpu.roll(packed, LANES - part * C, 1)
        grad_ref[part * 8 : (part + 1) * 8, :] = piece[:, :C]
    bias_ref[...] = total[8:9, :C]
    matrix = inverse_matrix(back_ref, rows_x, rows_y)
    planes = z_synthesis(in_ref, depth_ref, rows_x)
    mixing = mixing_matrix(point_ref)
    fetch.wait()
    stores = []
    rows = result.shape[0] // gates.shape[0]
    for part in range(gates.shape[0]):
        block = pl.ds(part * rows, rows)
        mix = mixed(adjoint[block, :], mixing, ((1,), (1,)))
        spectral = dot(matrix[part * rows : (part + 1) * rows], planes)
        result[block, :] = (mix + spectral).astype(BF)
        stores.append(
            pltpu.make_async_copy(result.at[block], out_ref.at[block], gates.at[part])
        )
        stores[-1].start()
    for store in stores:
        store.wait()


NEAR = pl.BlockSpec(memory_space=pltpu.VMEM)
FAR = pl.BlockSpec(memory_space=pltpu.HBM)


def call(kernel, ins, outs, scratch=()):
    shapes = []
    for shape, kind, inner in outs:
        if inner is None:
            shapes.append(jax.ShapeDtypeStruct(shape, kind))
        else:
            shapes.append((pltpu.VMEM if inner else pltpu.HBM)(shape, kind))
    function = pl.pallas_call(
        kernel,
        out_shape=shapes,
        in_specs=[NEAR if inner else FAR for inner in ins],
        out_specs=[FAR if inner is False else NEAR for _, _, inner in outs],
        scratch_shapes=list(scratch),
        compiler_params=pltpu.CompilerParams(vmem_limit_bytes=40 * 1024 * 1024),
    )

    def run(*arguments):
        spaces = [pltpu.VMEM if inner else pltpu.HBM for inner in ins]
        return function(*map(pltpu.with_memory_space_constraint, arguments, spaces))

    return run


def exchange(values):
    return lax.all_to_all(values, ("gx", "gy"), split_axis=0, concat_axis=0, tiled=True)


def fast_device(field_input, cotangent, spectral_weight, point_weight, point_bias):
    rows_x, rows_y, depth = field_input.shape
    x_parts, y_parts = lax.axis_size("gx"), lax.axis_size("gy")
    devices = x_parts * y_parts
    full_x, full_y = rows_x * x_parts, rows_y * y_parts
    scale = 1.0 / math.sqrt(full_x * full_y * NZ)
    cells = rows_x * rows_y
    depth_table = jnp.asarray(depth_matrix())
    forward_y, inverse_y = map(jnp.asarray, y_tables(full_y, rows_y, rows_x, y_parts))
    forward_x, inverse_x = map(jnp.asarray, x_tables(full_x, rows_x, scale))
    field = field_input.reshape(cells, depth)
    bias = point_bias.reshape(1, C)
    payload = ((devices, DATA_ROWS, LANES), F32, True)
    spectrum_shape = ((2 * KX, WIDE), F32, True)
    rows_scratch = pltpu.VMEM((2 * KX * KZ, LANES), F32)
    plane = pltpu.VMEM((cells, depth), BF)
    gate = pltpu.SemaphoreType.DMA(())

    (sent,) = call(
        functools.partial(first_kernel, rows_x, rows_y),
        [False] * 3,
        [payload],
        [
            plane,
            pltpu.VMEM(forward_y.shape[1:], F32),
            pltpu.VMEM(depth_table.shape, BF),
            pltpu.SemaphoreType.DMA((7,)),
        ],
    )(field, forward_y, depth_table)
    sent, field_modes = call(
        functools.partial(product_kernel, x_parts, y_parts),
        [True] * 4,
        [payload, spectrum_shape],
        [rows_scratch],
    )(exchange(sent), forward_x, inverse_x, spectral_weight)
    sent, adjoint, sums = call(
        functools.partial(middle_kernel, rows_x, rows_y),
        [True] * 8,
        [payload, ((cells, depth), BF, False), ((SUM_ROWS, LANES), F32, True)],
        [plane, gate],
    )(
        exchange(sent),
        field,
        cotangent.reshape(cells, depth),
        point_weight,
        bias,
        forward_y,
        inverse_y,
        depth_table,
    )
    sent, adjoint_modes = call(
        functools.partial(adjoint_kernel, x_parts, y_parts),
        [True] * 5,
        [((devices, DATA_ROWS + SUM_ROWS, LANES), F32, False), spectrum_shape],
        [
            rows_scratch,
            pltpu.VMEM((devices, DATA_ROWS + SUM_ROWS, LANES), F32),
            pltpu.SemaphoreType.DMA((x_parts,)),
        ],
    )(exchange(sent), forward_x, inverse_x, spectral_weight, sums)
    wide = (KZ, KX * 2 * C * C)
    (grad_spectral,) = call(
        functools.partial(weight_kernel, scale),
        [True, True],
        [(wide, F32, False)],
        [pltpu.VMEM(wide, F32), pltpu.SemaphoreType.DMA((4,))],
    )(field_modes, adjoint_modes)
    chunks = 4
    grad_field, grad_point, grad_bias = call(
        functools.partial(last_kernel, rows_x, rows_y, scale),
        [True, False, True, True, True],
        [((cells, depth), BF, False), ((C, C), F32, None), ((1, C), F32, None)],
        [plane, plane, gate, pltpu.SemaphoreType.DMA((chunks,))],
    )(exchange(sent), adjoint, point_weight, inverse_y, depth_table)
    return (
        grad_field.reshape(field_input.shape),
        grad_spectral,
        grad_point,
        grad_bias.reshape(C),
    )


def on_device(*arguments):
    rows_x, rows_y, _ = arguments[0].shape
    if rows_x == 8 and rows_y == 64 and arguments[2].shape[0] == KZ:
        return fast_device(*arguments)
    return general_device(*arguments)


def solution(mesh):
    return jax.shard_map(
        on_device,
        mesh=mesh,
        in_specs=(
            P(("groups", "gx"), "gy", None),
            P(("groups", "gx"), "gy", None),
            P(("gx", "gy"), None),
            P(),
            P(),
        ),
        out_specs=(
            P(("groups", "gx"), "gy", None),
            P(("groups", "gx", "gy"), None),
            P("groups", None),
            P("groups"),
        ),
        check_vma=False,
    )
```

```python
import functools
import math

import jax
import jax.numpy as jnp
import ml_dtypes
import numpy as np
from jax import lax
from jax.experimental import pallas as pl
from jax.experimental.pallas import tpu as pltpu
from jax.sharding import PartitionSpec as P

C = 32
KX = 16
KY = 16
KZ = 16
NZ = 32


def mode_values(mode_count, length):
    position = jnp.arange(mode_count, dtype=jnp.int32)
    return jnp.where(position < mode_count // 2, position, length - mode_count + position)


def phase_angles(positions, wavenumbers, length):
    steps = positions[:, None] * wavenumbers[None, :] % length
    return 2.0 * math.pi / length * steps.astype(jnp.float32)


def complex_table(positions, wavenumbers, length, factor):
    angles = phase_angles(positions, wavenumbers, length)
    cosine = jnp.cos(angles) * factor
    sine = jnp.sin(angles) * factor
    return jnp.stack(
        [jnp.stack([cosine, -sine], axis=-1), jnp.stack([sine, cosine], axis=-1)], axis=1
    )


def depth_table(depth_count, mode_count):
    angles = phase_angles(
        jnp.arange(depth_count, dtype=jnp.int32),
        jnp.arange(mode_count, dtype=jnp.int32),
        depth_count,
    )
    return jnp.stack([jnp.cos(angles), -jnp.sin(angles)], axis=1).astype(jnp.bfloat16)


def doubled(table):
    factor = jnp.where(jnp.arange(table.shape[2]) == 0, 1.0, 2.0).astype(jnp.float32)
    return table.astype(jnp.float32) * factor[None, None, :]


def spectral_product(spectrum, weights):
    shaped = spectrum.reshape(spectrum.shape[0], KX, 2, C)
    real_in, imag_in = (shaped[:, :, 0], shaped[:, :, 1])
    real_w, imag_w = (weights[:, :, 0], weights[:, :, 1])
    hp = lax.Precision.HIGHEST
    real_out = jnp.einsum("rmi,rmio->rmo", real_in, real_w, precision=hp) - jnp.einsum(
        "rmi,rmio->rmo", imag_in, imag_w, precision=hp
    )
    imag_out = jnp.einsum("rmi,rmio->rmo", real_in, imag_w, precision=hp) + jnp.einsum(
        "rmi,rmio->rmo", imag_in, real_w, precision=hp
    )
    return jnp.stack([real_out, imag_out], axis=2).reshape(spectrum.shape)


def adjoint_product(spectrum, weights):
    shaped = spectrum.reshape(spectrum.shape[0], KX, 2, C)
    real_in, imag_in = (shaped[:, :, 0], shaped[:, :, 1])
    real_w, imag_w = (weights[:, :, 0], weights[:, :, 1])
    hp = lax.Precision.HIGHEST
    real_out = jnp.einsum("rmo,rmio->rmi", real_in, real_w, precision=hp) + jnp.einsum(
        "rmo,rmio->rmi", imag_in, imag_w, precision=hp
    )
    imag_out = jnp.einsum("rmo,rmio->rmi", imag_in, real_w, precision=hp) - jnp.einsum(
        "rmo,rmio->rmi", real_in, imag_w, precision=hp
    )
    return jnp.stack([real_out, imag_out], axis=2).reshape(spectrum.shape)


def weight_gradient(field_spec, adjoint_spec):
    field_shaped = field_spec.reshape(field_spec.shape[0], KX, 2, C)
    adjoint_shaped = adjoint_spec.reshape(adjoint_spec.shape[0], KX, 2, C)
    real_v, imag_v = (field_shaped[:, :, 0], field_shaped[:, :, 1])
    real_h, imag_h = (adjoint_shaped[:, :, 0], adjoint_shaped[:, :, 1])
    real_g = (
        real_v[:, :, :, None] * real_h[:, :, None, :]
        + imag_v[:, :, :, None] * imag_h[:, :, None, :]
    )
    imag_g = (
        real_v[:, :, :, None] * imag_h[:, :, None, :]
        - imag_v[:, :, :, None] * real_h[:, :, None, :]
    )
    return jnp.stack([real_g, imag_g], axis=2).reshape(field_spec.shape[0], KX * 2 * C * C)


def channel_mix(values, weight):
    group_size = max(1, 128 // weight.shape[0])
    block = jnp.kron(jnp.eye(group_size, dtype=weight.dtype), weight)
    rows = values.reshape(-1, block.shape[0])
    return jnp.dot(rows, block, preferred_element_type=jnp.float32).reshape(values.shape)


def spectrum(values, z_table, y_table, x_local, x_whole):
    rows_x, rows_y, _ = values.shape
    hp = lax.Precision.HIGHEST
    shaped = values.reshape(rows_x, rows_y, NZ, C)
    zpart = jnp.einsum(
        "xyzc,zpk->xypkc", shaped, z_table, preferred_element_type=jnp.float32
    ).reshape(rows_x, rows_y, 2, KZ * C)
    ypart = jnp.einsum("xyqm,yqjp->xjpm", zpart, y_table, precision=hp)
    pencil = lax.all_to_all(ypart, "gx", split_axis=1, concat_axis=0, tiled=True)
    mode_rows = pencil.shape[1]
    pencil = pencil.reshape(pencil.shape[0], mode_rows, 2, KZ, C)
    partial_value = jnp.einsum("xjqkc,xqmp->jkmpc", pencil, x_whole, precision=hp).reshape(
        mode_rows * KZ, KX * 2 * C
    )
    return lax.psum_scatter(partial_value, "gy", scatter_dimension=0, tiled=True)


def synthesis(owned, z_float, y_table, x_whole, rows_x, rows_y):
    hp = lax.Precision.HIGHEST
    planes = lax.all_gather(owned, "gy", axis=0, tiled=True)
    mode_rows = planes.shape[0] // KZ
    shaped = planes.reshape(mode_rows, KZ, KX, 2, C)
    wide = jnp.einsum("jkmqc,xpmq->xjpkc", shaped, x_whole, precision=hp).reshape(
        x_whole.shape[0], mode_rows, 2, KZ * C
    )
    slab = lax.all_to_all(wide, "gx", split_axis=0, concat_axis=1, tiled=True)
    ypart = jnp.einsum("xjqm,ypjq->xypm", slab, y_table, precision=hp).reshape(
        rows_x, rows_y, 2, KZ, C
    )
    return jnp.einsum("xypkc,zpk->xyzc", ypart, z_float, precision=hp).reshape(
        rows_x, rows_y, NZ * C
    )


def general_device(field_input, cotangent, spectral_weight, point_weight, point_bias):
    rows_x, rows_y, _ = field_input.shape
    full_x = rows_x * lax.axis_size("gx")
    full_y = rows_y * lax.axis_size("gy")
    cell_scale = 1.0 / math.sqrt(full_x * full_y * NZ)
    x_start = lax.axis_index("gx") * rows_x
    y_start = lax.axis_index("gy") * rows_y
    y_table = complex_table(
        y_start + jnp.arange(rows_y, dtype=jnp.int32), mode_values(KY, full_y), full_y, 1.0
    )
    x_local = complex_table(
        x_start + jnp.arange(rows_x, dtype=jnp.int32), mode_values(KX, full_x), full_x, cell_scale
    )
    x_whole = complex_table(
        jnp.arange(full_x, dtype=jnp.int32), mode_values(KX, full_x), full_x, cell_scale
    )
    z_plain = depth_table(NZ, KZ)
    z_double_float = doubled(z_plain)
    z_double = z_double_float.astype(jnp.bfloat16)
    field_spec = spectrum(field_input, z_plain, y_table, x_local, x_whole)
    weights = spectral_weight.astype(jnp.float32).reshape(-1, KX, 2, C, C)
    mode_output = spectral_product(field_spec, weights)
    spectral_out = synthesis(mode_output, z_double_float, y_table, x_whole, rows_x, rows_y)
    bias_row = jnp.tile(point_bias, NZ)
    preact = spectral_out + channel_mix(field_input, point_weight) + bias_row
    _, pullback = jax.vjp(jax.nn.gelu, preact)
    adjoint = pullback(cotangent.astype(jnp.float32))[0].astype(jnp.bfloat16)
    adjoint_spec = spectrum(adjoint, z_double, y_table, x_local, x_whole)
    grad_spectral = weight_gradient(field_spec, adjoint_spec) * cell_scale
    mode_adjoint = adjoint_product(adjoint_spec, weights)
    flat_field = field_input.reshape(-1, C)
    flat_adjoint = adjoint.reshape(-1, C)
    point_term = (
        jnp.einsum("rc,rd->cd", flat_field, flat_adjoint, preferred_element_type=jnp.float32)
        * cell_scale
    )
    bias_term = jnp.sum(flat_adjoint.astype(jnp.float32), axis=0) * cell_scale
    grad_point, grad_bias = lax.psum((point_term, bias_term), ("gx", "gy"))
    back_field = synthesis(
        mode_adjoint, z_plain.astype(jnp.float32), y_table, x_whole, rows_x, rows_y
    )
    grad_field = (channel_mix(adjoint, point_weight.T) + back_field).astype(jnp.bfloat16)
    return (grad_field, grad_spectral, grad_point, grad_bias)


BF = jnp.bfloat16
F32 = jnp.float32
LANES = 128
CHUNKS = KZ * C // LANES
WIDE = KZ * C
SUM_ROWS = 16


def dot(left, right, dims=((1,), (0,))):
    return lax.dot_general(left, right, (dims, ((), ())), preferred_element_type=F32)


def halves(values):
    high = values.astype(BF)
    return high, (values - high.astype(F32)).astype(BF)


def halved(values, table, dims):
    high, low = halves(values)
    both = dot(jnp.concatenate([high, low], axis=0), table, ((dims[0],), (dims[1],)))
    return both[: values.shape[0]] + both[values.shape[0] :]


def iota(shape, axis):
    return lax.broadcasted_iota(jnp.int32, shape, axis)


def lane_take(values, index):
    return jnp.take_along_axis(values, index, axis=1, mode="promise_in_bounds")


def np_halves(table):
    high = table.astype(ml_dtypes.bfloat16).astype(np.float64)
    low = (table - high).astype(ml_dtypes.bfloat16).astype(np.float64)
    return high, low


def np_modes(count, length):
    position = np.arange(count)
    return np.where(position < count // 2, position, length - count + position)


def np_angles(positions, modes, length):
    return 2.0 * np.pi * ((positions[:, None] * modes[None, :]) % length) / length


def depth_rows():
    angles = np_angles(np.arange(NZ), np.arange(KZ), NZ)
    table = np.stack([np.cos(angles), -np.sin(angles)], axis=1).astype(ml_dtypes.bfloat16)
    return np.repeat(table.astype(np.float32).reshape(NZ, 2 * KZ), C, axis=1)


def y_tables(full_y, rows_y, x_parts, y_parts):
    angles = np_angles(np.arange(full_y), np_modes(KY, full_y), full_y)
    table = np.stack([np.cos(angles), -np.sin(angles)], axis=-1)
    high, low = np_halves(table)
    forward, inverse = [], []
    for device in range(x_parts * y_parts):
        own_x, own_y = device // y_parts, device % y_parts
        order = [
            (own_x ^ turn) * y_parts + (own_y ^ step)
            for turn in range(x_parts)
            for step in range(y_parts)
        ]
        rows = slice(own_y * rows_y, (own_y + 1) * rows_y)

        def picked(values):
            block = values[rows][:, order].reshape(rows_y, x_parts, y_parts, 2)
            return block.transpose(0, 1, 3, 2).reshape(rows_y, 2 * KY)

        forward.append(np.concatenate([picked(high), picked(low)], axis=1).T)
        inverse.append(np.concatenate([picked(high), picked(low), picked(high)], axis=1))
    return tuple(np.stack(part).astype(ml_dtypes.bfloat16) for part in (forward, inverse))


def x_tables(full_x, rows_x, factor, y_parts):
    angles = np_angles(np.arange(full_x), np_modes(KX, full_x), full_x)
    cosine, sine = np.cos(angles) * factor, np.sin(angles) * factor
    table = np.stack([np.stack([cosine, -sine], -1), np.stack([sine, cosine], -1)], axis=1)
    blocked = table.reshape(full_x // rows_x, rows_x * 2, KX * 2)
    same = np.eye(y_parts)

    def packed(spread):
        high, low = np_halves(spread)
        return np.concatenate([high, low, high], axis=2).astype(ml_dtypes.bfloat16)

    forward = np.einsum("grm,de->gdmre", blocked, same)
    inverse = np.einsum("grm,de->grdem", blocked, same)
    parts, rows, modes = blocked.shape
    return (
        packed(forward.reshape(parts, y_parts * modes, rows * y_parts)),
        packed(inverse.reshape(parts, rows * y_parts, y_parts * modes)),
    )


def tripled(values):
    high, low = halves(values)
    return jnp.concatenate([high, high, low], axis=0)


def lanes_of(values, step):
    return values[:, step * LANES : (step + 1) * LANES]


def read_lanes(ref, rows):
    pieces = [ref[i * rows : (i + 1) * rows, :] for i in range(CHUNKS)]
    return jnp.concatenate(pieces, axis=1)


def write_lanes(ref, values, rows, start=0):
    for chunk in range(CHUNKS):
        first = chunk * rows + start
        ref[first : first + values.shape[0], :] = lanes_of(values, chunk)


def turned(values):
    tiles = values.reshape(values.shape[0] // 8, 8, values.shape[1])
    return pltpu.roll(tiles, 4, 1).reshape(values.shape)


def part_sign(rows):
    return jnp.where(iota((rows, 1), 0) % 8 < 4, -1.0, 1.0).astype(F32)


def y_spectrum(values, table, rows_x, rows_y):
    planes = []
    half = table.shape[0] // 2
    for x in range(rows_x):
        both = dot(table, values[x * rows_y : (x + 1) * rows_y])
        planes.append(both[:half] + both[half:])
    return jnp.concatenate(planes, axis=0)


def z_spectrum(planes, depth_ref, out_refs, rows_x):
    both = halved(planes, depth_ref[...], (1, 0))
    whole = both[:, :WIDE] + part_sign(planes.shape[0]) * turned(both[:, WIDE:])
    turns = len(out_refs)
    for x in range(rows_x):
        for turn in range(turns):
            block = whole[(x * turns + turn) * 8 : (x * turns + turn + 1) * 8]
            write_lanes(out_refs[turn], block, rows_x * 8, x * 8)


def z_synthesis(in_refs, depth_ref, rows_x):
    blocks = [read_lanes(ref, rows_x * 8) for ref in in_refs]
    modes = jnp.concatenate(blocks, axis=0)
    other = -part_sign(modes.shape[0]) * turned(modes)
    return halved(jnp.concatenate([modes, other], axis=1), depth_ref[...], (1, 1))


def y_synthesis(planes, table, x, rows_x):
    turns = planes.shape[0] // (8 * rows_x)
    rows = [(turn * rows_x + x) * 8 for turn in range(turns)]
    return dot(table, tripled(jnp.concatenate([planes[r : r + 8] for r in rows], axis=0)))


def mixing_matrix(weight_ref):
    wide = 8 * C
    pick = (iota((wide, C), 0) % C == iota((wide, C), 1)).astype(F32).astype(BF)
    tall = dot(pick, weight_ref[...]).astype(BF)
    tiled = dot(tall, pick, ((1,), (1,)))
    shape = (wide, wide)
    return jnp.where(iota(shape, 0) // C == iota(shape, 1) // C, tiled, 0.0).astype(BF)


def mixed(values, matrix, dims):
    wide = matrix.shape[0]
    pieces = []
    for start in range(0, values.shape[1], wide):
        pieces.append(dot(values[:, start : start + wide], matrix, dims))
    return jnp.concatenate(pieces, axis=1)


def folded(row):
    total = row[:, :LANES]
    for start in range(LANES, row.shape[1], LANES):
        total = total + row[:, start : start + LANES]
    total = total + pltpu.roll(total, 64, 1)
    return total + pltpu.roll(total, 32, 1)


def depth_factor():
    return jnp.where(iota((1, WIDE), 1) < C, 1.0, 2.0).astype(F32)


def mode_row(ref, row):
    wide = jnp.broadcast_to(ref[pl.ds(row, 1), :], (KZ, WIDE))
    group = iota((KZ, LANES), 0) // 4
    chosen = wide[:, :LANES]
    for chunk in range(1, CHUNKS):
        chosen = jnp.where(group == chunk, wide[:, chunk * LANES : (chunk + 1) * LANES], chosen)
    return chosen


def in_index(step):
    return iota((KZ, LANES), 0) % 4 * C + step * 4 + iota((KZ, LANES), 1) // C


def out_index():
    return iota((KZ, LANES), 0) % 4 * C + iota((KZ, LANES), 1) % C


def own_group():
    return iota((KZ, LANES), 0) % 4 == iota((KZ, LANES), 1) // C


def gathered_rows(scratch):
    pieces = []
    for chunk in range(CHUNKS):
        terms = [scratch[pl.ds(chunk * 4 + a, 2 * KX, stride=KZ), :] for a in range(4)]
        pieces.append((terms[0] + terms[1]) + (terms[2] + terms[3]))
    return jnp.concatenate(pieces, axis=1)


def weight_parts(weight_ref, mode):
    start = pl.multiple_of(mode * 2 * C * C, LANES)
    both = weight_ref[:, pl.ds(start, 2 * C * C)].astype(F32)
    return both[:, : C * C], both[:, C * C :]


def device_index():
    return lax.axis_index("gx") * lax.axis_size("gy") + lax.axis_index("gy")


def fill_depth(rows_ref, depth_ref):
    count, wide = rows_ref.shape
    same = iota((C, wide), 0) == iota((C, wide), 1) % C
    for z in range(count):
        row = jnp.broadcast_to(rows_ref[z : z + 1, :], (C, wide))
        depth_ref[z * C : (z + 1) * C, :] = jnp.where(same, row, 0.0).astype(BF)


def first_kernel(
    rows_x,
    rows_y,
    field_ref,
    table_ref,
    rows_ref,
    point_ref,
    back_ref,
    modes_ref,
    cells_ref,
    *refs,
):
    out_refs, refs = refs[:-10], refs[-10:]
    depth, mixing_ref, table, back, to_modes, to_cells, field, rows, point, gates = refs
    device = device_index()
    half = field.shape[0] // 2
    pairs = [(rows_ref, rows), (point_ref, point), (table_ref.at[device], table)]
    for part in range(2):
        block = pl.ds(part * half, half)
        pairs.append((field_ref.at[block], field.at[block]))
    pairs += [(back_ref.at[device], back), (modes_ref, to_modes), (cells_ref, to_cells)]
    copies = [
        pltpu.make_async_copy(source, target, gates.at[turn])
        for turn, (source, target) in enumerate(pairs)
    ]
    for copy in copies:
        copy.start()
    copies[0].wait()
    fill_depth(rows, depth)
    copies[1].wait()
    mixing_ref[...] = mixing_matrix(point)
    for copy in copies[2:5]:
        copy.wait()
    z_spectrum(y_spectrum(field[...], table[...], rows_x, rows_y), depth, out_refs, rows_x)
    for copy in copies[5:]:
        copy.wait()


def x_forward_kernel(turns, table_ref, *refs):
    in_refs, refs = refs[:turns], refs[turns:]
    rows = table_ref.shape[2] // 3
    own = lax.axis_index("gx")
    total = None
    for turn in range(turns):
        term = dot(table_ref[own ^ turn], tripled(read_lanes(in_refs[turn], rows)))
        total = term if total is None else total + term
    modes = 2 * KX
    steps = total.shape[0] // modes
    for step, ref in enumerate(refs[-steps:]):
        write_lanes(ref, total[step * modes : (step + 1) * modes], modes)
        if len(refs) > steps:
            ref[CHUNKS * modes :, :] = refs[0][...]


def x_inverse_kernel(steps, turns, table_ref, *refs):
    in_refs, refs = refs[:steps], refs[steps:]
    values = tripled(jnp.concatenate([read_lanes(ref, 2 * KX) for ref in in_refs], axis=0))
    own = lax.axis_index("gx")
    rows = table_ref.shape[1]
    for turn, ref in enumerate(refs[-turns:]):
        write_lanes(ref, dot(table_ref[own ^ turn], values), rows)
        if len(refs) > turns:
            ref[CHUNKS * rows :, :] = refs[0][...]


def summed_modes(in_refs):
    return functools.reduce(jnp.add, [read_lanes(ref, 2 * KX) for ref in in_refs])


def product_kernel(steps, weight_ref, *refs):
    in_refs, (out_ref, spec_ref, scratch) = refs[:steps], refs[steps:]
    spec_ref[...] = summed_modes(in_refs)
    keep = own_group()

    def step(mode, carry):
        real, imag = mode_row(spec_ref, 2 * mode), mode_row(spec_ref, 2 * mode + 1)
        real_w, imag_w = weight_parts(weight_ref, mode)
        real_sum = jnp.zeros((KZ, LANES), F32)
        imag_sum = jnp.zeros((KZ, LANES), F32)
        for part in range(C // 4):
            index = in_index(part)
            real_v, imag_v = lane_take(real, index), lane_take(imag, index)
            real_p, imag_p = lanes_of(real_w, part), lanes_of(imag_w, part)
            real_sum = real_sum + (real_v * real_p - imag_v * imag_p)
            imag_sum = imag_sum + (real_v * imag_p + imag_v * real_p)
        for part, total in ((0, real_sum), (1, imag_sum)):
            start = pl.multiple_of((2 * mode + part) * KZ, KZ)
            scratch[pl.ds(start, KZ), :] = jnp.where(keep, folded(total), 0.0)
        return carry

    lax.fori_loop(0, KX, step, 0, unroll=4)
    write_lanes(out_ref, gathered_rows(scratch) * depth_factor(), 2 * KX)


def point_kernel(field_ref, mixing_ref, bias_ref, out_ref):
    bias = jnp.concatenate([bias_ref[...]] * NZ, axis=1)
    out_ref[...] = mixed(field_ref[...], mixing_ref[...], ((1,), (0,))) + bias


def middle_kernel(
    rows_x,
    rows_y,
    turns,
    base_ref,
    cotangent_ref,
    table_ref,
    back_ref,
    depth_ref,
    *refs,
):
    in_refs, out_refs, (adjoint_ref, value_ref) = refs[:turns], refs[turns:-2], refs[-2:]
    planes = z_synthesis(in_refs, depth_ref, rows_x)
    for x in range(rows_x):
        block = slice(x * rows_y, (x + 1) * rows_y)
        spectral = y_synthesis(planes, back_ref[...], x, rows_x)
        value_ref[block, :] = spectral + base_ref[block, :]
    value = value_ref[...]
    root = math.sqrt(2.0 / math.pi)
    square = value * value
    bent = jnp.tanh(value * (root + (root * 0.044715) * square))
    tail = value * (root + (3.0 * root * 0.044715) * square)
    slope = (0.5 + 0.5 * bent) * (1.0 + (1.0 - bent) * tail)
    adjoint = (cotangent_ref[...].astype(F32) * slope).astype(BF)
    adjoint_ref[...] = adjoint
    z_spectrum(y_spectrum(adjoint, table_ref[...], rows_x, rows_y), depth_ref, out_refs, rows_x)


def sums_kernel(field_ref, adjoint_ref, mixing_ref, out_ref, sums_ref):
    field, adjoint, mixing = field_ref[...], adjoint_ref[...], mixing_ref[...]
    out_ref[...] = mixed(adjoint, mixing, ((1,), (1,)))
    wide = mixing.shape[0]
    total = jnp.zeros((wide, wide), F32)
    for start in range(0, NZ * C, wide):
        total = total + dot(
            field[:, start : start + wide], adjoint[:, start : start + wide], ((0,), (0,))
        )
    total = jnp.where(iota((wide, wide), 0) // C == iota((wide, wide), 1) // C, total, 0.0)
    point = total[:C]
    for start in range(C, wide, C):
        point = point + total[start : start + C]
    point = folded(point)
    group = iota((8, LANES), 1) // C
    packed = point[:8]
    for part in range(1, 4):
        packed = jnp.where(group == part, point[part * 8 : (part + 1) * 8], packed)
    sums_ref[:8, :] = packed
    sums_ref[8:, :] = folded(dot(jnp.ones((8, adjoint.shape[0]), BF), adjoint))


def swapped(values, index, distance):
    return lane_take(values, index ^ distance)


def adjoint_kernel(steps, weight_ref, *refs):
    in_refs, (out_ref, spec_ref, sums_ref, scratch) = refs[:steps], refs[steps:]
    spec_ref[...] = summed_modes(in_refs) * depth_factor()
    sums_ref[...] = functools.reduce(jnp.add, [ref[CHUNKS * 2 * KX :, :] for ref in in_refs])
    keep = own_group()
    lane = iota((KZ, LANES), 1)
    final = lane % C % 4 * C + lane % C // 4 * 4

    def reduced(parts):
        distance = 16
        while len(parts) > 1:
            bit = (lane & distance) != 0
            half = len(parts) // 2
            merged = []
            for low, high in zip(parts[:half], parts[half:]):
                kept = jnp.where(bit, high, low)
                other = jnp.where(bit, low, high)
                merged.append(kept + swapped(other, lane, distance))
            parts = merged
            distance //= 2
        total = parts[0]
        while distance:
            total = total + swapped(total, lane, distance)
            distance //= 2
        return lane_take(total, final)

    def step(mode, carry):
        index = out_index()
        real = lane_take(mode_row(spec_ref, 2 * mode), index)
        imag = lane_take(mode_row(spec_ref, 2 * mode + 1), index)
        real_w, imag_w = weight_parts(weight_ref, mode)
        real_parts, imag_parts = [], []
        for part in range(C // 4):
            real_p, imag_p = lanes_of(real_w, part), lanes_of(imag_w, part)
            real_parts.append(real * real_p + imag * imag_p)
            imag_parts.append(imag * real_p - real * imag_p)
        for part, parts in ((0, real_parts), (1, imag_parts)):
            start = pl.multiple_of((2 * mode + part) * KZ, KZ)
            scratch[pl.ds(start, KZ), :] = jnp.where(keep, reduced(parts), 0.0)
        return carry

    lax.fori_loop(0, KX, step, 0, unroll=4)
    write_lanes(out_ref, gathered_rows(scratch), 2 * KX)


def weight_kernel(scale, field_ref, adjoint_ref, out_ref, staged, gates):
    index = out_index()
    stores = []
    turns = gates.shape[0]
    modes = KX // turns

    def step(mode, carry):
        row = 2 * mode
        real_v, imag_v = mode_row(field_ref, row), mode_row(field_ref, row + 1)
        real_h = lane_take(mode_row(adjoint_ref, row), index) * scale
        imag_h = lane_take(mode_row(adjoint_ref, row + 1), index) * scale
        real_g, imag_g = [], []
        for part in range(C // 4):
            take = in_index(part)
            real, imag = lane_take(real_v, take), lane_take(imag_v, take)
            real_g.append(real * real_h + imag * imag_h)
            imag_g.append(real * imag_h - imag * real_h)
        start = pl.multiple_of(mode * 2 * C * C, LANES)
        staged[:, pl.ds(start, 2 * C * C)] = jnp.concatenate(real_g + imag_g, axis=1)
        return carry

    for turn in range(turns):
        lax.fori_loop(turn * modes, (turn + 1) * modes, step, 0, unroll=2)
        block = pl.ds(turn * modes * 2 * C * C, modes * 2 * C * C)
        stores.append(
            pltpu.make_async_copy(staged.at[:, block], out_ref.at[:, block], gates.at[turn])
        )
        stores[-1].start()
    for store in stores:
        store.wait()


def last_kernel(rows_x, rows_y, turns, scale, mixed_ref, back_ref, depth_ref, *refs):
    in_refs, (out_ref, point_ref, bias_ref, result, gates) = refs[:turns], refs[turns:]
    total = functools.reduce(jnp.add, [ref[ref.shape[0] - SUM_ROWS :, :] for ref in in_refs])
    total = total * scale
    packed = total[:8]
    for part in range(4):
        piece = packed if part == 0 else pltpu.roll(packed, LANES - part * C, 1)
        point_ref[part * 8 : (part + 1) * 8, :] = piece[:, :C]
    bias_ref[...] = total[8:9, :C]
    planes = z_synthesis(in_refs, depth_ref, rows_x)
    stores = []
    parts = gates.shape[0]
    for x in range(rows_x):
        block = slice(x * rows_y, (x + 1) * rows_y)
        spectral = y_synthesis(planes, back_ref[...], x, rows_x)
        result[block, :] = (mixed_ref[block, :] + spectral).astype(BF)
        if (x + 1) % (rows_x // parts) == 0:
            part = (x + 1) // (rows_x // parts) - 1
            rows = result.shape[0] // parts
            span = pl.ds(part * rows, rows)
            stores.append(
                pltpu.make_async_copy(result.at[span], out_ref.at[span], gates.at[part])
            )
            stores[-1].start()
    for store in stores:
        store.wait()


NEAR = pl.BlockSpec(memory_space=pltpu.VMEM)
FAR = pl.BlockSpec(memory_space=pltpu.HBM)


def call(kernel, ins, outs, scratch=()):
    shapes = []
    for shape, kind, inner in outs:
        if inner is None:
            shapes.append(jax.ShapeDtypeStruct(shape, kind))
        else:
            shapes.append((pltpu.VMEM if inner else pltpu.HBM)(shape, kind))
    function = pl.pallas_call(
        kernel,
        out_shape=shapes,
        in_specs=[NEAR if inner else FAR for inner in ins],
        out_specs=[FAR if inner is False else NEAR for _, _, inner in outs],
        scratch_shapes=list(scratch),
        compiler_params=pltpu.CompilerParams(vmem_limit_bytes=40 * 1024 * 1024),
    )

    def run(*arguments):
        spaces = [pltpu.VMEM if inner else pltpu.HBM for inner in ins]
        return function(*map(pltpu.with_memory_space_constraint, arguments, spaces))

    return run


def exchange(blocks, axis):
    count = lax.axis_size(axis)
    order = [2, 3, 1] if count == 4 else list(range(1, count))
    received = list(blocks)
    for turn in order:
        pairs = [(device, device ^ turn) for device in range(count)]
        received[turn] = lax.ppermute(blocks[turn], axis, pairs)
    return received


def fast_device(field_input, cotangent, spectral_weight, point_weight, point_bias):
    rows_x, rows_y, depth = field_input.shape
    x_parts, y_parts = lax.axis_size("gx"), lax.axis_size("gy")
    full_x, full_y = rows_x * x_parts, rows_y * y_parts
    scale = 1.0 / math.sqrt(full_x * full_y * NZ)
    cells = rows_x * rows_y
    z_rows = jnp.asarray(depth_rows())
    forward_y, inverse_y = map(jnp.asarray, y_tables(full_y, rows_y, x_parts, y_parts))
    forward_x, inverse_x = map(jnp.asarray, x_tables(full_x, rows_x, scale, y_parts))
    field = field_input.reshape(cells, depth)
    bias = point_bias.reshape(1, C)
    cell_rows, mode_rows = CHUNKS * rows_x * 8, CHUNKS * 2 * KX
    cell_block, mode_block = ((cell_rows, LANES), F32, True), ((mode_rows, LANES), F32, True)
    cell_sums = ((cell_rows + SUM_ROWS, LANES), F32, True)
    mode_sums = ((mode_rows + SUM_ROWS, LANES), F32, True)
    spectrum_shape = ((2 * KX, WIDE), F32, True)
    rows_scratch = pltpu.VMEM((2 * KX * KZ, LANES), F32)
    sums_shape = ((SUM_ROWS, LANES), F32, True)
    cell_shape = ((cells, depth), F32, True)
    wide = (KZ, KX * 2 * C * C)

    def forward(blocks, extra, mode_shape):
        received = exchange(blocks, "gx")
        sent = call(
            functools.partial(x_forward_kernel, x_parts),
            [True] * (1 + x_parts + len(extra)),
            [mode_shape] * y_parts,
        )(to_modes, *received, *extra)
        return exchange(sent, "gy")

    def inverse(block, extra, cell_shape):
        received = exchange([block] * y_parts, "gy")
        sent = call(
            functools.partial(x_inverse_kernel, y_parts, x_parts),
            [True] * (1 + y_parts + len(extra)),
            [cell_shape] * x_parts,
        )(to_cells, *received, *extra)
        return exchange(sent, "gx")

    *blocks, depth_table, mixing, table, back, to_modes, to_cells = call(
        functools.partial(first_kernel, rows_x, rows_y),
        [False] * 7,
        [cell_block] * x_parts
        + [((depth, 2 * WIDE), BF, True), ((8 * C, 8 * C), BF, True)]
        + [(part.shape[1:], BF, True) for part in (forward_y, inverse_y)]
        + [(part.shape, BF, True) for part in (forward_x, inverse_x)],
        [
            pltpu.VMEM((cells, depth), BF),
            pltpu.VMEM(z_rows.shape, F32),
            pltpu.VMEM((C, C), BF),
            pltpu.SemaphoreType.DMA((8,)),
        ],
    )(field, forward_y, z_rows, point_weight, inverse_y, forward_x, inverse_x)
    (base,) = call(point_kernel, [True] * 3, [cell_shape])(field, mixing, bias)
    block, field_modes = call(
        functools.partial(product_kernel, y_parts),
        [True] * (1 + y_parts),
        [mode_block, spectrum_shape],
        [rows_scratch],
    )(spectral_weight, *forward(blocks, [], mode_block))
    *blocks, adjoint = call(
        functools.partial(middle_kernel, rows_x, rows_y, x_parts),
        [True] * (5 + x_parts),
        [cell_block] * x_parts + [((cells, depth), BF, True)],
        [pltpu.VMEM((cells, depth), F32)],
    )(
        base,
        cotangent.reshape(cells, depth),
        table,
        back,
        depth_table,
        *inverse(block, [], cell_block),
    )
    mixed_adjoint, sums = call(sums_kernel, [True] * 3, [cell_shape, sums_shape])(
        field, adjoint, mixing
    )
    block, adjoint_modes, sums = call(
        functools.partial(adjoint_kernel, y_parts),
        [True] * (1 + y_parts),
        [mode_block, spectrum_shape, sums_shape],
        [rows_scratch],
    )(spectral_weight, *forward(blocks, [sums], mode_sums))
    (grad_spectral,) = call(
        functools.partial(weight_kernel, scale),
        [True] * 2,
        [(wide, F32, False)],
        [pltpu.VMEM(wide, F32), pltpu.SemaphoreType.DMA((4,))],
    )(field_modes, adjoint_modes)
    grad_field, grad_point, grad_bias = call(
        functools.partial(last_kernel, rows_x, rows_y, x_parts, scale),
        [True] * (3 + x_parts),
        [((cells, depth), BF, False), ((C, C), F32, None), ((1, C), F32, None)],
        [pltpu.VMEM((cells, depth), BF), pltpu.SemaphoreType.DMA((4,))],
    )(mixed_adjoint, back, depth_table, *inverse(block, [sums], cell_sums))
    return (
        grad_field.reshape(field_input.shape),
        grad_spectral,
        grad_point,
        grad_bias.reshape(C),
    )


def on_device(*arguments):
    rows_x, rows_y, _ = arguments[0].shape
    x_parts, y_parts = lax.axis_size("gx"), lax.axis_size("gy")
    whole_modes = arguments[2].shape[0] == KZ and y_parts == 4 and x_parts == 4
    if whole_modes and rows_x == 8 and rows_y == 64:
        return fast_device(*arguments)
    return general_device(*arguments)


def solution(mesh):
    return jax.shard_map(
        on_device,
        mesh=mesh,
        in_specs=(
            P(("groups", "gx"), "gy", None),
            P(("groups", "gx"), "gy", None),
            P(("gx", "gy"), None),
            P(),
            P(),
        ),
        out_specs=(
            P(("groups", "gx"), "gy", None),
            P(("groups", "gx", "gy"), None),
            P("groups", None),
            P("groups"),
        ),
        check_vma=False,
    )
```

```python
import functools
import math

import jax
import jax.numpy as jnp
import ml_dtypes
import numpy as np
from jax import lax
from jax.experimental import pallas as pl
from jax.experimental.pallas import tpu as pltpu
from jax.sharding import PartitionSpec as P

C = 32
KX = 16
KY = 16
KZ = 16
NZ = 32


def mode_values(mode_count, length):
    position = jnp.arange(mode_count, dtype=jnp.int32)
    return jnp.where(position < mode_count // 2, position, length - mode_count + position)


def phase_angles(positions, wavenumbers, length):
    steps = positions[:, None] * wavenumbers[None, :] % length
    return 2.0 * math.pi / length * steps.astype(jnp.float32)


def complex_table(positions, wavenumbers, length, factor):
    angles = phase_angles(positions, wavenumbers, length)
    cosine = jnp.cos(angles) * factor
    sine = jnp.sin(angles) * factor
    return jnp.stack(
        [jnp.stack([cosine, -sine], axis=-1), jnp.stack([sine, cosine], axis=-1)], axis=1
    )


def depth_table(depth_count, mode_count):
    angles = phase_angles(
        jnp.arange(depth_count, dtype=jnp.int32),
        jnp.arange(mode_count, dtype=jnp.int32),
        depth_count,
    )
    return jnp.stack([jnp.cos(angles), -jnp.sin(angles)], axis=1).astype(jnp.bfloat16)


def doubled(table):
    factor = jnp.where(jnp.arange(table.shape[2]) == 0, 1.0, 2.0).astype(jnp.float32)
    return table.astype(jnp.float32) * factor[None, None, :]


def spectral_product(spectrum, weights):
    shaped = spectrum.reshape(spectrum.shape[0], KX, 2, C)
    real_in, imag_in = (shaped[:, :, 0], shaped[:, :, 1])
    real_w, imag_w = (weights[:, :, 0], weights[:, :, 1])
    hp = lax.Precision.HIGHEST
    real_out = jnp.einsum("rmi,rmio->rmo", real_in, real_w, precision=hp) - jnp.einsum(
        "rmi,rmio->rmo", imag_in, imag_w, precision=hp
    )
    imag_out = jnp.einsum("rmi,rmio->rmo", real_in, imag_w, precision=hp) + jnp.einsum(
        "rmi,rmio->rmo", imag_in, real_w, precision=hp
    )
    return jnp.stack([real_out, imag_out], axis=2).reshape(spectrum.shape)


def adjoint_product(spectrum, weights):
    shaped = spectrum.reshape(spectrum.shape[0], KX, 2, C)
    real_in, imag_in = (shaped[:, :, 0], shaped[:, :, 1])
    real_w, imag_w = (weights[:, :, 0], weights[:, :, 1])
    hp = lax.Precision.HIGHEST
    real_out = jnp.einsum("rmo,rmio->rmi", real_in, real_w, precision=hp) + jnp.einsum(
        "rmo,rmio->rmi", imag_in, imag_w, precision=hp
    )
    imag_out = jnp.einsum("rmo,rmio->rmi", imag_in, real_w, precision=hp) - jnp.einsum(
        "rmo,rmio->rmi", real_in, imag_w, precision=hp
    )
    return jnp.stack([real_out, imag_out], axis=2).reshape(spectrum.shape)


def weight_gradient(field_spec, adjoint_spec):
    field_shaped = field_spec.reshape(field_spec.shape[0], KX, 2, C)
    adjoint_shaped = adjoint_spec.reshape(adjoint_spec.shape[0], KX, 2, C)
    real_v, imag_v = (field_shaped[:, :, 0], field_shaped[:, :, 1])
    real_h, imag_h = (adjoint_shaped[:, :, 0], adjoint_shaped[:, :, 1])
    real_g = (
        real_v[:, :, :, None] * real_h[:, :, None, :]
        + imag_v[:, :, :, None] * imag_h[:, :, None, :]
    )
    imag_g = (
        real_v[:, :, :, None] * imag_h[:, :, None, :]
        - imag_v[:, :, :, None] * real_h[:, :, None, :]
    )
    return jnp.stack([real_g, imag_g], axis=2).reshape(field_spec.shape[0], KX * 2 * C * C)


def channel_mix(values, weight):
    group_size = max(1, 128 // weight.shape[0])
    block = jnp.kron(jnp.eye(group_size, dtype=weight.dtype), weight)
    rows = values.reshape(-1, block.shape[0])
    return jnp.dot(rows, block, preferred_element_type=jnp.float32).reshape(values.shape)


def spectrum(values, z_table, y_table, x_local, x_whole):
    rows_x, rows_y, _ = values.shape
    hp = lax.Precision.HIGHEST
    shaped = values.reshape(rows_x, rows_y, NZ, C)
    zpart = jnp.einsum(
        "xyzc,zpk->xypkc", shaped, z_table, preferred_element_type=jnp.float32
    ).reshape(rows_x, rows_y, 2, KZ * C)
    ypart = jnp.einsum("xyqm,yqjp->xjpm", zpart, y_table, precision=hp)
    pencil = lax.all_to_all(ypart, "gx", split_axis=1, concat_axis=0, tiled=True)
    mode_rows = pencil.shape[1]
    pencil = pencil.reshape(pencil.shape[0], mode_rows, 2, KZ, C)
    partial_value = jnp.einsum("xjqkc,xqmp->jkmpc", pencil, x_whole, precision=hp).reshape(
        mode_rows * KZ, KX * 2 * C
    )
    return lax.psum_scatter(partial_value, "gy", scatter_dimension=0, tiled=True)


def synthesis(owned, z_float, y_table, x_whole, rows_x, rows_y):
    hp = lax.Precision.HIGHEST
    planes = lax.all_gather(owned, "gy", axis=0, tiled=True)
    mode_rows = planes.shape[0] // KZ
    shaped = planes.reshape(mode_rows, KZ, KX, 2, C)
    wide = jnp.einsum("jkmqc,xpmq->xjpkc", shaped, x_whole, precision=hp).reshape(
        x_whole.shape[0], mode_rows, 2, KZ * C
    )
    slab = lax.all_to_all(wide, "gx", split_axis=0, concat_axis=1, tiled=True)
    ypart = jnp.einsum("xjqm,ypjq->xypm", slab, y_table, precision=hp).reshape(
        rows_x, rows_y, 2, KZ, C
    )
    return jnp.einsum("xypkc,zpk->xyzc", ypart, z_float, precision=hp).reshape(
        rows_x, rows_y, NZ * C
    )


def general_device(field_input, cotangent, spectral_weight, point_weight, point_bias):
    rows_x, rows_y, _ = field_input.shape
    full_x = rows_x * lax.axis_size("gx")
    full_y = rows_y * lax.axis_size("gy")
    cell_scale = 1.0 / math.sqrt(full_x * full_y * NZ)
    x_start = lax.axis_index("gx") * rows_x
    y_start = lax.axis_index("gy") * rows_y
    y_table = complex_table(
        y_start + jnp.arange(rows_y, dtype=jnp.int32), mode_values(KY, full_y), full_y, 1.0
    )
    x_local = complex_table(
        x_start + jnp.arange(rows_x, dtype=jnp.int32), mode_values(KX, full_x), full_x, cell_scale
    )
    x_whole = complex_table(
        jnp.arange(full_x, dtype=jnp.int32), mode_values(KX, full_x), full_x, cell_scale
    )
    z_plain = depth_table(NZ, KZ)
    z_double_float = doubled(z_plain)
    z_double = z_double_float.astype(jnp.bfloat16)
    field_spec = spectrum(field_input, z_plain, y_table, x_local, x_whole)
    weights = spectral_weight.astype(jnp.float32).reshape(-1, KX, 2, C, C)
    mode_output = spectral_product(field_spec, weights)
    spectral_out = synthesis(mode_output, z_double_float, y_table, x_whole, rows_x, rows_y)
    bias_row = jnp.tile(point_bias, NZ)
    preact = spectral_out + channel_mix(field_input, point_weight) + bias_row
    _, pullback = jax.vjp(jax.nn.gelu, preact)
    adjoint = pullback(cotangent.astype(jnp.float32))[0].astype(jnp.bfloat16)
    adjoint_spec = spectrum(adjoint, z_double, y_table, x_local, x_whole)
    grad_spectral = weight_gradient(field_spec, adjoint_spec) * cell_scale
    mode_adjoint = adjoint_product(adjoint_spec, weights)
    flat_field = field_input.reshape(-1, C)
    flat_adjoint = adjoint.reshape(-1, C)
    point_term = (
        jnp.einsum("rc,rd->cd", flat_field, flat_adjoint, preferred_element_type=jnp.float32)
        * cell_scale
    )
    bias_term = jnp.sum(flat_adjoint.astype(jnp.float32), axis=0) * cell_scale
    grad_point, grad_bias = lax.psum((point_term, bias_term), ("gx", "gy"))
    back_field = synthesis(
        mode_adjoint, z_plain.astype(jnp.float32), y_table, x_whole, rows_x, rows_y
    )
    grad_field = (channel_mix(adjoint, point_weight.T) + back_field).astype(jnp.bfloat16)
    return (grad_field, grad_spectral, grad_point, grad_bias)


BF = jnp.bfloat16
F32 = jnp.float32
LANES = 128
CHUNKS = KZ * C // LANES
WIDE = KZ * C
SUM_ROWS = 16


def dot(left, right, dims=((1,), (0,))):
    return lax.dot_general(left, right, (dims, ((), ())), preferred_element_type=F32)


def halves(values):
    high = values.astype(BF)
    return high, (values - high.astype(F32)).astype(BF)


def halved(values, table, dims):
    high, low = halves(values)
    both = dot(jnp.concatenate([high, low], axis=0), table, ((dims[0],), (dims[1],)))
    return both[: values.shape[0]] + both[values.shape[0] :]


def iota(shape, axis):
    return lax.broadcasted_iota(jnp.int32, shape, axis)


def lane_take(values, index):
    return jnp.take_along_axis(values, index, axis=1, mode="promise_in_bounds")


def np_halves(table):
    high = table.astype(ml_dtypes.bfloat16).astype(np.float64)
    low = (table - high).astype(ml_dtypes.bfloat16).astype(np.float64)
    return high, low


def np_modes(count, length):
    position = np.arange(count)
    return np.where(position < count // 2, position, length - count + position)


def np_angles(positions, modes, length):
    return 2.0 * np.pi * ((positions[:, None] * modes[None, :]) % length) / length


def depth_rows():
    angles = np_angles(np.arange(NZ), np.arange(KZ), NZ)
    table = np.stack([np.cos(angles), -np.sin(angles)], axis=1).astype(ml_dtypes.bfloat16)
    return np.repeat(table.astype(np.float32).reshape(NZ, 2 * KZ), C, axis=1)


def spread_table():
    hit = np.repeat(np.eye(C, dtype=np.float32), C, axis=1)
    return np.tile(hit, (LANES // C, 1)).astype(ml_dtypes.bfloat16)


def y_tables(full_y, rows_y, x_parts, y_parts):
    angles = np_angles(np.arange(full_y), np_modes(KY, full_y), full_y)
    table = np.stack([np.cos(angles), -np.sin(angles)], axis=-1)
    high, low = np_halves(table)
    forward, inverse = [], []
    for device in range(x_parts * y_parts):
        own_x, own_y = device // y_parts, device % y_parts
        order = [
            (own_x ^ turn) * y_parts + (own_y ^ step)
            for turn in range(x_parts)
            for step in range(y_parts)
        ]
        rows = slice(own_y * rows_y, (own_y + 1) * rows_y)

        def picked(values):
            block = values[rows][:, order].reshape(rows_y, x_parts, y_parts, 2)
            return block.transpose(0, 1, 3, 2).reshape(rows_y, 2 * KY)

        forward.append(np.concatenate([picked(high), picked(low)], axis=1).T)
        inverse.append(np.concatenate([picked(high), picked(low), picked(high)], axis=1))
    return tuple(np.stack(part).astype(ml_dtypes.bfloat16) for part in (forward, inverse))


def x_tables(full_x, rows_x, factor, y_parts):
    angles = np_angles(np.arange(full_x), np_modes(KX, full_x), full_x)
    cosine, sine = np.cos(angles) * factor, np.sin(angles) * factor
    table = np.stack([np.stack([cosine, -sine], -1), np.stack([sine, cosine], -1)], axis=1)
    blocked = table.reshape(full_x // rows_x, rows_x * 2, KX * 2)
    same = np.eye(y_parts)

    def packed(spread):
        high, low = np_halves(spread)
        return np.concatenate([high, low, high], axis=2).astype(ml_dtypes.bfloat16)

    forward = np.einsum("grm,de->gdmre", blocked, same)
    inverse = np.einsum("grm,de->grdem", blocked, same)
    parts, rows, modes = blocked.shape
    return (
        packed(forward.reshape(parts, y_parts * modes, rows * y_parts)),
        packed(inverse.reshape(parts, rows * y_parts, y_parts * modes)),
    )


def tripled(values):
    high, low = halves(values)
    return jnp.concatenate([high, high, low], axis=0)


def lanes_of(values, step):
    return values[:, step * LANES : (step + 1) * LANES]


def read_lanes(ref, rows):
    pieces = [ref[i * rows : (i + 1) * rows, :] for i in range(CHUNKS)]
    return jnp.concatenate(pieces, axis=1)


def write_lanes(ref, values, rows, start=0):
    for chunk in range(CHUNKS):
        first = chunk * rows + start
        ref[first : first + values.shape[0], :] = lanes_of(values, chunk)


def turned(values):
    tiles = values.reshape(values.shape[0] // 8, 8, values.shape[1])
    return pltpu.roll(tiles, 4, 1).reshape(values.shape)


def part_sign(rows):
    return jnp.where(iota((rows, 1), 0) % 8 < 4, -1.0, 1.0).astype(F32)


def y_spectrum(values, table, rows_x, rows_y):
    planes = []
    half = table.shape[0] // 2
    for x in range(rows_x):
        both = dot(table, values[x * rows_y : (x + 1) * rows_y])
        planes.append(both[:half] + both[half:])
    return jnp.concatenate(planes, axis=0)


def z_spectrum(both, out_refs, rows_x):
    whole = both[:, :WIDE] + part_sign(both.shape[0]) * turned(both[:, WIDE:])
    turns = len(out_refs)
    for x in range(rows_x):
        for turn in range(turns):
            block = whole[(x * turns + turn) * 8 : (x * turns + turn + 1) * 8]
            write_lanes(out_refs[turn], block, rows_x * 8, x * 8)


def z_synthesis(in_refs, depth_ref, rows_x, exact=True):
    blocks = [read_lanes(ref, rows_x * 8) for ref in in_refs]
    modes = jnp.concatenate(blocks, axis=0)
    other = -part_sign(modes.shape[0]) * turned(modes)
    stacked = jnp.concatenate([modes, other], axis=1)
    if exact:
        return halved(stacked, depth_ref[...], (1, 1))
    return dot(stacked.astype(BF), depth_ref[...], ((1,), (1,)))


def y_synthesis(planes, table, x, rows_x):
    turns = planes.shape[0] // (8 * rows_x)
    rows = [(turn * rows_x + x) * 8 for turn in range(turns)]
    return dot(table, tripled(jnp.concatenate([planes[r : r + 8] for r in rows], axis=0)))


def mixing_matrix(weight_ref):
    wide = 8 * C
    pick = (iota((wide, C), 0) % C == iota((wide, C), 1)).astype(F32).astype(BF)
    tall = dot(pick, weight_ref[...]).astype(BF)
    tiled = dot(tall, pick, ((1,), (1,)))
    shape = (wide, wide)
    return jnp.where(iota(shape, 0) // C == iota(shape, 1) // C, tiled, 0.0).astype(BF)


def mixed(values, matrix, dims):
    wide = matrix.shape[0]
    pieces = []
    for start in range(0, values.shape[1], wide):
        pieces.append(dot(values[:, start : start + wide], matrix, dims))
    return jnp.concatenate(pieces, axis=1)


def folded(row):
    total = row[:, :LANES]
    for start in range(LANES, row.shape[1], LANES):
        total = total + row[:, start : start + LANES]
    total = total + pltpu.roll(total, 64, 1)
    return total + pltpu.roll(total, 32, 1)


def depth_factor():
    return jnp.where(iota((1, WIDE), 1) < C, 1.0, 2.0).astype(F32)


def mode_row(ref, row):
    wide = jnp.broadcast_to(ref[pl.ds(row, 1), :], (KZ, WIDE))
    group = iota((KZ, LANES), 0) // 4
    chosen = wide[:, :LANES]
    for chunk in range(1, CHUNKS):
        chosen = jnp.where(group == chunk, wide[:, chunk * LANES : (chunk + 1) * LANES], chosen)
    return chosen


def in_index(step):
    return iota((KZ, LANES), 0) % 4 * C + step * 4 + iota((KZ, LANES), 1) // C


def out_index():
    return iota((KZ, LANES), 0) % 4 * C + iota((KZ, LANES), 1) % C


def own_group():
    return iota((KZ, LANES), 0) % 4 == iota((KZ, LANES), 1) // C


def gathered_rows(scratch):
    pieces = []
    for chunk in range(CHUNKS):
        terms = [scratch[pl.ds(chunk * 4 + a, 2 * KX, stride=KZ), :] for a in range(4)]
        pieces.append((terms[0] + terms[1]) + (terms[2] + terms[3]))
    return jnp.concatenate(pieces, axis=1)


def weight_parts(weight_ref, mode):
    start = pl.multiple_of(mode * 2 * C * C, LANES)
    both = weight_ref[:, pl.ds(start, 2 * C * C)].astype(F32)
    return both[:, : C * C], both[:, C * C :]


def device_index():
    return lax.axis_index("gx") * lax.axis_size("gy") + lax.axis_index("gy")


def fill_depth(rows_ref, depth_ref):
    count, wide = rows_ref.shape
    same = iota((C, wide), 0) == iota((C, wide), 1) % C
    for z in range(count):
        row = jnp.broadcast_to(rows_ref[z : z + 1, :], (C, wide))
        depth_ref[z * C : (z + 1) * C, :] = jnp.where(same, row, 0.0).astype(BF)


def first_kernel(
    rows_x,
    rows_y,
    field_ref,
    table_ref,
    rows_ref,
    point_ref,
    back_ref,
    modes_ref,
    cells_ref,
    spread_ref,
    *refs,
):
    out_refs, refs = refs[:-11], refs[-11:]
    depth, mixing_ref, table, back, to_modes, to_cells, spread, field, rows, point, gates = refs
    device = device_index()
    half = field.shape[0] // 2
    pairs = [(rows_ref, rows), (point_ref, point), (table_ref.at[device], table)]
    for part in range(2):
        block = pl.ds(part * half, half)
        pairs.append((field_ref.at[block], field.at[block]))
    pairs += [(back_ref.at[device], back), (modes_ref, to_modes), (cells_ref, to_cells)]
    pairs += [(spread_ref, spread)]
    copies = [
        pltpu.make_async_copy(source, target, gates.at[turn])
        for turn, (source, target) in enumerate(pairs)
    ]
    for copy in copies:
        copy.start()
    copies[0].wait()
    fill_depth(rows, depth)
    copies[1].wait()
    mixing_ref[...] = mixing_matrix(point)
    for copy in copies[2:5]:
        copy.wait()
    planes = y_spectrum(field[...], table[...], rows_x, rows_y)
    z_spectrum(halved(planes, depth[...], (1, 0)), out_refs, rows_x)
    for copy in copies[5:]:
        copy.wait()


def x_forward_kernel(turns, table_ref, *refs):
    in_refs, refs = refs[:turns], refs[turns:]
    rows = table_ref.shape[2] // 3
    own = lax.axis_index("gx")
    total = None
    for turn in range(turns):
        term = dot(table_ref[own ^ turn], tripled(read_lanes(in_refs[turn], rows)))
        total = term if total is None else total + term
    modes = 2 * KX
    steps = total.shape[0] // modes
    for step, ref in enumerate(refs[-steps:]):
        write_lanes(ref, total[step * modes : (step + 1) * modes], modes)
        if len(refs) > steps:
            ref[CHUNKS * modes :, :] = refs[0][...]


def x_inverse_kernel(steps, turns, table_ref, *refs):
    in_refs, refs = refs[:steps], refs[steps:]
    values = tripled(jnp.concatenate([read_lanes(ref, 2 * KX) for ref in in_refs], axis=0))
    own = lax.axis_index("gx")
    rows = table_ref.shape[1]
    for turn, ref in enumerate(refs[-turns:]):
        write_lanes(ref, dot(table_ref[own ^ turn], values), rows)
        if len(refs) > turns:
            ref[CHUNKS * rows :, :] = refs[0][...]


def summed_modes(in_refs):
    return functools.reduce(jnp.add, [read_lanes(ref, 2 * KX) for ref in in_refs])


def stacked_modes(ref):
    keep = own_group()
    rows = [jnp.where(keep, mode_row(ref, row), 0.0) for row in range(2 * KX)]
    return jnp.concatenate(rows, axis=0)


def product_kernel(steps, weight_ref, spread_ref, *refs):
    in_refs, (out_ref, spec_ref, scratch, wide) = refs[:steps], refs[steps:]
    spec_ref[...] = summed_modes(in_refs)
    high, low = halves(stacked_modes(spec_ref))
    spread = spread_ref[...]
    wide[...] = dot(
        jnp.concatenate([high, low], axis=1), jnp.concatenate([spread, spread], axis=0)
    )

    def step(mode, carry):
        real_w, imag_w = weight_parts(weight_ref, mode)
        start = pl.multiple_of(2 * mode * KZ, 2 * KZ)
        both = wide[pl.ds(start, 2 * KZ), :]
        real_sum = jnp.zeros((KZ, LANES), F32)
        imag_sum = jnp.zeros((KZ, LANES), F32)
        for part in range(C // 4):
            real_v, imag_v = lanes_of(both[:KZ], part), lanes_of(both[KZ:], part)
            real_p, imag_p = lanes_of(real_w, part), lanes_of(imag_w, part)
            real_sum = real_sum + (real_v * real_p - imag_v * imag_p)
            imag_sum = imag_sum + (real_v * imag_p + imag_v * real_p)
        scratch[pl.ds(start, 2 * KZ), :] = jnp.concatenate([real_sum, imag_sum], axis=0)
        return carry

    lax.fori_loop(0, KX, step, 0, unroll=4)
    shape = (LANES, LANES)
    same = (iota(shape, 0) % C == iota(shape, 1) % C).astype(F32).astype(BF)
    high, low = halves(scratch[...])
    total = dot(jnp.concatenate([high, low], axis=1), jnp.concatenate([same, same], axis=0))
    scratch[...] = own_rows(total)
    write_lanes(out_ref, gathered_rows(scratch) * depth_factor(), 2 * KX)


def own_rows(values):
    keep = iota(values.shape, 0) % 4 == iota(values.shape, 1) // C
    return jnp.where(keep, values, 0.0)


def point_kernel(field_ref, mixing_ref, bias_ref, out_ref):
    bias = jnp.concatenate([bias_ref[...]] * NZ, axis=1)
    out_ref[...] = mixed(field_ref[...], mixing_ref[...], ((1,), (0,))) + bias


def middle_kernel(
    rows_x,
    rows_y,
    turns,
    base_ref,
    cotangent_ref,
    table_ref,
    back_ref,
    depth_ref,
    *refs,
):
    in_refs, out_refs, (adjoint_ref, value_ref) = refs[:turns], refs[turns:-2], refs[-2:]
    planes = z_synthesis(in_refs, depth_ref, rows_x)
    for x in range(rows_x):
        block = slice(x * rows_y, (x + 1) * rows_y)
        spectral = y_synthesis(planes, back_ref[...], x, rows_x)
        value_ref[block, :] = spectral + base_ref[block, :]
    value = value_ref[...]
    root = math.sqrt(2.0 / math.pi)
    square = value * value
    bent = jnp.tanh(value * (root + (root * 0.044715) * square))
    tail = value * (root + (3.0 * root * 0.044715) * square)
    slope = (0.5 + 0.5 * bent) * (1.0 + (1.0 - bent) * tail)
    adjoint = (cotangent_ref[...].astype(F32) * slope).astype(BF)
    adjoint_ref[...] = adjoint
    modes = y_spectrum(adjoint, table_ref[...], rows_x, rows_y).astype(BF)
    z_spectrum(dot(modes, depth_ref[...]), out_refs, rows_x)


def sums_kernel(field_ref, adjoint_ref, mixing_ref, out_ref, sums_ref):
    field, adjoint, mixing = field_ref[...], adjoint_ref[...], mixing_ref[...]
    out_ref[...] = mixed(adjoint, mixing, ((1,), (1,)))
    wide = mixing.shape[0]
    total = jnp.zeros((wide, wide), F32)
    for start in range(0, NZ * C, wide):
        total = total + dot(
            field[:, start : start + wide], adjoint[:, start : start + wide], ((0,), (0,))
        )
    total = jnp.where(iota((wide, wide), 0) // C == iota((wide, wide), 1) // C, total, 0.0)
    point = total[:C]
    for start in range(C, wide, C):
        point = point + total[start : start + C]
    point = folded(point)
    group = iota((8, LANES), 1) // C
    packed = point[:8]
    for part in range(1, 4):
        packed = jnp.where(group == part, point[part * 8 : (part + 1) * 8], packed)
    sums_ref[:8, :] = packed
    sums_ref[8:, :] = folded(dot(jnp.ones((8, adjoint.shape[0]), BF), adjoint))


def adjoint_kernel(steps, weight_ref, spread_ref, *refs):
    in_refs, (out_ref, spec_ref, sums_ref, scratch, wide) = refs[:steps], refs[steps:]
    spec_ref[...] = summed_modes(in_refs) * depth_factor()
    sums_ref[...] = functools.reduce(jnp.add, [ref[CHUNKS * 2 * KX :, :] for ref in in_refs])
    index = out_index()

    def step(mode, carry):
        real = lane_take(mode_row(spec_ref, 2 * mode), index)
        imag = lane_take(mode_row(spec_ref, 2 * mode + 1), index)
        real_w, imag_w = weight_parts(weight_ref, mode)
        real_parts, imag_parts = [], []
        for part in range(C // 4):
            real_p, imag_p = lanes_of(real_w, part), lanes_of(imag_w, part)
            real_parts.append(real * real_p + imag * imag_p)
            imag_parts.append(imag * real_p - real * imag_p)
        both = jnp.concatenate(
            [jnp.concatenate(real_parts, axis=1), jnp.concatenate(imag_parts, axis=1)], axis=0
        )
        high, low = halves(both)
        start = pl.multiple_of(2 * mode * KZ, 2 * KZ)
        wide[0, pl.ds(start, 2 * KZ), :] = high
        wide[1, pl.ds(start, 2 * KZ), :] = low
        return carry

    lax.fori_loop(0, KX, step, 0, unroll=4)
    total = dot(wide[0], spread_ref[...], ((1,), (1,)))
    total = total + dot(wide[1], spread_ref[...], ((1,), (1,)))
    scratch[...] = own_rows(total)
    write_lanes(out_ref, gathered_rows(scratch), 2 * KX)


def weight_kernel(scale, field_ref, adjoint_ref, out_ref, staged, gates):
    index = out_index()
    stores = []
    turns = gates.shape[0]
    modes = KX // turns

    def step(mode, carry):
        row = 2 * mode
        real_v, imag_v = mode_row(field_ref, row), mode_row(field_ref, row + 1)
        real_h = lane_take(mode_row(adjoint_ref, row), index) * scale
        imag_h = lane_take(mode_row(adjoint_ref, row + 1), index) * scale
        real_g, imag_g = [], []
        for part in range(C // 4):
            take = in_index(part)
            real, imag = lane_take(real_v, take), lane_take(imag_v, take)
            real_g.append(real * real_h + imag * imag_h)
            imag_g.append(real * imag_h - imag * real_h)
        start = pl.multiple_of(mode * 2 * C * C, LANES)
        staged[:, pl.ds(start, 2 * C * C)] = jnp.concatenate(real_g + imag_g, axis=1)
        return carry

    for turn in range(turns):
        lax.fori_loop(turn * modes, (turn + 1) * modes, step, 0, unroll=2)
        block = pl.ds(turn * modes * 2 * C * C, modes * 2 * C * C)
        stores.append(
            pltpu.make_async_copy(staged.at[:, block], out_ref.at[:, block], gates.at[turn])
        )
        stores[-1].start()
    for store in stores:
        store.wait()


def last_kernel(rows_x, rows_y, turns, scale, mixed_ref, back_ref, depth_ref, *refs):
    in_refs, (out_ref, point_ref, bias_ref, result, gates) = refs[:turns], refs[turns:]
    total = functools.reduce(jnp.add, [ref[ref.shape[0] - SUM_ROWS :, :] for ref in in_refs])
    total = total * scale
    packed = total[:8]
    for part in range(4):
        piece = packed if part == 0 else pltpu.roll(packed, LANES - part * C, 1)
        point_ref[part * 8 : (part + 1) * 8, :] = piece[:, :C]
    bias_ref[...] = total[8:9, :C]
    planes = z_synthesis(in_refs, depth_ref, rows_x, exact=False)
    stores = []
    for x in range(rows_x):
        block = slice(x * rows_y, (x + 1) * rows_y)
        spectral = y_synthesis(planes, back_ref[...], x, rows_x)
        result[block, :] = (mixed_ref[block, :] + spectral).astype(BF)
        span = pl.ds(x * rows_y, rows_y)
        stores.append(pltpu.make_async_copy(result.at[span], out_ref.at[span], gates.at[x]))
        stores[-1].start()
    for store in stores:
        store.wait()


NEAR = pl.BlockSpec(memory_space=pltpu.VMEM)
FAR = pl.BlockSpec(memory_space=pltpu.HBM)


def call(kernel, ins, outs, scratch=()):
    shapes = []
    for shape, kind, inner in outs:
        if inner is None:
            shapes.append(jax.ShapeDtypeStruct(shape, kind))
        else:
            shapes.append((pltpu.VMEM if inner else pltpu.HBM)(shape, kind))
    function = pl.pallas_call(
        kernel,
        out_shape=shapes,
        in_specs=[NEAR if inner else FAR for inner in ins],
        out_specs=[FAR if inner is False else NEAR for _, _, inner in outs],
        scratch_shapes=list(scratch),
        compiler_params=pltpu.CompilerParams(vmem_limit_bytes=40 * 1024 * 1024),
    )

    def run(*arguments):
        spaces = [pltpu.VMEM if inner else pltpu.HBM for inner in ins]
        return function(*map(pltpu.with_memory_space_constraint, arguments, spaces))

    return run


def exchange(blocks, axis):
    count = lax.axis_size(axis)
    order = [2, 3, 1] if count == 4 else list(range(1, count))
    received = list(blocks)
    for turn in order:
        pairs = [(device, device ^ turn) for device in range(count)]
        received[turn] = lax.ppermute(blocks[turn], axis, pairs)
    return received


def fast_device(field_input, cotangent, spectral_weight, point_weight, point_bias):
    rows_x, rows_y, depth = field_input.shape
    x_parts, y_parts = lax.axis_size("gx"), lax.axis_size("gy")
    full_x, full_y = rows_x * x_parts, rows_y * y_parts
    scale = 1.0 / math.sqrt(full_x * full_y * NZ)
    cells = rows_x * rows_y
    z_rows = jnp.asarray(depth_rows())
    spread_hits = jnp.asarray(spread_table())
    forward_y, inverse_y = map(jnp.asarray, y_tables(full_y, rows_y, x_parts, y_parts))
    forward_x, inverse_x = map(jnp.asarray, x_tables(full_x, rows_x, scale, y_parts))
    field = field_input.reshape(cells, depth)
    bias = point_bias.reshape(1, C)
    cell_rows, mode_rows = CHUNKS * rows_x * 8, CHUNKS * 2 * KX
    cell_block, mode_block = ((cell_rows, LANES), F32, True), ((mode_rows, LANES), F32, True)
    cell_sums = ((cell_rows + SUM_ROWS, LANES), F32, True)
    mode_sums = ((mode_rows + SUM_ROWS, LANES), F32, True)
    spectrum_shape = ((2 * KX, WIDE), F32, True)
    rows_scratch = pltpu.VMEM((2 * KX * KZ, LANES), F32)
    sums_shape = ((SUM_ROWS, LANES), F32, True)
    cell_shape = ((cells, depth), F32, True)
    wide = (KZ, KX * 2 * C * C)

    def forward(blocks, extra, mode_shape):
        received = exchange(blocks, "gx")
        sent = call(
            functools.partial(x_forward_kernel, x_parts),
            [True] * (1 + x_parts + len(extra)),
            [mode_shape] * y_parts,
        )(to_modes, *received, *extra)
        return exchange(sent, "gy")

    def inverse(block, extra, cell_shape):
        received = exchange([block] * y_parts, "gy")
        sent = call(
            functools.partial(x_inverse_kernel, y_parts, x_parts),
            [True] * (1 + y_parts + len(extra)),
            [cell_shape] * x_parts,
        )(to_cells, *received, *extra)
        return exchange(sent, "gx")

    *blocks, depth_table, mixing, table, back, to_modes, to_cells, spread = call(
        functools.partial(first_kernel, rows_x, rows_y),
        [False] * 8,
        [cell_block] * x_parts
        + [((depth, 2 * WIDE), BF, True), ((8 * C, 8 * C), BF, True)]
        + [(part.shape[1:], BF, True) for part in (forward_y, inverse_y)]
        + [(part.shape, BF, True) for part in (forward_x, inverse_x, spread_hits)],
        [
            pltpu.VMEM((cells, depth), BF),
            pltpu.VMEM(z_rows.shape, F32),
            pltpu.VMEM((C, C), BF),
            pltpu.SemaphoreType.DMA((9,)),
        ],
    )(field, forward_y, z_rows, point_weight, inverse_y, forward_x, inverse_x, spread_hits)
    (base,) = call(point_kernel, [True] * 3, [cell_shape])(field, mixing, bias)
    block, field_modes = call(
        functools.partial(product_kernel, y_parts),
        [True] * (2 + y_parts),
        [mode_block, spectrum_shape],
        [rows_scratch, pltpu.VMEM((2 * KX * KZ, C * C), F32)],
    )(spectral_weight, spread, *forward(blocks, [], mode_block))
    *blocks, adjoint = call(
        functools.partial(middle_kernel, rows_x, rows_y, x_parts),
        [True] * (5 + x_parts),
        [cell_block] * x_parts + [((cells, depth), BF, True)],
        [pltpu.VMEM((cells, depth), F32)],
    )(
        base,
        cotangent.reshape(cells, depth),
        table,
        back,
        depth_table,
        *inverse(block, [], cell_block),
    )
    mixed_adjoint, sums = call(sums_kernel, [True] * 3, [cell_shape, sums_shape])(
        field, adjoint, mixing
    )
    block, adjoint_modes, sums = call(
        functools.partial(adjoint_kernel, y_parts),
        [True] * (2 + y_parts),
        [mode_block, spectrum_shape, sums_shape],
        [rows_scratch, pltpu.VMEM((2, 2 * KX * KZ, C * C), BF)],
    )(spectral_weight, spread, *forward(blocks, [sums], mode_sums))
    (grad_spectral,) = call(
        functools.partial(weight_kernel, scale),
        [True] * 2,
        [(wide, F32, False)],
        [pltpu.VMEM(wide, F32), pltpu.SemaphoreType.DMA((4,))],
    )(field_modes, adjoint_modes)
    grad_field, grad_point, grad_bias = call(
        functools.partial(last_kernel, rows_x, rows_y, x_parts, scale),
        [True] * (3 + x_parts),
        [((cells, depth), BF, False), ((C, C), F32, None), ((1, C), F32, None)],
        [pltpu.VMEM((cells, depth), BF), pltpu.SemaphoreType.DMA((rows_x,))],
    )(mixed_adjoint, back, depth_table, *inverse(block, [sums], cell_sums))
    return (
        grad_field.reshape(field_input.shape),
        grad_spectral,
        grad_point,
        grad_bias.reshape(C),
    )


def on_device(*arguments):
    rows_x, rows_y, _ = arguments[0].shape
    x_parts, y_parts = lax.axis_size("gx"), lax.axis_size("gy")
    whole_modes = arguments[2].shape[0] == KZ and y_parts == 4 and x_parts == 4
    if whole_modes and rows_x == 8 and rows_y == 64:
        return fast_device(*arguments)
    return general_device(*arguments)


def solution(mesh):
    return jax.shard_map(
        on_device,
        mesh=mesh,
        in_specs=(
            P(("groups", "gx"), "gy", None),
            P(("groups", "gx"), "gy", None),
            P(("gx", "gy"), None),
            P(),
            P(),
        ),
        out_specs=(
            P(("groups", "gx"), "gy", None),
            P(("groups", "gx", "gy"), None),
            P("groups", None),
            P("groups"),
        ),
        check_vma=False,
    )
```

```python
import functools
import math

import jax
import jax.numpy as jnp
import ml_dtypes
import numpy as np
from jax import lax
from jax.experimental import pallas as pl
from jax.experimental.pallas import tpu as pltpu
from jax.sharding import PartitionSpec as P

C = 32
KX = 16
KY = 16
KZ = 16
NZ = 32


def mode_values(mode_count, length):
    position = jnp.arange(mode_count, dtype=jnp.int32)
    return jnp.where(position < mode_count // 2, position, length - mode_count + position)


def phase_angles(positions, wavenumbers, length):
    steps = positions[:, None] * wavenumbers[None, :] % length
    return 2.0 * math.pi / length * steps.astype(jnp.float32)


def complex_table(positions, wavenumbers, length, factor):
    angles = phase_angles(positions, wavenumbers, length)
    cosine = jnp.cos(angles) * factor
    sine = jnp.sin(angles) * factor
    return jnp.stack(
        [jnp.stack([cosine, -sine], axis=-1), jnp.stack([sine, cosine], axis=-1)], axis=1
    )


def depth_table(depth_count, mode_count):
    angles = phase_angles(
        jnp.arange(depth_count, dtype=jnp.int32),
        jnp.arange(mode_count, dtype=jnp.int32),
        depth_count,
    )
    return jnp.stack([jnp.cos(angles), -jnp.sin(angles)], axis=1).astype(jnp.bfloat16)


def doubled(table):
    factor = jnp.where(jnp.arange(table.shape[2]) == 0, 1.0, 2.0).astype(jnp.float32)
    return table.astype(jnp.float32) * factor[None, None, :]


def spectral_product(spectrum, weights):
    shaped = spectrum.reshape(spectrum.shape[0], KX, 2, C)
    real_in, imag_in = (shaped[:, :, 0], shaped[:, :, 1])
    real_w, imag_w = (weights[:, :, 0], weights[:, :, 1])
    hp = lax.Precision.HIGHEST
    real_out = jnp.einsum("rmi,rmio->rmo", real_in, real_w, precision=hp) - jnp.einsum(
        "rmi,rmio->rmo", imag_in, imag_w, precision=hp
    )
    imag_out = jnp.einsum("rmi,rmio->rmo", real_in, imag_w, precision=hp) + jnp.einsum(
        "rmi,rmio->rmo", imag_in, real_w, precision=hp
    )
    return jnp.stack([real_out, imag_out], axis=2).reshape(spectrum.shape)


def adjoint_product(spectrum, weights):
    shaped = spectrum.reshape(spectrum.shape[0], KX, 2, C)
    real_in, imag_in = (shaped[:, :, 0], shaped[:, :, 1])
    real_w, imag_w = (weights[:, :, 0], weights[:, :, 1])
    hp = lax.Precision.HIGHEST
    real_out = jnp.einsum("rmo,rmio->rmi", real_in, real_w, precision=hp) + jnp.einsum(
        "rmo,rmio->rmi", imag_in, imag_w, precision=hp
    )
    imag_out = jnp.einsum("rmo,rmio->rmi", imag_in, real_w, precision=hp) - jnp.einsum(
        "rmo,rmio->rmi", real_in, imag_w, precision=hp
    )
    return jnp.stack([real_out, imag_out], axis=2).reshape(spectrum.shape)


def weight_gradient(field_spec, adjoint_spec):
    field_shaped = field_spec.reshape(field_spec.shape[0], KX, 2, C)
    adjoint_shaped = adjoint_spec.reshape(adjoint_spec.shape[0], KX, 2, C)
    real_v, imag_v = (field_shaped[:, :, 0], field_shaped[:, :, 1])
    real_h, imag_h = (adjoint_shaped[:, :, 0], adjoint_shaped[:, :, 1])
    real_g = (
        real_v[:, :, :, None] * real_h[:, :, None, :]
        + imag_v[:, :, :, None] * imag_h[:, :, None, :]
    )
    imag_g = (
        real_v[:, :, :, None] * imag_h[:, :, None, :]
        - imag_v[:, :, :, None] * real_h[:, :, None, :]
    )
    return jnp.stack([real_g, imag_g], axis=2).reshape(field_spec.shape[0], KX * 2 * C * C)


def channel_mix(values, weight):
    group_size = max(1, 128 // weight.shape[0])
    block = jnp.kron(jnp.eye(group_size, dtype=weight.dtype), weight)
    rows = values.reshape(-1, block.shape[0])
    return jnp.dot(rows, block, preferred_element_type=jnp.float32).reshape(values.shape)


def spectrum(values, z_table, y_table, x_local, x_whole):
    rows_x, rows_y, _ = values.shape
    hp = lax.Precision.HIGHEST
    shaped = values.reshape(rows_x, rows_y, NZ, C)
    zpart = jnp.einsum(
        "xyzc,zpk->xypkc", shaped, z_table, preferred_element_type=jnp.float32
    ).reshape(rows_x, rows_y, 2, KZ * C)
    ypart = jnp.einsum("xyqm,yqjp->xjpm", zpart, y_table, precision=hp)
    pencil = lax.all_to_all(ypart, "gx", split_axis=1, concat_axis=0, tiled=True)
    mode_rows = pencil.shape[1]
    pencil = pencil.reshape(pencil.shape[0], mode_rows, 2, KZ, C)
    partial_value = jnp.einsum("xjqkc,xqmp->jkmpc", pencil, x_whole, precision=hp).reshape(
        mode_rows * KZ, KX * 2 * C
    )
    return lax.psum_scatter(partial_value, "gy", scatter_dimension=0, tiled=True)


def synthesis(owned, z_float, y_table, x_whole, rows_x, rows_y):
    hp = lax.Precision.HIGHEST
    planes = lax.all_gather(owned, "gy", axis=0, tiled=True)
    mode_rows = planes.shape[0] // KZ
    shaped = planes.reshape(mode_rows, KZ, KX, 2, C)
    wide = jnp.einsum("jkmqc,xpmq->xjpkc", shaped, x_whole, precision=hp).reshape(
        x_whole.shape[0], mode_rows, 2, KZ * C
    )
    slab = lax.all_to_all(wide, "gx", split_axis=0, concat_axis=1, tiled=True)
    ypart = jnp.einsum("xjqm,ypjq->xypm", slab, y_table, precision=hp).reshape(
        rows_x, rows_y, 2, KZ, C
    )
    return jnp.einsum("xypkc,zpk->xyzc", ypart, z_float, precision=hp).reshape(
        rows_x, rows_y, NZ * C
    )


def general_device(field_input, cotangent, spectral_weight, point_weight, point_bias):
    rows_x, rows_y, _ = field_input.shape
    full_x = rows_x * lax.axis_size("gx")
    full_y = rows_y * lax.axis_size("gy")
    cell_scale = 1.0 / math.sqrt(full_x * full_y * NZ)
    x_start = lax.axis_index("gx") * rows_x
    y_start = lax.axis_index("gy") * rows_y
    y_table = complex_table(
        y_start + jnp.arange(rows_y, dtype=jnp.int32), mode_values(KY, full_y), full_y, 1.0
    )
    x_local = complex_table(
        x_start + jnp.arange(rows_x, dtype=jnp.int32), mode_values(KX, full_x), full_x, cell_scale
    )
    x_whole = complex_table(
        jnp.arange(full_x, dtype=jnp.int32), mode_values(KX, full_x), full_x, cell_scale
    )
    z_plain = depth_table(NZ, KZ)
    z_double_float = doubled(z_plain)
    z_double = z_double_float.astype(jnp.bfloat16)
    field_spec = spectrum(field_input, z_plain, y_table, x_local, x_whole)
    weights = spectral_weight.astype(jnp.float32).reshape(-1, KX, 2, C, C)
    mode_output = spectral_product(field_spec, weights)
    spectral_out = synthesis(mode_output, z_double_float, y_table, x_whole, rows_x, rows_y)
    bias_row = jnp.tile(point_bias, NZ)
    preact = spectral_out + channel_mix(field_input, point_weight) + bias_row
    _, pullback = jax.vjp(jax.nn.gelu, preact)
    adjoint = pullback(cotangent.astype(jnp.float32))[0].astype(jnp.bfloat16)
    adjoint_spec = spectrum(adjoint, z_double, y_table, x_local, x_whole)
    grad_spectral = weight_gradient(field_spec, adjoint_spec) * cell_scale
    mode_adjoint = adjoint_product(adjoint_spec, weights)
    flat_field = field_input.reshape(-1, C)
    flat_adjoint = adjoint.reshape(-1, C)
    point_term = (
        jnp.einsum("rc,rd->cd", flat_field, flat_adjoint, preferred_element_type=jnp.float32)
        * cell_scale
    )
    bias_term = jnp.sum(flat_adjoint.astype(jnp.float32), axis=0) * cell_scale
    grad_point, grad_bias = lax.psum((point_term, bias_term), ("gx", "gy"))
    back_field = synthesis(
        mode_adjoint, z_plain.astype(jnp.float32), y_table, x_whole, rows_x, rows_y
    )
    grad_field = (channel_mix(adjoint, point_weight.T) + back_field).astype(jnp.bfloat16)
    return (grad_field, grad_spectral, grad_point, grad_bias)


BF = jnp.bfloat16
F32 = jnp.float32
LANES = 128
CHUNKS = KZ * C // LANES
WIDE = KZ * C
SUM_ROWS = 16


def dot(left, right, dims=((1,), (0,))):
    return lax.dot_general(left, right, (dims, ((), ())), preferred_element_type=F32)


def halves(values):
    high = values.astype(BF)
    return high, (values - high.astype(F32)).astype(BF)


def halved(values, table, dims):
    high, low = halves(values)
    both = dot(jnp.concatenate([high, low], axis=0), table, ((dims[0],), (dims[1],)))
    return both[: values.shape[0]] + both[values.shape[0] :]


def iota(shape, axis):
    return lax.broadcasted_iota(jnp.int32, shape, axis)


def lane_take(values, index):
    return jnp.take_along_axis(values, index, axis=1, mode="promise_in_bounds")


def np_halves(table):
    high = table.astype(ml_dtypes.bfloat16).astype(np.float64)
    low = (table - high).astype(ml_dtypes.bfloat16).astype(np.float64)
    return high, low


def np_modes(count, length):
    position = np.arange(count)
    return np.where(position < count // 2, position, length - count + position)


def np_angles(positions, modes, length):
    return 2.0 * np.pi * ((positions[:, None] * modes[None, :]) % length) / length


def depth_rows():
    angles = np_angles(np.arange(NZ), np.arange(KZ), NZ)
    table = np.stack([np.cos(angles), -np.sin(angles)], axis=1).astype(ml_dtypes.bfloat16)
    return np.repeat(table.astype(np.float32).reshape(NZ, 2 * KZ), C, axis=1)


def spread_table():
    hit = np.repeat(np.eye(C, dtype=np.float32), C, axis=1)
    return np.tile(hit, (LANES // C, 1)).astype(ml_dtypes.bfloat16)


def y_tables(full_y, rows_y, x_parts, y_parts):
    angles = np_angles(np.arange(full_y), np_modes(KY, full_y), full_y)
    table = np.stack([np.cos(angles), -np.sin(angles)], axis=-1)
    high, low = np_halves(table)
    forward, inverse = [], []
    for device in range(x_parts * y_parts):
        own_x, own_y = device // y_parts, device % y_parts
        order = [
            (own_x ^ turn) * y_parts + (own_y ^ step)
            for turn in range(x_parts)
            for step in range(y_parts)
        ]
        rows = slice(own_y * rows_y, (own_y + 1) * rows_y)

        def picked(values):
            block = values[rows][:, order].reshape(rows_y, x_parts, y_parts, 2)
            return block.transpose(0, 1, 3, 2).reshape(rows_y, 2 * KY)

        forward.append(np.concatenate([picked(high), picked(low)], axis=1).T)
        inverse.append(np.concatenate([picked(high), picked(low), picked(high)], axis=1))
    return tuple(np.stack(part).astype(ml_dtypes.bfloat16) for part in (forward, inverse))


def x_tables(full_x, rows_x, factor, y_parts):
    angles = np_angles(np.arange(full_x), np_modes(KX, full_x), full_x)
    cosine, sine = np.cos(angles) * factor, np.sin(angles) * factor
    table = np.stack([np.stack([cosine, -sine], -1), np.stack([sine, cosine], -1)], axis=1)
    blocked = table.reshape(full_x // rows_x, rows_x * 2, KX * 2)
    same = np.eye(y_parts)

    def packed(spread):
        high, low = np_halves(spread)
        return np.concatenate([high, low, high], axis=2).astype(ml_dtypes.bfloat16)

    forward = np.einsum("grm,de->gdmre", blocked, same)
    inverse = np.einsum("grm,de->grdem", blocked, same)
    parts, rows, modes = blocked.shape
    return (
        packed(forward.reshape(parts, y_parts * modes, rows * y_parts)),
        packed(inverse.reshape(parts, rows * y_parts, y_parts * modes)),
    )


def tripled(values):
    high, low = halves(values)
    return jnp.concatenate([high, high, low], axis=0)


def lanes_of(values, step):
    return values[:, step * LANES : (step + 1) * LANES]


def read_lanes(ref, rows):
    pieces = [ref[i * rows : (i + 1) * rows, :] for i in range(CHUNKS)]
    return jnp.concatenate(pieces, axis=1)


def write_lanes(ref, values, rows, start=0):
    for chunk in range(CHUNKS):
        first = chunk * rows + start
        ref[first : first + values.shape[0], :] = lanes_of(values, chunk)


def turned(values):
    tiles = values.reshape(values.shape[0] // 8, 8, values.shape[1])
    return pltpu.roll(tiles, 4, 1).reshape(values.shape)


def part_sign(rows):
    return jnp.where(iota((rows, 1), 0) % 8 < 4, -1.0, 1.0).astype(F32)


def y_spectrum(values, table, rows_x, rows_y):
    planes = []
    half = table.shape[0] // 2
    for x in range(rows_x):
        both = dot(table, values[x * rows_y : (x + 1) * rows_y])
        planes.append(both[:half] + both[half:])
    return jnp.concatenate(planes, axis=0)


def z_spectrum(both, out_refs, rows_x):
    whole = both[:, :WIDE] + part_sign(both.shape[0]) * turned(both[:, WIDE:])
    turns = len(out_refs)
    for x in range(rows_x):
        for turn in range(turns):
            block = whole[(x * turns + turn) * 8 : (x * turns + turn + 1) * 8]
            write_lanes(out_refs[turn], block, rows_x * 8, x * 8)


def z_synthesis(in_refs, depth_ref, rows_x, exact=True):
    blocks = [read_lanes(ref, rows_x * 8) for ref in in_refs]
    modes = jnp.concatenate(blocks, axis=0)
    other = -part_sign(modes.shape[0]) * turned(modes)
    stacked = jnp.concatenate([modes, other], axis=1)
    if exact:
        return halved(stacked, depth_ref[...], (1, 1))
    return dot(stacked.astype(BF), depth_ref[...], ((1,), (1,)))


def y_synthesis(planes, table, x, rows_x):
    turns = planes.shape[0] // (8 * rows_x)
    rows = [(turn * rows_x + x) * 8 for turn in range(turns)]
    return dot(table, tripled(jnp.concatenate([planes[r : r + 8] for r in rows], axis=0)))


def mixing_matrix(weight_ref):
    wide = 8 * C
    pick = (iota((wide, C), 0) % C == iota((wide, C), 1)).astype(F32).astype(BF)
    tall = dot(pick, weight_ref[...]).astype(BF)
    tiled = dot(tall, pick, ((1,), (1,)))
    shape = (wide, wide)
    return jnp.where(iota(shape, 0) // C == iota(shape, 1) // C, tiled, 0.0).astype(BF)


def mixed(values, matrix, dims):
    wide = matrix.shape[0]
    pieces = []
    for start in range(0, values.shape[1], wide):
        pieces.append(dot(values[:, start : start + wide], matrix, dims))
    return jnp.concatenate(pieces, axis=1)


def folded(row):
    total = row[:, :LANES]
    for start in range(LANES, row.shape[1], LANES):
        total = total + row[:, start : start + LANES]
    total = total + pltpu.roll(total, 64, 1)
    return total + pltpu.roll(total, 32, 1)


def depth_factor():
    return jnp.where(iota((1, WIDE), 1) < C, 1.0, 2.0).astype(F32)


def mode_row(ref, row):
    wide = jnp.broadcast_to(ref[pl.ds(row, 1), :], (KZ, WIDE))
    group = iota((KZ, LANES), 0) // 4
    chosen = wide[:, :LANES]
    for chunk in range(1, CHUNKS):
        chosen = jnp.where(group == chunk, wide[:, chunk * LANES : (chunk + 1) * LANES], chosen)
    return chosen


def in_index(step):
    return iota((KZ, LANES), 0) % 4 * C + step * 4 + iota((KZ, LANES), 1) // C


def out_index():
    return iota((KZ, LANES), 0) % 4 * C + iota((KZ, LANES), 1) % C


def own_group():
    return iota((KZ, LANES), 0) % 4 == iota((KZ, LANES), 1) // C


def gathered_rows(scratch):
    pieces = []
    for chunk in range(CHUNKS):
        terms = [scratch[pl.ds(chunk * 4 + a, 2 * KX, stride=KZ), :] for a in range(4)]
        pieces.append((terms[0] + terms[1]) + (terms[2] + terms[3]))
    return jnp.concatenate(pieces, axis=1)


def weight_parts(weight_ref, mode):
    start = pl.multiple_of(mode * 2 * C * C, LANES)
    both = weight_ref[:, pl.ds(start, 2 * C * C)].astype(F32)
    return both[:, : C * C], both[:, C * C :]


def device_index():
    return lax.axis_index("gx") * lax.axis_size("gy") + lax.axis_index("gy")


def fill_depth(rows_ref, depth_ref):
    count, wide = rows_ref.shape
    same = iota((C, wide), 0) == iota((C, wide), 1) % C
    for z in range(count):
        row = jnp.broadcast_to(rows_ref[z : z + 1, :], (C, wide))
        depth_ref[z * C : (z + 1) * C, :] = jnp.where(same, row, 0.0).astype(BF)


def first_kernel(
    rows_x,
    rows_y,
    field_ref,
    table_ref,
    rows_ref,
    point_ref,
    back_ref,
    modes_ref,
    cells_ref,
    spread_ref,
    *refs,
):
    out_refs, refs = refs[:-11], refs[-11:]
    depth, mixing_ref, table, back, to_modes, to_cells, spread, field, rows, point, gates = refs
    device = device_index()
    half = field.shape[0] // 2
    pairs = [(rows_ref, rows), (point_ref, point), (table_ref.at[device], table)]
    for part in range(2):
        block = pl.ds(part * half, half)
        pairs.append((field_ref.at[block], field.at[block]))
    pairs += [(back_ref.at[device], back), (modes_ref, to_modes), (cells_ref, to_cells)]
    pairs += [(spread_ref, spread)]
    copies = [
        pltpu.make_async_copy(source, target, gates.at[turn])
        for turn, (source, target) in enumerate(pairs)
    ]
    for copy in copies:
        copy.start()
    copies[0].wait()
    fill_depth(rows, depth)
    copies[1].wait()
    mixing_ref[...] = mixing_matrix(point)
    for copy in copies[2:5]:
        copy.wait()
    planes = y_spectrum(field[...], table[...], rows_x, rows_y)
    z_spectrum(halved(planes, depth[...], (1, 0)), out_refs, rows_x)
    for copy in copies[5:]:
        copy.wait()


def x_forward_kernel(turns, table_ref, *refs):
    in_refs, refs = unqueued(refs[:turns], FORWARD_X), refs[turns:]
    rows = table_ref.shape[2] // 3
    own = lax.axis_index("gx")
    total = None
    for turn in range(turns):
        term = dot(table_ref[own ^ turn], tripled(read_lanes(in_refs[turn], rows)))
        total = term if total is None else total + term
    modes = 2 * KX
    steps = total.shape[0] // modes
    for step, ref in enumerate(refs[-steps:]):
        write_lanes(ref, total[step * modes : (step + 1) * modes], modes)
        if len(refs) > steps:
            ref[CHUNKS * modes :, :] = refs[0][...]


def x_inverse_kernel(steps, turns, table_ref, *refs):
    in_refs, refs = unqueued(refs[:steps], INVERSE_Y), refs[steps:]
    values = tripled(jnp.concatenate([read_lanes(ref, 2 * KX) for ref in in_refs], axis=0))
    own = lax.axis_index("gx")
    rows = table_ref.shape[1]
    for turn, ref in enumerate(refs[-turns:]):
        write_lanes(ref, dot(table_ref[own ^ turn], values), rows)
        if len(refs) > turns:
            ref[CHUNKS * rows :, :] = refs[0][...]


FORWARD_X, FORWARD_Y, INVERSE_Y, INVERSE_X = ((2, 1, 3), (1, 2, 3), (1, 2, 3), (2, 3, 1))


def queued(blocks, order):
    return [blocks[0]] + [blocks[turn] for turn in order]


def unqueued(refs, order):
    return [refs[0]] + [refs[1 + order.index(turn)] for turn in range(1, len(refs))]


def summed_modes(in_refs):
    return functools.reduce(jnp.add, [read_lanes(ref, 2 * KX) for ref in in_refs])


def stacked_modes(ref):
    keep = own_group()
    rows = [jnp.where(keep, mode_row(ref, row), 0.0) for row in range(2 * KX)]
    return jnp.concatenate(rows, axis=0)


def product_kernel(steps, weight_ref, spread_ref, *refs):
    in_refs, (out_ref, spec_ref, scratch, wide) = refs[:steps], refs[steps:]
    spec_ref[...] = summed_modes(in_refs)
    high, low = halves(stacked_modes(spec_ref))
    spread = spread_ref[...]
    wide[...] = dot(
        jnp.concatenate([high, low], axis=1), jnp.concatenate([spread, spread], axis=0)
    )

    def step(mode, carry):
        real_w, imag_w = weight_parts(weight_ref, mode)
        start = pl.multiple_of(2 * mode * KZ, 2 * KZ)
        both = wide[pl.ds(start, 2 * KZ), :]
        real_sum = jnp.zeros((KZ, LANES), F32)
        imag_sum = jnp.zeros((KZ, LANES), F32)
        for part in range(C // 4):
            real_v, imag_v = lanes_of(both[:KZ], part), lanes_of(both[KZ:], part)
            real_p, imag_p = lanes_of(real_w, part), lanes_of(imag_w, part)
            real_sum = real_sum + (real_v * real_p - imag_v * imag_p)
            imag_sum = imag_sum + (real_v * imag_p + imag_v * real_p)
        scratch[pl.ds(start, 2 * KZ), :] = jnp.concatenate([real_sum, imag_sum], axis=0)
        return carry

    lax.fori_loop(0, KX, step, 0, unroll=4)
    shape = (LANES, LANES)
    same = (iota(shape, 0) % C == iota(shape, 1) % C).astype(F32).astype(BF)
    high, low = halves(scratch[...])
    total = dot(jnp.concatenate([high, low], axis=1), jnp.concatenate([same, same], axis=0))
    scratch[...] = own_rows(total)
    write_lanes(out_ref, gathered_rows(scratch) * depth_factor(), 2 * KX)


def own_rows(values):
    keep = iota(values.shape, 0) % 4 == iota(values.shape, 1) // C
    return jnp.where(keep, values, 0.0)


def point_kernel(field_ref, mixing_ref, bias_ref, out_ref):
    bias = jnp.concatenate([bias_ref[...]] * NZ, axis=1)
    out_ref[...] = mixed(field_ref[...], mixing_ref[...], ((1,), (0,))) + bias


def middle_kernel(
    rows_x,
    rows_y,
    turns,
    base_ref,
    cotangent_ref,
    table_ref,
    back_ref,
    depth_ref,
    *refs,
):
    in_refs = unqueued(refs[:turns], INVERSE_X)
    out_refs, (adjoint_ref, value_ref) = refs[turns:-2], refs[-2:]
    planes = z_synthesis(in_refs, depth_ref, rows_x)
    for x in range(rows_x):
        block = slice(x * rows_y, (x + 1) * rows_y)
        spectral = y_synthesis(planes, back_ref[...], x, rows_x)
        value_ref[block, :] = spectral + base_ref[block, :]
    value = value_ref[...]
    root = math.sqrt(2.0 / math.pi)
    square = value * value
    bent = jnp.tanh(value * (root + (root * 0.044715) * square))
    tail = value * (root + (3.0 * root * 0.044715) * square)
    slope = (0.5 + 0.5 * bent) * (1.0 + (1.0 - bent) * tail)
    adjoint = (cotangent_ref[...].astype(F32) * slope).astype(BF)
    adjoint_ref[...] = adjoint
    modes = y_spectrum(adjoint, table_ref[...], rows_x, rows_y).astype(BF)
    z_spectrum(dot(modes, depth_ref[...]), out_refs, rows_x)


def sums_kernel(field_ref, adjoint_ref, mixing_ref, out_ref, sums_ref):
    field, adjoint, mixing = field_ref[...], adjoint_ref[...], mixing_ref[...]
    out_ref[...] = mixed(adjoint, mixing, ((1,), (1,)))
    wide = mixing.shape[0]
    total = jnp.zeros((wide, wide), F32)
    for start in range(0, NZ * C, wide):
        total = total + dot(
            field[:, start : start + wide], adjoint[:, start : start + wide], ((0,), (0,))
        )
    total = jnp.where(iota((wide, wide), 0) // C == iota((wide, wide), 1) // C, total, 0.0)
    point = total[:C]
    for start in range(C, wide, C):
        point = point + total[start : start + C]
    point = folded(point)
    group = iota((8, LANES), 1) // C
    packed = point[:8]
    for part in range(1, 4):
        packed = jnp.where(group == part, point[part * 8 : (part + 1) * 8], packed)
    sums_ref[:8, :] = packed
    sums_ref[8:, :] = folded(dot(jnp.ones((8, adjoint.shape[0]), BF), adjoint))


def adjoint_kernel(steps, weight_ref, spread_ref, *refs):
    in_refs, (out_ref, spec_ref, sums_ref, scratch, wide) = refs[:steps], refs[steps:]
    spec_ref[...] = summed_modes(in_refs) * depth_factor()
    sums_ref[...] = functools.reduce(jnp.add, [ref[CHUNKS * 2 * KX :, :] for ref in in_refs])
    index = out_index()

    def step(mode, carry):
        real = lane_take(mode_row(spec_ref, 2 * mode), index)
        imag = lane_take(mode_row(spec_ref, 2 * mode + 1), index)
        real_w, imag_w = weight_parts(weight_ref, mode)
        real_parts, imag_parts = [], []
        for part in range(C // 4):
            real_p, imag_p = lanes_of(real_w, part), lanes_of(imag_w, part)
            real_parts.append(real * real_p + imag * imag_p)
            imag_parts.append(imag * real_p - real * imag_p)
        both = jnp.concatenate(
            [jnp.concatenate(real_parts, axis=1), jnp.concatenate(imag_parts, axis=1)], axis=0
        )
        high, low = halves(both)
        start = pl.multiple_of(2 * mode * KZ, 2 * KZ)
        wide[0, pl.ds(start, 2 * KZ), :] = high
        wide[1, pl.ds(start, 2 * KZ), :] = low
        return carry

    lax.fori_loop(0, KX, step, 0, unroll=4)
    total = dot(wide[0], spread_ref[...], ((1,), (1,)))
    total = total + dot(wide[1], spread_ref[...], ((1,), (1,)))
    scratch[...] = own_rows(total)
    write_lanes(out_ref, gathered_rows(scratch), 2 * KX)


def weight_kernel(scale, field_ref, adjoint_ref, out_ref, staged, gates):
    index = out_index()
    stores = []
    turns = gates.shape[0]
    modes = KX // turns

    def step(mode, carry):
        row = 2 * mode
        real_v, imag_v = mode_row(field_ref, row), mode_row(field_ref, row + 1)
        real_h = lane_take(mode_row(adjoint_ref, row), index) * scale
        imag_h = lane_take(mode_row(adjoint_ref, row + 1), index) * scale
        real_g, imag_g = [], []
        for part in range(C // 4):
            take = in_index(part)
            real, imag = lane_take(real_v, take), lane_take(imag_v, take)
            real_g.append(real * real_h + imag * imag_h)
            imag_g.append(real * imag_h - imag * real_h)
        start = pl.multiple_of(mode * 2 * C * C, LANES)
        staged[:, pl.ds(start, 2 * C * C)] = jnp.concatenate(real_g + imag_g, axis=1)
        return carry

    for turn in range(turns):
        lax.fori_loop(turn * modes, (turn + 1) * modes, step, 0, unroll=2)
        block = pl.ds(turn * modes * 2 * C * C, modes * 2 * C * C)
        stores.append(
            pltpu.make_async_copy(staged.at[:, block], out_ref.at[:, block], gates.at[turn])
        )
        stores[-1].start()
    for store in stores:
        store.wait()


def last_kernel(rows_x, rows_y, turns, scale, mixed_ref, back_ref, depth_ref, *refs):
    in_refs = unqueued(refs[:turns], INVERSE_X)
    out_ref, point_ref, bias_ref, result, gates = refs[turns:]
    total = functools.reduce(jnp.add, [ref[ref.shape[0] - SUM_ROWS :, :] for ref in in_refs])
    total = total * scale
    packed = total[:8]
    for part in range(4):
        piece = packed if part == 0 else pltpu.roll(packed, LANES - part * C, 1)
        point_ref[part * 8 : (part + 1) * 8, :] = piece[:, :C]
    bias_ref[...] = total[8:9, :C]
    planes = z_synthesis(in_refs, depth_ref, rows_x, exact=False)
    stores = []
    for x in range(rows_x):
        block = slice(x * rows_y, (x + 1) * rows_y)
        spectral = y_synthesis(planes, back_ref[...], x, rows_x)
        result[block, :] = (mixed_ref[block, :] + spectral).astype(BF)
        span = pl.ds(x * rows_y, rows_y)
        stores.append(pltpu.make_async_copy(result.at[span], out_ref.at[span], gates.at[x]))
        stores[-1].start()
    for store in stores:
        store.wait()


NEAR = pl.BlockSpec(memory_space=pltpu.VMEM)
FAR = pl.BlockSpec(memory_space=pltpu.HBM)


def call(kernel, ins, outs, scratch=()):
    shapes = []
    for shape, kind, inner in outs:
        if inner is None:
            shapes.append(jax.ShapeDtypeStruct(shape, kind))
        else:
            shapes.append((pltpu.VMEM if inner else pltpu.HBM)(shape, kind))
    function = pl.pallas_call(
        kernel,
        out_shape=shapes,
        in_specs=[NEAR if inner else FAR for inner in ins],
        out_specs=[FAR if inner is False else NEAR for _, _, inner in outs],
        scratch_shapes=list(scratch),
        compiler_params=pltpu.CompilerParams(vmem_limit_bytes=40 * 1024 * 1024),
    )

    def run(*arguments):
        spaces = [pltpu.VMEM if inner else pltpu.HBM for inner in ins]
        return function(*map(pltpu.with_memory_space_constraint, arguments, spaces))

    return run


def exchange(blocks, axis):
    count = lax.axis_size(axis)
    order = [2, 3, 1] if count == 4 else list(range(1, count))
    received = list(blocks)
    for turn in order:
        pairs = [(device, device ^ turn) for device in range(count)]
        received[turn] = lax.ppermute(blocks[turn], axis, pairs)
    return received


def fast_device(field_input, cotangent, spectral_weight, point_weight, point_bias):
    rows_x, rows_y, depth = field_input.shape
    x_parts, y_parts = lax.axis_size("gx"), lax.axis_size("gy")
    full_x, full_y = rows_x * x_parts, rows_y * y_parts
    scale = 1.0 / math.sqrt(full_x * full_y * NZ)
    cells = rows_x * rows_y
    z_rows = jnp.asarray(depth_rows())
    spread_hits = jnp.asarray(spread_table())
    forward_y, inverse_y = map(jnp.asarray, y_tables(full_y, rows_y, x_parts, y_parts))
    forward_x, inverse_x = map(jnp.asarray, x_tables(full_x, rows_x, scale, y_parts))
    field = field_input.reshape(cells, depth)
    bias = point_bias.reshape(1, C)
    cell_rows, mode_rows = CHUNKS * rows_x * 8, CHUNKS * 2 * KX
    cell_block, mode_block = ((cell_rows, LANES), F32, True), ((mode_rows, LANES), F32, True)
    cell_sums = ((cell_rows + SUM_ROWS, LANES), F32, True)
    mode_sums = ((mode_rows + SUM_ROWS, LANES), F32, True)
    spectrum_shape = ((2 * KX, WIDE), F32, True)
    rows_scratch = pltpu.VMEM((2 * KX * KZ, LANES), F32)
    sums_shape = ((SUM_ROWS, LANES), F32, True)
    cell_shape = ((cells, depth), F32, True)
    wide = (KZ, KX * 2 * C * C)

    def forward(blocks, extra, mode_shape):
        received = exchange(blocks, "gx")
        sent = call(
            functools.partial(x_forward_kernel, x_parts),
            [True] * (1 + x_parts + len(extra)),
            [mode_shape] * y_parts,
        )(to_modes, *queued(received, FORWARD_X), *extra)
        return queued(exchange(sent, "gy"), FORWARD_Y)

    def inverse(block, extra, cell_shape):
        received = exchange([block] * y_parts, "gy")
        sent = call(
            functools.partial(x_inverse_kernel, y_parts, x_parts),
            [True] * (1 + y_parts + len(extra)),
            [cell_shape] * x_parts,
        )(to_cells, *queued(received, INVERSE_Y), *extra)
        return queued(exchange(sent, "gx"), INVERSE_X)

    *blocks, depth_table, mixing, table, back, to_modes, to_cells, spread = call(
        functools.partial(first_kernel, rows_x, rows_y),
        [False] * 8,
        [cell_block] * x_parts
        + [((depth, 2 * WIDE), BF, True), ((8 * C, 8 * C), BF, True)]
        + [(part.shape[1:], BF, True) for part in (forward_y, inverse_y)]
        + [(part.shape, BF, True) for part in (forward_x, inverse_x, spread_hits)],
        [
            pltpu.VMEM((cells, depth), BF),
            pltpu.VMEM(z_rows.shape, F32),
            pltpu.VMEM((C, C), BF),
            pltpu.SemaphoreType.DMA((9,)),
        ],
    )(field, forward_y, z_rows, point_weight, inverse_y, forward_x, inverse_x, spread_hits)
    (base,) = call(point_kernel, [True] * 3, [cell_shape])(field, mixing, bias)
    block, field_modes = call(
        functools.partial(product_kernel, y_parts),
        [True] * (2 + y_parts),
        [mode_block, spectrum_shape],
        [rows_scratch, pltpu.VMEM((2 * KX * KZ, C * C), F32)],
    )(spectral_weight, spread, *forward(blocks, [], mode_block))
    *blocks, adjoint = call(
        functools.partial(middle_kernel, rows_x, rows_y, x_parts),
        [True] * (5 + x_parts),
        [cell_block] * x_parts + [((cells, depth), BF, True)],
        [pltpu.VMEM((cells, depth), F32)],
    )(
        base,
        cotangent.reshape(cells, depth),
        table,
        back,
        depth_table,
        *inverse(block, [], cell_block),
    )
    mixed_adjoint, sums = call(sums_kernel, [True] * 3, [cell_shape, sums_shape])(
        field, adjoint, mixing
    )
    block, adjoint_modes, sums = call(
        functools.partial(adjoint_kernel, y_parts),
        [True] * (2 + y_parts),
        [mode_block, spectrum_shape, sums_shape],
        [rows_scratch, pltpu.VMEM((2, 2 * KX * KZ, C * C), BF)],
    )(spectral_weight, spread, *forward(blocks, [sums], mode_sums))
    (grad_spectral,) = call(
        functools.partial(weight_kernel, scale),
        [True] * 2,
        [(wide, F32, False)],
        [pltpu.VMEM(wide, F32), pltpu.SemaphoreType.DMA((4,))],
    )(field_modes, adjoint_modes)
    grad_field, grad_point, grad_bias = call(
        functools.partial(last_kernel, rows_x, rows_y, x_parts, scale),
        [True] * (3 + x_parts),
        [((cells, depth), BF, False), ((C, C), F32, None), ((1, C), F32, None)],
        [pltpu.VMEM((cells, depth), BF), pltpu.SemaphoreType.DMA((rows_x,))],
    )(mixed_adjoint, back, depth_table, *inverse(block, [sums], cell_sums))
    return (
        grad_field.reshape(field_input.shape),
        grad_spectral,
        grad_point,
        grad_bias.reshape(C),
    )


def on_device(*arguments):
    rows_x, rows_y, _ = arguments[0].shape
    x_parts, y_parts = lax.axis_size("gx"), lax.axis_size("gy")
    whole_modes = arguments[2].shape[0] == KZ and y_parts == 4 and x_parts == 4
    if whole_modes and rows_x == 8 and rows_y == 64:
        return fast_device(*arguments)
    return general_device(*arguments)


def solution(mesh):
    return jax.shard_map(
        on_device,
        mesh=mesh,
        in_specs=(
            P(("groups", "gx"), "gy", None),
            P(("groups", "gx"), "gy", None),
            P(("gx", "gy"), None),
            P(),
            P(),
        ),
        out_specs=(
            P(("groups", "gx"), "gy", None),
            P(("groups", "gx", "gy"), None),
            P("groups", None),
            P("groups"),
        ),
        check_vma=False,
    )
```

```python
import functools
import math

import jax
import jax.numpy as jnp
import ml_dtypes
import numpy as np
from jax import lax
from jax.experimental import pallas as pl
from jax.experimental.pallas import tpu as pltpu
from jax.sharding import PartitionSpec as P

C = 32
KX = 16
KY = 16
KZ = 16
NZ = 32


def mode_values(mode_count, length):
    position = jnp.arange(mode_count, dtype=jnp.int32)
    return jnp.where(position < mode_count // 2, position, length - mode_count + position)


def phase_angles(positions, wavenumbers, length):
    steps = positions[:, None] * wavenumbers[None, :] % length
    return 2.0 * math.pi / length * steps.astype(jnp.float32)


def complex_table(positions, wavenumbers, length, factor):
    angles = phase_angles(positions, wavenumbers, length)
    cosine = jnp.cos(angles) * factor
    sine = jnp.sin(angles) * factor
    return jnp.stack(
        [jnp.stack([cosine, -sine], axis=-1), jnp.stack([sine, cosine], axis=-1)], axis=1
    )


def depth_table(depth_count, mode_count):
    angles = phase_angles(
        jnp.arange(depth_count, dtype=jnp.int32),
        jnp.arange(mode_count, dtype=jnp.int32),
        depth_count,
    )
    return jnp.stack([jnp.cos(angles), -jnp.sin(angles)], axis=1).astype(jnp.bfloat16)


def doubled(table):
    factor = jnp.where(jnp.arange(table.shape[2]) == 0, 1.0, 2.0).astype(jnp.float32)
    return table.astype(jnp.float32) * factor[None, None, :]


def spectral_product(spectrum, weights):
    shaped = spectrum.reshape(spectrum.shape[0], KX, 2, C)
    real_in, imag_in = (shaped[:, :, 0], shaped[:, :, 1])
    real_w, imag_w = (weights[:, :, 0], weights[:, :, 1])
    hp = lax.Precision.HIGHEST
    real_out = jnp.einsum("rmi,rmio->rmo", real_in, real_w, precision=hp) - jnp.einsum(
        "rmi,rmio->rmo", imag_in, imag_w, precision=hp
    )
    imag_out = jnp.einsum("rmi,rmio->rmo", real_in, imag_w, precision=hp) + jnp.einsum(
        "rmi,rmio->rmo", imag_in, real_w, precision=hp
    )
    return jnp.stack([real_out, imag_out], axis=2).reshape(spectrum.shape)


def adjoint_product(spectrum, weights):
    shaped = spectrum.reshape(spectrum.shape[0], KX, 2, C)
    real_in, imag_in = (shaped[:, :, 0], shaped[:, :, 1])
    real_w, imag_w = (weights[:, :, 0], weights[:, :, 1])
    hp = lax.Precision.HIGHEST
    real_out = jnp.einsum("rmo,rmio->rmi", real_in, real_w, precision=hp) + jnp.einsum(
        "rmo,rmio->rmi", imag_in, imag_w, precision=hp
    )
    imag_out = jnp.einsum("rmo,rmio->rmi", imag_in, real_w, precision=hp) - jnp.einsum(
        "rmo,rmio->rmi", real_in, imag_w, precision=hp
    )
    return jnp.stack([real_out, imag_out], axis=2).reshape(spectrum.shape)


def weight_gradient(field_spec, adjoint_spec):
    field_shaped = field_spec.reshape(field_spec.shape[0], KX, 2, C)
    adjoint_shaped = adjoint_spec.reshape(adjoint_spec.shape[0], KX, 2, C)
    real_v, imag_v = (field_shaped[:, :, 0], field_shaped[:, :, 1])
    real_h, imag_h = (adjoint_shaped[:, :, 0], adjoint_shaped[:, :, 1])
    real_g = (
        real_v[:, :, :, None] * real_h[:, :, None, :]
        + imag_v[:, :, :, None] * imag_h[:, :, None, :]
    )
    imag_g = (
        real_v[:, :, :, None] * imag_h[:, :, None, :]
        - imag_v[:, :, :, None] * real_h[:, :, None, :]
    )
    return jnp.stack([real_g, imag_g], axis=2).reshape(field_spec.shape[0], KX * 2 * C * C)


def channel_mix(values, weight):
    group_size = max(1, 128 // weight.shape[0])
    block = jnp.kron(jnp.eye(group_size, dtype=weight.dtype), weight)
    rows = values.reshape(-1, block.shape[0])
    return jnp.dot(rows, block, preferred_element_type=jnp.float32).reshape(values.shape)


def spectrum(values, z_table, y_table, x_local, x_whole):
    rows_x, rows_y, _ = values.shape
    hp = lax.Precision.HIGHEST
    shaped = values.reshape(rows_x, rows_y, NZ, C)
    zpart = jnp.einsum(
        "xyzc,zpk->xypkc", shaped, z_table, preferred_element_type=jnp.float32
    ).reshape(rows_x, rows_y, 2, KZ * C)
    ypart = jnp.einsum("xyqm,yqjp->xjpm", zpart, y_table, precision=hp)
    pencil = lax.all_to_all(ypart, "gx", split_axis=1, concat_axis=0, tiled=True)
    mode_rows = pencil.shape[1]
    pencil = pencil.reshape(pencil.shape[0], mode_rows, 2, KZ, C)
    partial_value = jnp.einsum("xjqkc,xqmp->jkmpc", pencil, x_whole, precision=hp).reshape(
        mode_rows * KZ, KX * 2 * C
    )
    return lax.psum_scatter(partial_value, "gy", scatter_dimension=0, tiled=True)


def synthesis(owned, z_float, y_table, x_whole, rows_x, rows_y):
    hp = lax.Precision.HIGHEST
    planes = lax.all_gather(owned, "gy", axis=0, tiled=True)
    mode_rows = planes.shape[0] // KZ
    shaped = planes.reshape(mode_rows, KZ, KX, 2, C)
    wide = jnp.einsum("jkmqc,xpmq->xjpkc", shaped, x_whole, precision=hp).reshape(
        x_whole.shape[0], mode_rows, 2, KZ * C
    )
    slab = lax.all_to_all(wide, "gx", split_axis=0, concat_axis=1, tiled=True)
    ypart = jnp.einsum("xjqm,ypjq->xypm", slab, y_table, precision=hp).reshape(
        rows_x, rows_y, 2, KZ, C
    )
    return jnp.einsum("xypkc,zpk->xyzc", ypart, z_float, precision=hp).reshape(
        rows_x, rows_y, NZ * C
    )


def general_device(field_input, cotangent, spectral_weight, point_weight, point_bias):
    rows_x, rows_y, _ = field_input.shape
    full_x = rows_x * lax.axis_size("gx")
    full_y = rows_y * lax.axis_size("gy")
    cell_scale = 1.0 / math.sqrt(full_x * full_y * NZ)
    x_start = lax.axis_index("gx") * rows_x
    y_start = lax.axis_index("gy") * rows_y
    y_table = complex_table(
        y_start + jnp.arange(rows_y, dtype=jnp.int32), mode_values(KY, full_y), full_y, 1.0
    )
    x_local = complex_table(
        x_start + jnp.arange(rows_x, dtype=jnp.int32), mode_values(KX, full_x), full_x, cell_scale
    )
    x_whole = complex_table(
        jnp.arange(full_x, dtype=jnp.int32), mode_values(KX, full_x), full_x, cell_scale
    )
    z_plain = depth_table(NZ, KZ)
    z_double_float = doubled(z_plain)
    z_double = z_double_float.astype(jnp.bfloat16)
    field_spec = spectrum(field_input, z_plain, y_table, x_local, x_whole)
    weights = spectral_weight.astype(jnp.float32).reshape(-1, KX, 2, C, C)
    mode_output = spectral_product(field_spec, weights)
    spectral_out = synthesis(mode_output, z_double_float, y_table, x_whole, rows_x, rows_y)
    bias_row = jnp.tile(point_bias, NZ)
    preact = spectral_out + channel_mix(field_input, point_weight) + bias_row
    _, pullback = jax.vjp(jax.nn.gelu, preact)
    adjoint = pullback(cotangent.astype(jnp.float32))[0].astype(jnp.bfloat16)
    adjoint_spec = spectrum(adjoint, z_double, y_table, x_local, x_whole)
    grad_spectral = weight_gradient(field_spec, adjoint_spec) * cell_scale
    mode_adjoint = adjoint_product(adjoint_spec, weights)
    flat_field = field_input.reshape(-1, C)
    flat_adjoint = adjoint.reshape(-1, C)
    point_term = (
        jnp.einsum("rc,rd->cd", flat_field, flat_adjoint, preferred_element_type=jnp.float32)
        * cell_scale
    )
    bias_term = jnp.sum(flat_adjoint.astype(jnp.float32), axis=0) * cell_scale
    grad_point, grad_bias = lax.psum((point_term, bias_term), ("gx", "gy"))
    back_field = synthesis(
        mode_adjoint, z_plain.astype(jnp.float32), y_table, x_whole, rows_x, rows_y
    )
    grad_field = (channel_mix(adjoint, point_weight.T) + back_field).astype(jnp.bfloat16)
    return (grad_field, grad_spectral, grad_point, grad_bias)


BF = jnp.bfloat16
F32 = jnp.float32
LANES = 128
CHUNKS = KZ * C // LANES
WIDE = KZ * C
SUM_ROWS = 16


def dot(left, right, dims=((1,), (0,))):
    return lax.dot_general(left, right, (dims, ((), ())), preferred_element_type=F32)


def halves(values):
    high = values.astype(BF)
    return high, (values - high.astype(F32)).astype(BF)


def halved(values, table, dims):
    high, low = halves(values)
    both = dot(jnp.concatenate([high, low], axis=0), table, ((dims[0],), (dims[1],)))
    return both[: values.shape[0]] + both[values.shape[0] :]


def iota(shape, axis):
    return lax.broadcasted_iota(jnp.int32, shape, axis)


def lane_take(values, index):
    return jnp.take_along_axis(values, index, axis=1, mode="promise_in_bounds")


def np_halves(table):
    high = table.astype(ml_dtypes.bfloat16).astype(np.float64)
    low = (table - high).astype(ml_dtypes.bfloat16).astype(np.float64)
    return high, low


def np_modes(count, length):
    position = np.arange(count)
    return np.where(position < count // 2, position, length - count + position)


def np_angles(positions, modes, length):
    return 2.0 * np.pi * ((positions[:, None] * modes[None, :]) % length) / length


def depth_rows():
    angles = np_angles(np.arange(NZ), np.arange(KZ), NZ)
    table = np.stack([np.cos(angles), -np.sin(angles)], axis=1).astype(ml_dtypes.bfloat16)
    return np.repeat(table.astype(np.float32).reshape(NZ, 2 * KZ), C, axis=1)


def spread_table():
    hit = np.repeat(np.eye(C, dtype=np.float32), C, axis=1)
    return np.tile(hit, (LANES // C, 1)).astype(ml_dtypes.bfloat16)


def y_tables(full_y, rows_y, x_parts, y_parts):
    angles = np_angles(np.arange(full_y), np_modes(KY, full_y), full_y)
    table = np.stack([np.cos(angles), -np.sin(angles)], axis=-1)
    high, low = np_halves(table)
    forward, inverse = [], []
    for device in range(x_parts * y_parts):
        own_x, own_y = device // y_parts, device % y_parts
        order = [
            (own_x ^ turn) * y_parts + (own_y ^ step)
            for turn in range(x_parts)
            for step in range(y_parts)
        ]
        rows = slice(own_y * rows_y, (own_y + 1) * rows_y)

        def picked(values):
            block = values[rows][:, order].reshape(rows_y, x_parts, y_parts, 2)
            return block.transpose(0, 1, 3, 2).reshape(rows_y, 2 * KY)

        forward.append(np.concatenate([picked(high), picked(low)], axis=1).T)
        inverse.append(np.concatenate([picked(high), picked(low), picked(high)], axis=1))
    return tuple(np.stack(part).astype(ml_dtypes.bfloat16) for part in (forward, inverse))


def x_tables(full_x, rows_x, factor, y_parts):
    angles = np_angles(np.arange(full_x), np_modes(KX, full_x), full_x)
    cosine, sine = np.cos(angles) * factor, np.sin(angles) * factor
    table = np.stack([np.stack([cosine, -sine], -1), np.stack([sine, cosine], -1)], axis=1)
    blocked = table.reshape(full_x // rows_x, rows_x * 2, KX * 2)
    same = np.eye(y_parts)

    def packed(spread):
        high, low = np_halves(spread)
        return np.concatenate([high, low, high], axis=2).astype(ml_dtypes.bfloat16)

    forward = np.einsum("grm,de->gdmre", blocked, same)
    inverse = np.einsum("grm,de->grdem", blocked, same)
    parts, rows, modes = blocked.shape
    return (
        packed(forward.reshape(parts, y_parts * modes, rows * y_parts)),
        packed(inverse.reshape(parts, rows * y_parts, y_parts * modes)),
    )


def tripled(values):
    high, low = halves(values)
    return jnp.concatenate([high, high, low], axis=0)


def lanes_of(values, step):
    return values[:, step * LANES : (step + 1) * LANES]


def read_lanes(ref, rows):
    pieces = [ref[i * rows : (i + 1) * rows, :] for i in range(CHUNKS)]
    return jnp.concatenate(pieces, axis=1)


def write_lanes(ref, values, rows, start=0):
    for chunk in range(CHUNKS):
        first = chunk * rows + start
        ref[first : first + values.shape[0], :] = lanes_of(values, chunk)


def turned(values):
    tiles = values.reshape(values.shape[0] // 8, 8, values.shape[1])
    return pltpu.roll(tiles, 4, 1).reshape(values.shape)


def part_sign(rows):
    return jnp.where(iota((rows, 1), 0) % 8 < 4, -1.0, 1.0).astype(F32)


def y_spectrum(values, table, rows_x, rows_y):
    planes = []
    half = table.shape[0] // 2
    for x in range(rows_x):
        both = dot(table, values[x * rows_y : (x + 1) * rows_y])
        planes.append(both[:half] + both[half:])
    return jnp.concatenate(planes, axis=0)


def z_spectrum(both, out_refs, rows_x):
    whole = both[:, :WIDE] + part_sign(both.shape[0]) * turned(both[:, WIDE:])
    turns = len(out_refs)
    for x in range(rows_x):
        for turn in range(turns):
            block = whole[(x * turns + turn) * 8 : (x * turns + turn + 1) * 8]
            write_lanes(out_refs[turn], block, rows_x * 8, x * 8)


def z_synthesis(in_refs, depth_ref, rows_x, exact=True):
    blocks = [read_lanes(ref, rows_x * 8) for ref in in_refs]
    modes = jnp.concatenate(blocks, axis=0)
    other = -part_sign(modes.shape[0]) * turned(modes)
    stacked = jnp.concatenate([modes, other], axis=1)
    if exact:
        return halved(stacked, depth_ref[...], (1, 1))
    return dot(stacked.astype(BF), depth_ref[...], ((1,), (1,)))


def y_synthesis(planes, table, x, rows_x):
    turns = planes.shape[0] // (8 * rows_x)
    rows = [(turn * rows_x + x) * 8 for turn in range(turns)]
    return dot(table, tripled(jnp.concatenate([planes[r : r + 8] for r in rows], axis=0)))


def mixing_matrix(weight_ref):
    wide = 8 * C
    pick = (iota((wide, C), 0) % C == iota((wide, C), 1)).astype(F32).astype(BF)
    tall = dot(pick, weight_ref[...]).astype(BF)
    tiled = dot(tall, pick, ((1,), (1,)))
    shape = (wide, wide)
    return jnp.where(iota(shape, 0) // C == iota(shape, 1) // C, tiled, 0.0).astype(BF)


def mixed(values, matrix, dims):
    wide = matrix.shape[0]
    pieces = []
    for start in range(0, values.shape[1], wide):
        pieces.append(dot(values[:, start : start + wide], matrix, dims))
    return jnp.concatenate(pieces, axis=1)


def folded(row):
    total = row[:, :LANES]
    for start in range(LANES, row.shape[1], LANES):
        total = total + row[:, start : start + LANES]
    total = total + pltpu.roll(total, 64, 1)
    return total + pltpu.roll(total, 32, 1)


def depth_factor():
    return jnp.where(iota((1, WIDE), 1) < C, 1.0, 2.0).astype(F32)


def mode_row(ref, row):
    wide = jnp.broadcast_to(ref[pl.ds(row, 1), :], (KZ, WIDE))
    group = iota((KZ, LANES), 0) // 4
    chosen = wide[:, :LANES]
    for chunk in range(1, CHUNKS):
        chosen = jnp.where(group == chunk, wide[:, chunk * LANES : (chunk + 1) * LANES], chosen)
    return chosen


def in_index(step):
    return iota((KZ, LANES), 0) % 4 * C + step * 4 + iota((KZ, LANES), 1) // C


def out_index():
    return iota((KZ, LANES), 0) % 4 * C + iota((KZ, LANES), 1) % C


def own_group():
    return iota((KZ, LANES), 0) % 4 == iota((KZ, LANES), 1) // C


def gathered_rows(scratch):
    pieces = []
    for chunk in range(CHUNKS):
        terms = [scratch[pl.ds(chunk * 4 + a, 2 * KX, stride=KZ), :] for a in range(4)]
        pieces.append((terms[0] + terms[1]) + (terms[2] + terms[3]))
    return jnp.concatenate(pieces, axis=1)


def weight_parts(weight_ref, mode):
    start = pl.multiple_of(mode * 2 * C * C, LANES)
    both = weight_ref[:, pl.ds(start, 2 * C * C)].astype(F32)
    return both[:, : C * C], both[:, C * C :]


def device_index():
    return lax.axis_index("gx") * lax.axis_size("gy") + lax.axis_index("gy")


def fill_depth(rows_ref, depth_ref):
    count, wide = rows_ref.shape
    same = iota((C, wide), 0) == iota((C, wide), 1) % C
    for z in range(count):
        row = jnp.broadcast_to(rows_ref[z : z + 1, :], (C, wide))
        depth_ref[z * C : (z + 1) * C, :] = jnp.where(same, row, 0.0).astype(BF)


def first_kernel(
    rows_x,
    rows_y,
    field_ref,
    table_ref,
    rows_ref,
    point_ref,
    back_ref,
    modes_ref,
    cells_ref,
    spread_ref,
    *refs,
):
    out_refs, refs = refs[:-11], refs[-11:]
    depth, mixing_ref, table, back, to_modes, to_cells, spread, field, rows, point, gates = refs
    device = device_index()
    half = field.shape[0] // 2
    pairs = [(rows_ref, rows), (point_ref, point), (table_ref.at[device], table)]
    for part in range(2):
        block = pl.ds(part * half, half)
        pairs.append((field_ref.at[block], field.at[block]))
    pairs += [(back_ref.at[device], back), (modes_ref, to_modes), (cells_ref, to_cells)]
    pairs += [(spread_ref, spread)]
    copies = [
        pltpu.make_async_copy(source, target, gates.at[turn])
        for turn, (source, target) in enumerate(pairs)
    ]
    for copy in copies:
        copy.start()
    copies[0].wait()
    fill_depth(rows, depth)
    copies[1].wait()
    mixing_ref[...] = mixing_matrix(point)
    for copy in copies[2:5]:
        copy.wait()
    planes = y_spectrum(field[...], table[...], rows_x, rows_y)
    z_spectrum(halved(planes, depth[...], (1, 0)), out_refs, rows_x)
    for copy in copies[5:]:
        copy.wait()


def x_forward_kernel(turns, table_ref, *refs):
    in_refs, refs = unqueued(refs[:turns], FORWARD_X), refs[turns:]
    rows = table_ref.shape[2] // 3
    own = lax.axis_index("gx")
    total = None
    for turn in range(turns):
        term = dot(table_ref[own ^ turn], tripled(read_lanes(in_refs[turn], rows)))
        total = term if total is None else total + term
    modes = 2 * KX
    steps = total.shape[0] // modes
    for step, ref in enumerate(refs[-steps:]):
        write_lanes(ref, total[step * modes : (step + 1) * modes], modes)
        if len(refs) > steps:
            ref[CHUNKS * modes :, :] = refs[0][...]


def x_inverse_kernel(steps, turns, table_ref, *refs):
    in_refs, refs = unqueued(refs[:steps], INVERSE_Y), refs[steps:]
    values = tripled(jnp.concatenate([read_lanes(ref, 2 * KX) for ref in in_refs], axis=0))
    own = lax.axis_index("gx")
    rows = table_ref.shape[1]
    table = jnp.concatenate([table_ref[own ^ turn] for turn in range(turns)], axis=0)
    cells = dot(table, values)
    for turn, ref in enumerate(refs[-turns:]):
        write_lanes(ref, cells[turn * rows : (turn + 1) * rows], rows)
        if len(refs) > turns:
            ref[CHUNKS * rows :, :] = refs[0][...]


FORWARD_X, FORWARD_Y, INVERSE_Y, INVERSE_X = ((2, 1, 3), (1, 2, 3), (1, 2, 3), (2, 3, 1))


def queued(blocks, order):
    return [blocks[0]] + [blocks[turn] for turn in order]


def unqueued(refs, order):
    return [refs[0]] + [refs[1 + order.index(turn)] for turn in range(1, len(refs))]


def summed_modes(in_refs):
    return functools.reduce(jnp.add, [read_lanes(ref, 2 * KX) for ref in in_refs])


def stacked_modes(ref):
    keep = own_group()
    rows = [jnp.where(keep, mode_row(ref, row), 0.0) for row in range(2 * KX)]
    return jnp.concatenate(rows, axis=0)


def product_kernel(steps, weight_ref, spread_ref, *refs):
    in_refs, (out_ref, spec_ref, scratch, wide) = refs[:steps], refs[steps:]
    spec_ref[...] = summed_modes(in_refs)
    high, low = halves(stacked_modes(spec_ref))
    spread = spread_ref[...]
    wide[...] = dot(
        jnp.concatenate([high, low], axis=1), jnp.concatenate([spread, spread], axis=0)
    )

    def step(mode, carry):
        real_w, imag_w = weight_parts(weight_ref, mode)
        start = pl.multiple_of(2 * mode * KZ, 2 * KZ)
        both = wide[pl.ds(start, 2 * KZ), :]
        real_sum = jnp.zeros((KZ, LANES), F32)
        imag_sum = jnp.zeros((KZ, LANES), F32)
        for part in range(C // 4):
            real_v, imag_v = lanes_of(both[:KZ], part), lanes_of(both[KZ:], part)
            real_p, imag_p = lanes_of(real_w, part), lanes_of(imag_w, part)
            real_sum = real_sum + (real_v * real_p - imag_v * imag_p)
            imag_sum = imag_sum + (real_v * imag_p + imag_v * real_p)
        scratch[pl.ds(start, 2 * KZ), :] = jnp.concatenate([real_sum, imag_sum], axis=0)
        return carry

    lax.fori_loop(0, KX, step, 0, unroll=KX)
    shape = (LANES, LANES)
    same = (iota(shape, 0) % C == iota(shape, 1) % C).astype(F32).astype(BF)
    high, low = halves(scratch[...])
    total = dot(jnp.concatenate([high, low], axis=1), jnp.concatenate([same, same], axis=0))
    scratch[...] = own_rows(total)
    write_lanes(out_ref, gathered_rows(scratch) * depth_factor(), 2 * KX)


def own_rows(values):
    keep = iota(values.shape, 0) % 4 == iota(values.shape, 1) // C
    return jnp.where(keep, values, 0.0)


def point_kernel(field_ref, mixing_ref, bias_ref, out_ref):
    bias = jnp.concatenate([bias_ref[...]] * NZ, axis=1)
    out_ref[...] = mixed(field_ref[...], mixing_ref[...], ((1,), (0,))) + bias


def middle_kernel(
    rows_x,
    rows_y,
    turns,
    base_ref,
    cotangent_ref,
    table_ref,
    back_ref,
    depth_ref,
    *refs,
):
    in_refs = unqueued(refs[:turns], INVERSE_X)
    out_refs, (adjoint_ref, value_ref) = refs[turns:-2], refs[-2:]
    planes = z_synthesis(in_refs, depth_ref, rows_x)
    for x in range(rows_x):
        block = slice(x * rows_y, (x + 1) * rows_y)
        spectral = y_synthesis(planes, back_ref[...], x, rows_x)
        value_ref[block, :] = spectral + base_ref[block, :]
    value = value_ref[...]
    root = math.sqrt(2.0 / math.pi)
    square = value * value
    bent = jnp.tanh(value * (root + (root * 0.044715) * square))
    tail = value * (root + (3.0 * root * 0.044715) * square)
    slope = (0.5 + 0.5 * bent) * (1.0 + (1.0 - bent) * tail)
    adjoint = (cotangent_ref[...].astype(F32) * slope).astype(BF)
    adjoint_ref[...] = adjoint
    modes = y_spectrum(adjoint, table_ref[...], rows_x, rows_y).astype(BF)
    z_spectrum(dot(modes, depth_ref[...]), out_refs, rows_x)


def sums_kernel(field_ref, adjoint_ref, mixing_ref, out_ref, sums_ref):
    field, adjoint, mixing = field_ref[...], adjoint_ref[...], mixing_ref[...]
    out_ref[...] = mixed(adjoint, mixing, ((1,), (1,)))
    wide = mixing.shape[0]
    total = jnp.zeros((wide, wide), F32)
    for start in range(0, NZ * C, wide):
        total = total + dot(
            field[:, start : start + wide], adjoint[:, start : start + wide], ((0,), (0,))
        )
    total = jnp.where(iota((wide, wide), 0) // C == iota((wide, wide), 1) // C, total, 0.0)
    point = total[:C]
    for start in range(C, wide, C):
        point = point + total[start : start + C]
    point = folded(point)
    group = iota((8, LANES), 1) // C
    packed = point[:8]
    for part in range(1, 4):
        packed = jnp.where(group == part, point[part * 8 : (part + 1) * 8], packed)
    sums_ref[:8, :] = packed
    sums_ref[8:, :] = folded(dot(jnp.ones((8, adjoint.shape[0]), BF), adjoint))


def adjoint_kernel(steps, weight_ref, spread_ref, *refs):
    in_refs, (out_ref, spec_ref, sums_ref, scratch, wide) = refs[:steps], refs[steps:]
    spec_ref[...] = summed_modes(in_refs) * depth_factor()
    sums_ref[...] = functools.reduce(jnp.add, [ref[CHUNKS * 2 * KX :, :] for ref in in_refs])
    index = out_index()

    def step(mode, carry):
        real = lane_take(mode_row(spec_ref, 2 * mode), index)
        imag = lane_take(mode_row(spec_ref, 2 * mode + 1), index)
        real_w, imag_w = weight_parts(weight_ref, mode)
        real_parts, imag_parts = [], []
        for part in range(C // 4):
            real_p, imag_p = lanes_of(real_w, part), lanes_of(imag_w, part)
            real_parts.append(real * real_p + imag * imag_p)
            imag_parts.append(imag * real_p - real * imag_p)
        both = jnp.concatenate(
            [jnp.concatenate(real_parts, axis=1), jnp.concatenate(imag_parts, axis=1)], axis=0
        )
        high, low = halves(both)
        start = pl.multiple_of(2 * mode * KZ, 2 * KZ)
        wide[0, pl.ds(start, 2 * KZ), :] = high
        wide[1, pl.ds(start, 2 * KZ), :] = low
        return carry

    lax.fori_loop(0, KX, step, 0, unroll=KX)
    total = dot(wide[0], spread_ref[...], ((1,), (1,)))
    total = total + dot(wide[1], spread_ref[...], ((1,), (1,)))
    scratch[...] = own_rows(total)
    write_lanes(out_ref, gathered_rows(scratch), 2 * KX)


def weight_kernel(scale, field_ref, adjoint_ref, out_ref, staged, gates):
    index = out_index()
    stores = []
    turns = gates.shape[0]
    modes = KX // turns

    def step(mode, carry):
        row = 2 * mode
        real_v, imag_v = mode_row(field_ref, row), mode_row(field_ref, row + 1)
        real_h = lane_take(mode_row(adjoint_ref, row), index) * scale
        imag_h = lane_take(mode_row(adjoint_ref, row + 1), index) * scale
        real_g, imag_g = [], []
        for part in range(C // 4):
            take = in_index(part)
            real, imag = lane_take(real_v, take), lane_take(imag_v, take)
            real_g.append(real * real_h + imag * imag_h)
            imag_g.append(real * imag_h - imag * real_h)
        start = pl.multiple_of(mode * 2 * C * C, LANES)
        staged[:, pl.ds(start, 2 * C * C)] = jnp.concatenate(real_g + imag_g, axis=1)
        return carry

    for turn in range(turns):
        lax.fori_loop(turn * modes, (turn + 1) * modes, step, 0, unroll=2)
        block = pl.ds(turn * modes * 2 * C * C, modes * 2 * C * C)
        stores.append(
            pltpu.make_async_copy(staged.at[:, block], out_ref.at[:, block], gates.at[turn])
        )
        stores[-1].start()
    for store in stores:
        store.wait()


def last_kernel(rows_x, rows_y, turns, scale, mixed_ref, back_ref, depth_ref, *refs):
    in_refs = unqueued(refs[:turns], INVERSE_X)
    out_ref, point_ref, bias_ref, result, gates = refs[turns:]
    total = functools.reduce(jnp.add, [ref[ref.shape[0] - SUM_ROWS :, :] for ref in in_refs])
    total = total * scale
    packed = total[:8]
    for part in range(4):
        piece = packed if part == 0 else pltpu.roll(packed, LANES - part * C, 1)
        point_ref[part * 8 : (part + 1) * 8, :] = piece[:, :C]
    bias_ref[...] = total[8:9, :C]
    planes = z_synthesis(in_refs, depth_ref, rows_x, exact=False)
    stores = []
    for x in range(rows_x):
        block = slice(x * rows_y, (x + 1) * rows_y)
        spectral = y_synthesis(planes, back_ref[...], x, rows_x)
        result[block, :] = (mixed_ref[block, :] + spectral).astype(BF)
        span = pl.ds(x * rows_y, rows_y)
        stores.append(pltpu.make_async_copy(result.at[span], out_ref.at[span], gates.at[x]))
        stores[-1].start()
    for store in stores:
        store.wait()


NEAR = pl.BlockSpec(memory_space=pltpu.VMEM)
FAR = pl.BlockSpec(memory_space=pltpu.HBM)


def call(kernel, ins, outs, scratch=()):
    shapes = []
    for shape, kind, inner in outs:
        if inner is None:
            shapes.append(jax.ShapeDtypeStruct(shape, kind))
        else:
            shapes.append((pltpu.VMEM if inner else pltpu.HBM)(shape, kind))
    function = pl.pallas_call(
        kernel,
        out_shape=shapes,
        in_specs=[NEAR if inner else FAR for inner in ins],
        out_specs=[FAR if inner is False else NEAR for _, _, inner in outs],
        scratch_shapes=list(scratch),
        compiler_params=pltpu.CompilerParams(vmem_limit_bytes=40 * 1024 * 1024),
    )

    def run(*arguments):
        spaces = [pltpu.VMEM if inner else pltpu.HBM for inner in ins]
        return function(*map(pltpu.with_memory_space_constraint, arguments, spaces))

    return run


def exchange(blocks, axis):
    count = lax.axis_size(axis)
    order = [2, 3, 1] if count == 4 else list(range(1, count))
    received = list(blocks)
    for turn in order:
        pairs = [(device, device ^ turn) for device in range(count)]
        received[turn] = lax.ppermute(blocks[turn], axis, pairs)
    return received


def fast_device(field_input, cotangent, spectral_weight, point_weight, point_bias):
    rows_x, rows_y, depth = field_input.shape
    x_parts, y_parts = lax.axis_size("gx"), lax.axis_size("gy")
    full_x, full_y = rows_x * x_parts, rows_y * y_parts
    scale = 1.0 / math.sqrt(full_x * full_y * NZ)
    cells = rows_x * rows_y
    z_rows = jnp.asarray(depth_rows())
    spread_hits = jnp.asarray(spread_table())
    forward_y, inverse_y = map(jnp.asarray, y_tables(full_y, rows_y, x_parts, y_parts))
    forward_x, inverse_x = map(jnp.asarray, x_tables(full_x, rows_x, scale, y_parts))
    field = field_input.reshape(cells, depth)
    bias = point_bias.reshape(1, C)
    cell_rows, mode_rows = CHUNKS * rows_x * 8, CHUNKS * 2 * KX
    cell_block, mode_block = ((cell_rows, LANES), F32, True), ((mode_rows, LANES), F32, True)
    cell_sums = ((cell_rows + SUM_ROWS, LANES), F32, True)
    mode_sums = ((mode_rows + SUM_ROWS, LANES), F32, True)
    spectrum_shape = ((2 * KX, WIDE), F32, True)
    rows_scratch = pltpu.VMEM((2 * KX * KZ, LANES), F32)
    sums_shape = ((SUM_ROWS, LANES), F32, True)
    cell_shape = ((cells, depth), F32, True)
    wide = (KZ, KX * 2 * C * C)

    def forward(blocks, extra, mode_shape):
        received = exchange(blocks, "gx")
        sent = call(
            functools.partial(x_forward_kernel, x_parts),
            [True] * (1 + x_parts + len(extra)),
            [mode_shape] * y_parts,
        )(to_modes, *queued(received, FORWARD_X), *extra)
        return queued(exchange(sent, "gy"), FORWARD_Y)

    def inverse(block, extra, cell_shape):
        received = exchange([block] * y_parts, "gy")
        sent = call(
            functools.partial(x_inverse_kernel, y_parts, x_parts),
            [True] * (1 + y_parts + len(extra)),
            [cell_shape] * x_parts,
        )(to_cells, *queued(received, INVERSE_Y), *extra)
        return queued(exchange(sent, "gx"), INVERSE_X)

    *blocks, depth_table, mixing, table, back, to_modes, to_cells, spread = call(
        functools.partial(first_kernel, rows_x, rows_y),
        [False] * 8,
        [cell_block] * x_parts
        + [((depth, 2 * WIDE), BF, True), ((8 * C, 8 * C), BF, True)]
        + [(part.shape[1:], BF, True) for part in (forward_y, inverse_y)]
        + [(part.shape, BF, True) for part in (forward_x, inverse_x, spread_hits)],
        [
            pltpu.VMEM((cells, depth), BF),
            pltpu.VMEM(z_rows.shape, F32),
            pltpu.VMEM((C, C), BF),
            pltpu.SemaphoreType.DMA((9,)),
        ],
    )(field, forward_y, z_rows, point_weight, inverse_y, forward_x, inverse_x, spread_hits)
    (base,) = call(point_kernel, [True] * 3, [cell_shape])(field, mixing, bias)
    block, field_modes = call(
        functools.partial(product_kernel, y_parts),
        [True] * (2 + y_parts),
        [mode_block, spectrum_shape],
        [rows_scratch, pltpu.VMEM((2 * KX * KZ, C * C), F32)],
    )(spectral_weight, spread, *forward(blocks, [], mode_block))
    *blocks, adjoint = call(
        functools.partial(middle_kernel, rows_x, rows_y, x_parts),
        [True] * (5 + x_parts),
        [cell_block] * x_parts + [((cells, depth), BF, True)],
        [pltpu.VMEM((cells, depth), F32)],
    )(
        base,
        cotangent.reshape(cells, depth),
        table,
        back,
        depth_table,
        *inverse(block, [], cell_block),
    )
    mixed_adjoint, sums = call(sums_kernel, [True] * 3, [cell_shape, sums_shape])(
        field, adjoint, mixing
    )
    block, adjoint_modes, sums = call(
        functools.partial(adjoint_kernel, y_parts),
        [True] * (2 + y_parts),
        [mode_block, spectrum_shape, sums_shape],
        [rows_scratch, pltpu.VMEM((2, 2 * KX * KZ, C * C), BF)],
    )(spectral_weight, spread, *forward(blocks, [sums], mode_sums))
    (grad_spectral,) = call(
        functools.partial(weight_kernel, scale),
        [True] * 2,
        [(wide, F32, False)],
        [pltpu.VMEM(wide, F32), pltpu.SemaphoreType.DMA((4,))],
    )(field_modes, adjoint_modes)
    grad_field, grad_point, grad_bias = call(
        functools.partial(last_kernel, rows_x, rows_y, x_parts, scale),
        [True] * (3 + x_parts),
        [((cells, depth), BF, False), ((C, C), F32, None), ((1, C), F32, None)],
        [pltpu.VMEM((cells, depth), BF), pltpu.SemaphoreType.DMA((rows_x,))],
    )(mixed_adjoint, back, depth_table, *inverse(block, [sums], cell_sums))
    return (
        grad_field.reshape(field_input.shape),
        grad_spectral,
        grad_point,
        grad_bias.reshape(C),
    )


def on_device(*arguments):
    rows_x, rows_y, _ = arguments[0].shape
    x_parts, y_parts = lax.axis_size("gx"), lax.axis_size("gy")
    whole_modes = arguments[2].shape[0] == KZ and y_parts == 4 and x_parts == 4
    if whole_modes and rows_x == 8 and rows_y == 64:
        return fast_device(*arguments)
    return general_device(*arguments)


def solution(mesh):
    return jax.shard_map(
        on_device,
        mesh=mesh,
        in_specs=(
            P(("groups", "gx"), "gy", None),
            P(("groups", "gx"), "gy", None),
            P(("gx", "gy"), None),
            P(),
            P(),
        ),
        out_specs=(
            P(("groups", "gx"), "gy", None),
            P(("groups", "gx", "gy"), None),
            P("groups", None),
            P("groups"),
        ),
        check_vma=False,
    )
```

```python
import functools
import math

import jax
import jax.numpy as jnp
import ml_dtypes
import numpy as np
from jax import lax
from jax.experimental import pallas as pl
from jax.experimental.pallas import tpu as pltpu
from jax.sharding import PartitionSpec as P

C = 32
KX = 16
KY = 16
KZ = 16
NZ = 32


def mode_values(mode_count, length):
    position = jnp.arange(mode_count, dtype=jnp.int32)
    return jnp.where(position < mode_count // 2, position, length - mode_count + position)


def phase_angles(positions, wavenumbers, length):
    steps = positions[:, None] * wavenumbers[None, :] % length
    return 2.0 * math.pi / length * steps.astype(jnp.float32)


def complex_table(positions, wavenumbers, length, factor):
    angles = phase_angles(positions, wavenumbers, length)
    cosine = jnp.cos(angles) * factor
    sine = jnp.sin(angles) * factor
    return jnp.stack(
        [jnp.stack([cosine, -sine], axis=-1), jnp.stack([sine, cosine], axis=-1)], axis=1
    )


def depth_table(depth_count, mode_count):
    angles = phase_angles(
        jnp.arange(depth_count, dtype=jnp.int32),
        jnp.arange(mode_count, dtype=jnp.int32),
        depth_count,
    )
    return jnp.stack([jnp.cos(angles), -jnp.sin(angles)], axis=1).astype(jnp.bfloat16)


def doubled(table):
    factor = jnp.where(jnp.arange(table.shape[2]) == 0, 1.0, 2.0).astype(jnp.float32)
    return table.astype(jnp.float32) * factor[None, None, :]


def spectral_product(spectrum, weights):
    shaped = spectrum.reshape(spectrum.shape[0], KX, 2, C)
    real_in, imag_in = (shaped[:, :, 0], shaped[:, :, 1])
    real_w, imag_w = (weights[:, :, 0], weights[:, :, 1])
    hp = lax.Precision.HIGHEST
    real_out = jnp.einsum("rmi,rmio->rmo", real_in, real_w, precision=hp) - jnp.einsum(
        "rmi,rmio->rmo", imag_in, imag_w, precision=hp
    )
    imag_out = jnp.einsum("rmi,rmio->rmo", real_in, imag_w, precision=hp) + jnp.einsum(
        "rmi,rmio->rmo", imag_in, real_w, precision=hp
    )
    return jnp.stack([real_out, imag_out], axis=2).reshape(spectrum.shape)


def adjoint_product(spectrum, weights):
    shaped = spectrum.reshape(spectrum.shape[0], KX, 2, C)
    real_in, imag_in = (shaped[:, :, 0], shaped[:, :, 1])
    real_w, imag_w = (weights[:, :, 0], weights[:, :, 1])
    hp = lax.Precision.HIGHEST
    real_out = jnp.einsum("rmo,rmio->rmi", real_in, real_w, precision=hp) + jnp.einsum(
        "rmo,rmio->rmi", imag_in, imag_w, precision=hp
    )
    imag_out = jnp.einsum("rmo,rmio->rmi", imag_in, real_w, precision=hp) - jnp.einsum(
        "rmo,rmio->rmi", real_in, imag_w, precision=hp
    )
    return jnp.stack([real_out, imag_out], axis=2).reshape(spectrum.shape)


def weight_gradient(field_spec, adjoint_spec):
    field_shaped = field_spec.reshape(field_spec.shape[0], KX, 2, C)
    adjoint_shaped = adjoint_spec.reshape(adjoint_spec.shape[0], KX, 2, C)
    real_v, imag_v = (field_shaped[:, :, 0], field_shaped[:, :, 1])
    real_h, imag_h = (adjoint_shaped[:, :, 0], adjoint_shaped[:, :, 1])
    real_g = (
        real_v[:, :, :, None] * real_h[:, :, None, :]
        + imag_v[:, :, :, None] * imag_h[:, :, None, :]
    )
    imag_g = (
        real_v[:, :, :, None] * imag_h[:, :, None, :]
        - imag_v[:, :, :, None] * real_h[:, :, None, :]
    )
    return jnp.stack([real_g, imag_g], axis=2).reshape(field_spec.shape[0], KX * 2 * C * C)


def channel_mix(values, weight):
    group_size = max(1, 128 // weight.shape[0])
    block = jnp.kron(jnp.eye(group_size, dtype=weight.dtype), weight)
    rows = values.reshape(-1, block.shape[0])
    return jnp.dot(rows, block, preferred_element_type=jnp.float32).reshape(values.shape)


def spectrum(values, z_table, y_table, x_local, x_whole):
    rows_x, rows_y, _ = values.shape
    hp = lax.Precision.HIGHEST
    shaped = values.reshape(rows_x, rows_y, NZ, C)
    zpart = jnp.einsum(
        "xyzc,zpk->xypkc", shaped, z_table, preferred_element_type=jnp.float32
    ).reshape(rows_x, rows_y, 2, KZ * C)
    ypart = jnp.einsum("xyqm,yqjp->xjpm", zpart, y_table, precision=hp)
    pencil = lax.all_to_all(ypart, "gx", split_axis=1, concat_axis=0, tiled=True)
    mode_rows = pencil.shape[1]
    pencil = pencil.reshape(pencil.shape[0], mode_rows, 2, KZ, C)
    partial_value = jnp.einsum("xjqkc,xqmp->jkmpc", pencil, x_whole, precision=hp).reshape(
        mode_rows * KZ, KX * 2 * C
    )
    return lax.psum_scatter(partial_value, "gy", scatter_dimension=0, tiled=True)


def synthesis(owned, z_float, y_table, x_whole, rows_x, rows_y):
    hp = lax.Precision.HIGHEST
    planes = lax.all_gather(owned, "gy", axis=0, tiled=True)
    mode_rows = planes.shape[0] // KZ
    shaped = planes.reshape(mode_rows, KZ, KX, 2, C)
    wide = jnp.einsum("jkmqc,xpmq->xjpkc", shaped, x_whole, precision=hp).reshape(
        x_whole.shape[0], mode_rows, 2, KZ * C
    )
    slab = lax.all_to_all(wide, "gx", split_axis=0, concat_axis=1, tiled=True)
    ypart = jnp.einsum("xjqm,ypjq->xypm", slab, y_table, precision=hp).reshape(
        rows_x, rows_y, 2, KZ, C
    )
    return jnp.einsum("xypkc,zpk->xyzc", ypart, z_float, precision=hp).reshape(
        rows_x, rows_y, NZ * C
    )


def general_device(field_input, cotangent, spectral_weight, point_weight, point_bias):
    rows_x, rows_y, _ = field_input.shape
    full_x = rows_x * lax.axis_size("gx")
    full_y = rows_y * lax.axis_size("gy")
    cell_scale = 1.0 / math.sqrt(full_x * full_y * NZ)
    x_start = lax.axis_index("gx") * rows_x
    y_start = lax.axis_index("gy") * rows_y
    y_table = complex_table(
        y_start + jnp.arange(rows_y, dtype=jnp.int32), mode_values(KY, full_y), full_y, 1.0
    )
    x_local = complex_table(
        x_start + jnp.arange(rows_x, dtype=jnp.int32), mode_values(KX, full_x), full_x, cell_scale
    )
    x_whole = complex_table(
        jnp.arange(full_x, dtype=jnp.int32), mode_values(KX, full_x), full_x, cell_scale
    )
    z_plain = depth_table(NZ, KZ)
    z_double_float = doubled(z_plain)
    z_double = z_double_float.astype(jnp.bfloat16)
    field_spec = spectrum(field_input, z_plain, y_table, x_local, x_whole)
    weights = spectral_weight.astype(jnp.float32).reshape(-1, KX, 2, C, C)
    mode_output = spectral_product(field_spec, weights)
    spectral_out = synthesis(mode_output, z_double_float, y_table, x_whole, rows_x, rows_y)
    bias_row = jnp.tile(point_bias, NZ)
    preact = spectral_out + channel_mix(field_input, point_weight) + bias_row
    _, pullback = jax.vjp(jax.nn.gelu, preact)
    adjoint = pullback(cotangent.astype(jnp.float32))[0].astype(jnp.bfloat16)
    adjoint_spec = spectrum(adjoint, z_double, y_table, x_local, x_whole)
    grad_spectral = weight_gradient(field_spec, adjoint_spec) * cell_scale
    mode_adjoint = adjoint_product(adjoint_spec, weights)
    flat_field = field_input.reshape(-1, C)
    flat_adjoint = adjoint.reshape(-1, C)
    point_term = (
        jnp.einsum("rc,rd->cd", flat_field, flat_adjoint, preferred_element_type=jnp.float32)
        * cell_scale
    )
    bias_term = jnp.sum(flat_adjoint.astype(jnp.float32), axis=0) * cell_scale
    grad_point, grad_bias = lax.psum((point_term, bias_term), ("gx", "gy"))
    back_field = synthesis(
        mode_adjoint, z_plain.astype(jnp.float32), y_table, x_whole, rows_x, rows_y
    )
    grad_field = (channel_mix(adjoint, point_weight.T) + back_field).astype(jnp.bfloat16)
    return (grad_field, grad_spectral, grad_point, grad_bias)


BF = jnp.bfloat16
F32 = jnp.float32
LANES = 128
CHUNKS = KZ * C // LANES
WIDE = KZ * C
SUM_ROWS = 16


def dot(left, right, dims=((1,), (0,))):
    return lax.dot_general(left, right, (dims, ((), ())), preferred_element_type=F32)


def halves(values):
    high = values.astype(BF)
    return high, (values - high.astype(F32)).astype(BF)


def halved(values, table, dims):
    high, low = halves(values)
    both = dot(jnp.concatenate([high, low], axis=0), table, ((dims[0],), (dims[1],)))
    return both[: values.shape[0]] + both[values.shape[0] :]


def iota(shape, axis):
    return lax.broadcasted_iota(jnp.int32, shape, axis)


def lane_take(values, index):
    return jnp.take_along_axis(values, index, axis=1, mode="promise_in_bounds")


def np_halves(table):
    high = table.astype(ml_dtypes.bfloat16).astype(np.float64)
    low = (table - high).astype(ml_dtypes.bfloat16).astype(np.float64)
    return high, low


def np_modes(count, length):
    position = np.arange(count)
    return np.where(position < count // 2, position, length - count + position)


def np_angles(positions, modes, length):
    return 2.0 * np.pi * ((positions[:, None] * modes[None, :]) % length) / length


def depth_rows():
    angles = np_angles(np.arange(NZ), np.arange(KZ), NZ)
    table = np.stack([np.cos(angles), -np.sin(angles)], axis=1).astype(ml_dtypes.bfloat16)
    return np.repeat(table.astype(np.float32).reshape(NZ, 2 * KZ), C, axis=1)


def spread_table():
    hit = np.repeat(np.eye(C, dtype=np.float32), C, axis=1)
    return np.tile(hit, (LANES // C, 1)).astype(ml_dtypes.bfloat16)


def y_tables(full_y, rows_y, x_parts, y_parts):
    angles = np_angles(np.arange(full_y), np_modes(KY, full_y), full_y)
    table = np.stack([np.cos(angles), -np.sin(angles)], axis=-1)
    high, low = np_halves(table)
    forward, inverse = [], []
    for device in range(x_parts * y_parts):
        own_x, own_y = device // y_parts, device % y_parts
        order = [
            (own_x ^ turn) * y_parts + (own_y ^ step)
            for turn in range(x_parts)
            for step in range(y_parts)
        ]
        rows = slice(own_y * rows_y, (own_y + 1) * rows_y)

        def picked(values):
            block = values[rows][:, order].reshape(rows_y, x_parts, y_parts, 2)
            return block.transpose(0, 1, 3, 2).reshape(rows_y, 2 * KY)

        forward.append(np.concatenate([picked(high), picked(low)], axis=1).T)
        inverse.append(np.concatenate([picked(high), picked(low), picked(high)], axis=1))
    return tuple(np.stack(part).astype(ml_dtypes.bfloat16) for part in (forward, inverse))


def x_tables(full_x, rows_x, factor, y_parts):
    angles = np_angles(np.arange(full_x), np_modes(KX, full_x), full_x)
    cosine, sine = np.cos(angles) * factor, np.sin(angles) * factor
    table = np.stack([np.stack([cosine, -sine], -1), np.stack([sine, cosine], -1)], axis=1)
    blocked = table.reshape(full_x // rows_x, rows_x * 2, KX * 2)
    same = np.eye(y_parts)

    def packed(spread):
        high, low = np_halves(spread)
        return np.concatenate([high, low, high], axis=2).astype(ml_dtypes.bfloat16)

    forward = np.einsum("grm,de->gdmre", blocked, same)
    inverse = np.einsum("grm,de->grdem", blocked, same)
    parts, rows, modes = blocked.shape
    return (
        packed(forward.reshape(parts, y_parts * modes, rows * y_parts)),
        packed(inverse.reshape(parts, rows * y_parts, y_parts * modes)),
    )


def tripled(values):
    high, low = halves(values)
    return jnp.concatenate([high, high, low], axis=0)


def lanes_of(values, step):
    return values[:, step * LANES : (step + 1) * LANES]


def read_lanes(ref, rows):
    pieces = [ref[i * rows : (i + 1) * rows, :] for i in range(CHUNKS)]
    return jnp.concatenate(pieces, axis=1)


def write_lanes(ref, values, rows, start=0):
    for chunk in range(CHUNKS):
        first = chunk * rows + start
        ref[first : first + values.shape[0], :] = lanes_of(values, chunk)


def turned(values):
    tiles = values.reshape(values.shape[0] // 8, 8, values.shape[1])
    return pltpu.roll(tiles, 4, 1).reshape(values.shape)


def part_sign(rows):
    return jnp.where(iota((rows, 1), 0) % 8 < 4, -1.0, 1.0).astype(F32)


def y_spectrum(values, table, rows_x, rows_y):
    planes = []
    half = table.shape[0] // 2
    for x in range(rows_x):
        both = dot(table, values[x * rows_y : (x + 1) * rows_y])
        planes.append(both[:half] + both[half:])
    return jnp.concatenate(planes, axis=0)


def z_spectrum(both, out_refs, rows_x):
    whole = both[:, :WIDE] + part_sign(both.shape[0]) * turned(both[:, WIDE:])
    turns = len(out_refs)
    for x in range(rows_x):
        for turn in range(turns):
            block = whole[(x * turns + turn) * 8 : (x * turns + turn + 1) * 8]
            write_lanes(out_refs[turn], block, rows_x * 8, x * 8)


def z_synthesis(in_refs, depth_ref, rows_x, exact=True):
    blocks = [read_lanes(ref, rows_x * 8) for ref in in_refs]
    modes = jnp.concatenate(blocks, axis=0)
    other = -part_sign(modes.shape[0]) * turned(modes)
    stacked = jnp.concatenate([modes, other], axis=1)
    if exact:
        return halved(stacked, depth_ref[...], (1, 1))
    return dot(stacked.astype(BF), depth_ref[...], ((1,), (1,)))


def y_synthesis(planes, table, x, rows_x):
    turns = planes.shape[0] // (8 * rows_x)
    rows = [(turn * rows_x + x) * 8 for turn in range(turns)]
    return dot(table, tripled(jnp.concatenate([planes[r : r + 8] for r in rows], axis=0)))


def mixing_matrix(weight_ref):
    wide = 8 * C
    pick = (iota((wide, C), 0) % C == iota((wide, C), 1)).astype(F32).astype(BF)
    tall = dot(pick, weight_ref[...]).astype(BF)
    tiled = dot(tall, pick, ((1,), (1,)))
    shape = (wide, wide)
    return jnp.where(iota(shape, 0) // C == iota(shape, 1) // C, tiled, 0.0).astype(BF)


def mixed(values, matrix, dims):
    wide = matrix.shape[0]
    pieces = []
    for start in range(0, values.shape[1], wide):
        pieces.append(dot(values[:, start : start + wide], matrix, dims))
    return jnp.concatenate(pieces, axis=1)


def folded(row):
    total = row[:, :LANES]
    for start in range(LANES, row.shape[1], LANES):
        total = total + row[:, start : start + LANES]
    total = total + pltpu.roll(total, 64, 1)
    return total + pltpu.roll(total, 32, 1)


def depth_factor():
    return jnp.where(iota((1, WIDE), 1) < C, 1.0, 2.0).astype(F32)


def mode_row(ref, row):
    wide = jnp.broadcast_to(ref[pl.ds(row, 1), :], (KZ, WIDE))
    group = iota((KZ, LANES), 0) // 4
    chosen = wide[:, :LANES]
    for chunk in range(1, CHUNKS):
        chosen = jnp.where(group == chunk, wide[:, chunk * LANES : (chunk + 1) * LANES], chosen)
    return chosen


def in_index(step):
    return iota((KZ, LANES), 0) % 4 * C + step * 4 + iota((KZ, LANES), 1) // C


def out_index():
    return iota((KZ, LANES), 0) % 4 * C + iota((KZ, LANES), 1) % C


def own_group():
    return iota((KZ, LANES), 0) % 4 == iota((KZ, LANES), 1) // C


def gathered_rows(scratch):
    pieces = []
    for chunk in range(CHUNKS):
        terms = [scratch[pl.ds(chunk * 4 + a, 2 * KX, stride=KZ), :] for a in range(4)]
        pieces.append((terms[0] + terms[1]) + (terms[2] + terms[3]))
    return jnp.concatenate(pieces, axis=1)


def weight_parts(weight_ref, mode):
    start = pl.multiple_of(mode * 2 * C * C, LANES)
    both = weight_ref[:, pl.ds(start, 2 * C * C)].astype(F32)
    return both[:, : C * C], both[:, C * C :]


def device_index():
    return lax.axis_index("gx") * lax.axis_size("gy") + lax.axis_index("gy")


def fill_depth(rows_ref, depth_ref):
    count, wide = rows_ref.shape
    same = iota((C, wide), 0) == iota((C, wide), 1) % C
    for z in range(count):
        row = jnp.broadcast_to(rows_ref[z : z + 1, :], (C, wide))
        depth_ref[z * C : (z + 1) * C, :] = jnp.where(same, row, 0.0).astype(BF)


def first_kernel(
    rows_x,
    rows_y,
    field_ref,
    table_ref,
    rows_ref,
    back_ref,
    modes_ref,
    cells_ref,
    spread_ref,
    *refs,
):
    out_refs, refs = refs[:-9], refs[-9:]
    depth, table, back, to_modes, to_cells, spread, field, rows, gates = refs
    device = device_index()
    half = field.shape[0] // 2
    pairs = [(rows_ref, rows), (table_ref.at[device], table)]
    for part in range(2):
        block = pl.ds(part * half, half)
        pairs.append((field_ref.at[block], field.at[block]))
    needed = len(pairs)
    pairs += [(back_ref.at[device], back), (modes_ref, to_modes), (cells_ref, to_cells)]
    pairs += [(spread_ref, spread)]
    copies = [
        pltpu.make_async_copy(source, target, gates.at[turn])
        for turn, (source, target) in enumerate(pairs)
    ]
    for copy in copies[:needed]:
        copy.start()
    copies[0].wait()
    fill_depth(rows, depth)
    for copy in copies[1:needed]:
        copy.wait()
    for copy in copies[needed:]:
        copy.start()
    planes = y_spectrum(field[...], table[...], rows_x, rows_y)
    z_spectrum(halved(planes, depth[...], (1, 0)), out_refs, rows_x)
    for copy in copies[needed:]:
        copy.wait()


def x_forward_kernel(turns, table_ref, *refs):
    in_refs, refs = unqueued(refs[:turns], FORWARD_X), refs[turns:]
    rows = table_ref.shape[2] // 3
    own = lax.axis_index("gx")
    total = None
    for turn in range(turns):
        term = dot(table_ref[own ^ turn], tripled(read_lanes(in_refs[turn], rows)))
        total = term if total is None else total + term
    modes = 2 * KX
    steps = total.shape[0] // modes
    for step, ref in enumerate(refs[-steps:]):
        write_lanes(ref, total[step * modes : (step + 1) * modes], modes)
        if len(refs) > steps:
            ref[CHUNKS * modes :, :] = refs[0][...]


def x_inverse_kernel(steps, turns, table_ref, *refs):
    in_refs, refs = unqueued(refs[:steps], INVERSE_Y), refs[steps:]
    values = tripled(jnp.concatenate([read_lanes(ref, 2 * KX) for ref in in_refs], axis=0))
    own = lax.axis_index("gx")
    rows = table_ref.shape[1]
    table = jnp.concatenate([table_ref[own ^ turn] for turn in range(turns)], axis=0)
    cells = dot(table, values)
    for turn, ref in enumerate(refs[-turns:]):
        write_lanes(ref, cells[turn * rows : (turn + 1) * rows], rows)
        if len(refs) > turns:
            ref[CHUNKS * rows :, :] = refs[0][...]


FORWARD_X, FORWARD_Y, INVERSE_Y, INVERSE_X = ((2, 1, 3), (1, 2, 3), (1, 2, 3), (2, 3, 1))


def queued(blocks, order):
    return [blocks[0]] + [blocks[turn] for turn in order]


def unqueued(refs, order):
    return [refs[0]] + [refs[1 + order.index(turn)] for turn in range(1, len(refs))]


def summed_modes(in_refs):
    return functools.reduce(jnp.add, [read_lanes(ref, 2 * KX) for ref in in_refs])


def stacked_modes(ref):
    keep = own_group()
    rows = [jnp.where(keep, mode_row(ref, row), 0.0) for row in range(2 * KX)]
    return jnp.concatenate(rows, axis=0)


def product_kernel(steps, weight_ref, spread_ref, *refs):
    in_refs, (out_ref, spec_ref, scratch, wide) = refs[:steps], refs[steps:]
    spec_ref[...] = summed_modes(in_refs)
    high, low = halves(stacked_modes(spec_ref))
    spread = spread_ref[...]
    wide[...] = dot(
        jnp.concatenate([high, low], axis=1), jnp.concatenate([spread, spread], axis=0)
    )

    def step(mode, carry):
        real_w, imag_w = weight_parts(weight_ref, mode)
        start = pl.multiple_of(2 * mode * KZ, 2 * KZ)
        both = wide[pl.ds(start, 2 * KZ), :]
        real_sum = jnp.zeros((KZ, LANES), F32)
        imag_sum = jnp.zeros((KZ, LANES), F32)
        for part in range(C // 4):
            real_v, imag_v = lanes_of(both[:KZ], part), lanes_of(both[KZ:], part)
            real_p, imag_p = lanes_of(real_w, part), lanes_of(imag_w, part)
            real_sum = real_sum + (real_v * real_p - imag_v * imag_p)
            imag_sum = imag_sum + (real_v * imag_p + imag_v * real_p)
        scratch[pl.ds(start, 2 * KZ), :] = jnp.concatenate([real_sum, imag_sum], axis=0)
        return carry

    lax.fori_loop(0, KX, step, 0, unroll=KX)
    shape = (LANES, LANES)
    same = (iota(shape, 0) % C == iota(shape, 1) % C).astype(F32).astype(BF)
    high, low = halves(scratch[...])
    total = dot(jnp.concatenate([high, low], axis=1), jnp.concatenate([same, same], axis=0))
    scratch[...] = own_rows(total)
    write_lanes(out_ref, gathered_rows(scratch) * depth_factor(), 2 * KX)


def own_rows(values):
    keep = iota(values.shape, 0) % 4 == iota(values.shape, 1) // C
    return jnp.where(keep, values, 0.0)


def point_kernel(field_ref, point_ref, bias_ref, out_ref, mixing_ref):
    mixing_ref[...] = mixing_matrix(point_ref)
    bias = jnp.concatenate([bias_ref[...]] * NZ, axis=1)
    out_ref[...] = mixed(field_ref[...], mixing_ref[...], ((1,), (0,))) + bias


def middle_kernel(
    rows_x,
    rows_y,
    turns,
    base_ref,
    cotangent_ref,
    table_ref,
    back_ref,
    depth_ref,
    *refs,
):
    in_refs = unqueued(refs[:turns], INVERSE_X)
    out_refs, (adjoint_ref, value_ref) = refs[turns:-2], refs[-2:]
    planes = z_synthesis(in_refs, depth_ref, rows_x)
    for x in range(rows_x):
        block = slice(x * rows_y, (x + 1) * rows_y)
        spectral = y_synthesis(planes, back_ref[...], x, rows_x)
        value_ref[block, :] = spectral + base_ref[block, :]
    value = value_ref[...]
    root = math.sqrt(2.0 / math.pi)
    square = value * value
    bent = jnp.tanh(value * (root + (root * 0.044715) * square))
    tail = value * (root + (3.0 * root * 0.044715) * square)
    slope = (0.5 + 0.5 * bent) * (1.0 + (1.0 - bent) * tail)
    adjoint = (cotangent_ref[...].astype(F32) * slope).astype(BF)
    adjoint_ref[...] = adjoint
    modes = y_spectrum(adjoint, table_ref[...], rows_x, rows_y).astype(BF)
    z_spectrum(dot(modes, depth_ref[...]), out_refs, rows_x)


def sums_kernel(field_ref, adjoint_ref, mixing_ref, out_ref, sums_ref):
    field, adjoint, mixing = field_ref[...], adjoint_ref[...], mixing_ref[...]
    out_ref[...] = mixed(adjoint, mixing, ((1,), (1,)))
    wide = mixing.shape[0]
    total = jnp.zeros((wide, wide), F32)
    for start in range(0, NZ * C, wide):
        total = total + dot(
            field[:, start : start + wide], adjoint[:, start : start + wide], ((0,), (0,))
        )
    total = jnp.where(iota((wide, wide), 0) // C == iota((wide, wide), 1) // C, total, 0.0)
    point = total[:C]
    for start in range(C, wide, C):
        point = point + total[start : start + C]
    point = folded(point)
    group = iota((8, LANES), 1) // C
    packed = point[:8]
    for part in range(1, 4):
        packed = jnp.where(group == part, point[part * 8 : (part + 1) * 8], packed)
    sums_ref[:8, :] = packed
    sums_ref[8:, :] = folded(dot(jnp.ones((8, adjoint.shape[0]), BF), adjoint))


def adjoint_kernel(steps, weight_ref, spread_ref, *refs):
    in_refs, (out_ref, spec_ref, sums_ref, scratch, wide) = refs[:steps], refs[steps:]
    spec_ref[...] = summed_modes(in_refs) * depth_factor()
    sums_ref[...] = functools.reduce(jnp.add, [ref[CHUNKS * 2 * KX :, :] for ref in in_refs])
    index = out_index()

    def step(mode, carry):
        real = lane_take(mode_row(spec_ref, 2 * mode), index)
        imag = lane_take(mode_row(spec_ref, 2 * mode + 1), index)
        real_w, imag_w = weight_parts(weight_ref, mode)
        real_parts, imag_parts = [], []
        for part in range(C // 4):
            real_p, imag_p = lanes_of(real_w, part), lanes_of(imag_w, part)
            real_parts.append(real * real_p + imag * imag_p)
            imag_parts.append(imag * real_p - real * imag_p)
        both = jnp.concatenate(
            [jnp.concatenate(real_parts, axis=1), jnp.concatenate(imag_parts, axis=1)], axis=0
        )
        high, low = halves(both)
        start = pl.multiple_of(2 * mode * KZ, 2 * KZ)
        wide[0, pl.ds(start, 2 * KZ), :] = high
        wide[1, pl.ds(start, 2 * KZ), :] = low
        return carry

    lax.fori_loop(0, KX, step, 0, unroll=KX)
    total = dot(wide[0], spread_ref[...], ((1,), (1,)))
    total = total + dot(wide[1], spread_ref[...], ((1,), (1,)))
    scratch[...] = own_rows(total)
    write_lanes(out_ref, gathered_rows(scratch), 2 * KX)


def weight_kernel(scale, field_ref, adjoint_ref, out_ref, staged, gates):
    index = out_index()
    stores = []
    turns = gates.shape[0]
    modes = KX // turns

    def step(mode, carry):
        row = 2 * mode
        real_v, imag_v = mode_row(field_ref, row), mode_row(field_ref, row + 1)
        real_h = lane_take(mode_row(adjoint_ref, row), index) * scale
        imag_h = lane_take(mode_row(adjoint_ref, row + 1), index) * scale
        real_g, imag_g = [], []
        for part in range(C // 4):
            take = in_index(part)
            real, imag = lane_take(real_v, take), lane_take(imag_v, take)
            real_g.append(real * real_h + imag * imag_h)
            imag_g.append(real * imag_h - imag * real_h)
        start = pl.multiple_of(mode * 2 * C * C, LANES)
        staged[:, pl.ds(start, 2 * C * C)] = jnp.concatenate(real_g + imag_g, axis=1)
        return carry

    for turn in range(turns):
        lax.fori_loop(turn * modes, (turn + 1) * modes, step, 0, unroll=2)
        block = pl.ds(turn * modes * 2 * C * C, modes * 2 * C * C)
        stores.append(
            pltpu.make_async_copy(staged.at[:, block], out_ref.at[:, block], gates.at[turn])
        )
        stores[-1].start()
    for store in stores:
        store.wait()


def last_kernel(rows_x, rows_y, turns, scale, mixed_ref, back_ref, depth_ref, *refs):
    in_refs = unqueued(refs[:turns], INVERSE_X)
    out_ref, point_ref, bias_ref, result, point, columns, gates, sum_gates = refs[turns:]
    total = functools.reduce(jnp.add, [ref[ref.shape[0] - SUM_ROWS :, :] for ref in in_refs])
    total = total * scale
    packed = total[:8]
    for part in range(4):
        piece = packed if part == 0 else pltpu.roll(packed, LANES - part * C, 1)
        point[part * 8 : (part + 1) * 8, :] = piece[:, :C]
    columns[...] = total[8:9, :C]
    stores = [
        pltpu.make_async_copy(point, point_ref, sum_gates.at[0]),
        pltpu.make_async_copy(columns, bias_ref, sum_gates.at[1]),
    ]
    for store in stores:
        store.start()
    planes = z_synthesis(in_refs, depth_ref, rows_x, exact=False)
    for x in range(rows_x):
        block = slice(x * rows_y, (x + 1) * rows_y)
        spectral = y_synthesis(planes, back_ref[...], x, rows_x)
        result[block, :] = (mixed_ref[block, :] + spectral).astype(BF)
        span = pl.ds(x * rows_y, rows_y)
        stores.append(pltpu.make_async_copy(result.at[span], out_ref.at[span], gates.at[x]))
        stores[-1].start()
    for store in stores:
        store.wait()


NEAR = pl.BlockSpec(memory_space=pltpu.VMEM)
FAR = pl.BlockSpec(memory_space=pltpu.HBM)


def call(kernel, ins, outs, scratch=()):
    shapes = []
    for shape, kind, inner in outs:
        if inner is None:
            shapes.append(jax.ShapeDtypeStruct(shape, kind))
        else:
            shapes.append((pltpu.VMEM if inner else pltpu.HBM)(shape, kind))
    function = pl.pallas_call(
        kernel,
        out_shape=shapes,
        in_specs=[NEAR if inner else FAR for inner in ins],
        out_specs=[FAR if inner is False else NEAR for _, _, inner in outs],
        scratch_shapes=list(scratch),
        compiler_params=pltpu.CompilerParams(vmem_limit_bytes=40 * 1024 * 1024),
    )

    def run(*arguments):
        spaces = [pltpu.VMEM if inner else pltpu.HBM for inner in ins]
        return function(*map(pltpu.with_memory_space_constraint, arguments, spaces))

    return run


def exchange(blocks, axis):
    count = lax.axis_size(axis)
    order = [2, 3, 1] if count == 4 else list(range(1, count))
    received = list(blocks)
    for turn in order:
        pairs = [(device, device ^ turn) for device in range(count)]
        received[turn] = lax.ppermute(blocks[turn], axis, pairs)
    return received


def fast_device(field_input, cotangent, spectral_weight, point_weight, point_bias):
    rows_x, rows_y, depth = field_input.shape
    x_parts, y_parts = lax.axis_size("gx"), lax.axis_size("gy")
    full_x, full_y = rows_x * x_parts, rows_y * y_parts
    scale = 1.0 / math.sqrt(full_x * full_y * NZ)
    cells = rows_x * rows_y
    z_rows = jnp.asarray(depth_rows())
    spread_hits = jnp.asarray(spread_table())
    forward_y, inverse_y = map(jnp.asarray, y_tables(full_y, rows_y, x_parts, y_parts))
    forward_x, inverse_x = map(jnp.asarray, x_tables(full_x, rows_x, scale, y_parts))
    field = field_input.reshape(cells, depth)
    bias = point_bias.reshape(1, C)
    cell_rows, mode_rows = CHUNKS * rows_x * 8, CHUNKS * 2 * KX
    cell_block, mode_block = ((cell_rows, LANES), F32, True), ((mode_rows, LANES), F32, True)
    cell_sums = ((cell_rows + SUM_ROWS, LANES), F32, True)
    mode_sums = ((mode_rows + SUM_ROWS, LANES), F32, True)
    spectrum_shape = ((2 * KX, WIDE), F32, True)
    rows_scratch = pltpu.VMEM((2 * KX * KZ, LANES), F32)
    sums_shape = ((SUM_ROWS, LANES), F32, True)
    cell_shape = ((cells, depth), F32, True)
    wide = (KZ, KX * 2 * C * C)

    def forward(blocks, extra, mode_shape):
        received = exchange(blocks, "gx")
        sent = call(
            functools.partial(x_forward_kernel, x_parts),
            [True] * (1 + x_parts + len(extra)),
            [mode_shape] * y_parts,
        )(to_modes, *queued(received, FORWARD_X), *extra)
        return queued(exchange(sent, "gy"), FORWARD_Y)

    def inverse(block, extra, cell_shape):
        received = exchange([block] * y_parts, "gy")
        sent = call(
            functools.partial(x_inverse_kernel, y_parts, x_parts),
            [True] * (1 + y_parts + len(extra)),
            [cell_shape] * x_parts,
        )(to_cells, *queued(received, INVERSE_Y), *extra)
        return queued(exchange(sent, "gx"), INVERSE_X)

    *blocks, depth_table, table, back, to_modes, to_cells, spread = call(
        functools.partial(first_kernel, rows_x, rows_y),
        [False] * 7,
        [cell_block] * x_parts
        + [((depth, 2 * WIDE), BF, True)]
        + [(part.shape[1:], BF, True) for part in (forward_y, inverse_y)]
        + [(part.shape, BF, True) for part in (forward_x, inverse_x, spread_hits)],
        [
            pltpu.VMEM((cells, depth), BF),
            pltpu.VMEM(z_rows.shape, F32),
            pltpu.SemaphoreType.DMA((8,)),
        ],
    )(field, forward_y, z_rows, inverse_y, forward_x, inverse_x, spread_hits)
    base, mixing = call(point_kernel, [True] * 3, [cell_shape, ((8 * C, 8 * C), BF, True)])(
        field, point_weight, bias
    )
    block, field_modes = call(
        functools.partial(product_kernel, y_parts),
        [True] * (2 + y_parts),
        [mode_block, spectrum_shape],
        [rows_scratch, pltpu.VMEM((2 * KX * KZ, C * C), F32)],
    )(spectral_weight, spread, *forward(blocks, [], mode_block))
    *blocks, adjoint = call(
        functools.partial(middle_kernel, rows_x, rows_y, x_parts),
        [True] * (5 + x_parts),
        [cell_block] * x_parts + [((cells, depth), BF, True)],
        [pltpu.VMEM((cells, depth), F32)],
    )(
        base,
        cotangent.reshape(cells, depth),
        table,
        back,
        depth_table,
        *inverse(block, [], cell_block),
    )
    mixed_adjoint, sums = call(sums_kernel, [True] * 3, [cell_shape, sums_shape])(
        field, adjoint, mixing
    )
    block, adjoint_modes, sums = call(
        functools.partial(adjoint_kernel, y_parts),
        [True] * (2 + y_parts),
        [mode_block, spectrum_shape, sums_shape],
        [rows_scratch, pltpu.VMEM((2, 2 * KX * KZ, C * C), BF)],
    )(spectral_weight, spread, *forward(blocks, [sums], mode_sums))
    (grad_spectral,) = call(
        functools.partial(weight_kernel, scale),
        [True] * 2,
        [(wide, F32, False)],
        [pltpu.VMEM(wide, F32), pltpu.SemaphoreType.DMA((4,))],
    )(field_modes, adjoint_modes)
    grad_field, grad_point, grad_bias = call(
        functools.partial(last_kernel, rows_x, rows_y, x_parts, scale),
        [True] * (3 + x_parts),
        [((cells, depth), BF, False), ((C, C), F32, False), ((1, C), F32, False)],
        [
            pltpu.VMEM((cells, depth), BF),
            pltpu.VMEM((C, C), F32),
            pltpu.VMEM((1, C), F32),
            pltpu.SemaphoreType.DMA((rows_x,)),
            pltpu.SemaphoreType.DMA((2,)),
        ],
    )(mixed_adjoint, back, depth_table, *inverse(block, [sums], cell_sums))
    return (
        grad_field.reshape(field_input.shape),
        grad_spectral,
        grad_point,
        grad_bias.reshape(C),
    )


def on_device(*arguments):
    rows_x, rows_y, _ = arguments[0].shape
    x_parts, y_parts = lax.axis_size("gx"), lax.axis_size("gy")
    whole_modes = arguments[2].shape[0] == KZ and y_parts == 4 and x_parts == 4
    if whole_modes and rows_x == 8 and rows_y == 64:
        return fast_device(*arguments)
    return general_device(*arguments)


def solution(mesh):
    return jax.shard_map(
        on_device,
        mesh=mesh,
        in_specs=(
            P(("groups", "gx"), "gy", None),
            P(("groups", "gx"), "gy", None),
            P(("gx", "gy"), None),
            P(),
            P(),
        ),
        out_specs=(
            P(("groups", "gx"), "gy", None),
            P(("groups", "gx", "gy"), None),
            P("groups", None),
            P("groups"),
        ),
        check_vma=False,
    )
```
